32 devices in a mesh: dp: 8 (over z, y), fsdp: 4 (over x, core).
Axes of the slice: x: 2, y: 2, z: 4, core: 2. Of those that a mesh axis runs over, the one named last changes fastest.
Arguments:
- doc_hidden: bfloat16 [32, 1024, 1024], P(('dp', 'fsdp')), may hold values from -6 to 6
- query_hidden: bfloat16 [32, 32, 1024], P(('dp', 'fsdp')), may hold values from -6 to 6
- w_query: bfloat16 [1024, 1024], P(('dp', 'fsdp')), may hold values from -0.25 to 0.25
- w_key: bfloat16 [1024, 1024], P(('dp', 'fsdp')), may hold values from -0.25 to 0.25
- w_value: bfloat16 [1024, 1024], P(('dp', 'fsdp')), may hold values from -0.1875 to 0.1875
- w_out: bfloat16 [1024, 1024], P(('dp', 'fsdp')), may hold values from -0.75 to 0.75
- w_up: bfloat16 [1024, 4096], P(('dp', 'fsdp')), may hold values from -0.1875 to 0.1875
- w_down: bfloat16 [4096, 1024], P(('dp', 'fsdp')), may hold values from -0.125 to 0.125
- w_proj: bfloat16 [1024, 128], P(('dp', 'fsdp')), may hold values from -0.1875 to 0.1875
- biases: bfloat16 [6, 1024], P(None, ('dp', 'fsdp')), may hold values from -2 to 2
- gains: bfloat16 [2, 1024], P(None, ('dp', 'fsdp')), may hold values from 0.5 to 1.5
- up_bias: bfloat16 [4096], P(('dp', 'fsdp')), may hold values from -2 to 2
- seg_lengths: int32 [32, 9], P(('dp', 'fsdp')), may hold values from 1 to 512, 1024 in all within a row
- positives: int32 [32], replicated, may hold values from 0 to 255
Outputs:
- loss: float32 [], replicated
- doc_grad: float32 [32, 1024, 1024], P(('dp', 'fsdp'))
- query_grad: float32 [32, 32, 1024], P(('dp', 'fsdp'))
- w_query_grad: float32 [1024, 1024], P(('dp', 'fsdp'))
- w_key_grad: float32 [1024, 1024], P(('dp', 'fsdp'))
- w_value_grad: float32 [1024, 1024], P(('dp', 'fsdp'))
- w_out_grad: float32 [1024, 1024], P(('dp', 'fsdp'))
- w_up_grad: float32 [1024, 4096], P(('dp', 'fsdp'))
- w_down_grad: float32 [4096, 1024], P(('dp', 'fsdp'))
- w_proj_grad: float32 [1024, 128], P(('dp', 'fsdp'))
- biases_grad: float32 [6, 1024], P(None, ('dp', 'fsdp'))
- gains_grad: float32 [2, 1024], P(None, ('dp', 'fsdp'))
- up_bias_grad: float32 [4096], P(('dp', 'fsdp'))
The draws below stay inside these ranges and needn't reach their ends.
Inputs may be any that keep to these rules, and one draw needn't show every extreme that they name: `seg_lengths`: in each row the first 8 entries are the lengths of the row's documents in order and the last is the padding at the row's end; a row's entries sum to 1024. positives[q] = r * 8 + c names document slot c of packed row r.
All inputs are finite; a program needn't handle non-finite values.
Results may differ from the reference program's by a relative error of at most 0.019.
The reference program's roundings to bfloat16 on the way count: a program that leaves them out, or rounds other values in their place, can miss the bound.
Values may be sent and summed in bfloat16 or wider, within the bound.
A program may use at most 256 MiB of HBM per device.

```python
import math
from functools import partial
import jax
import jax.numpy as jnp
import numpy as np
from jax import lax

D = 1024
HEADS = 16
HEAD_DIM = 64
FF = 4096
P_SIZE = 128
ROW_LEN = 1024
DOCS_ROW = 8
SEARCH_TERM_SPAN = 32
ROWS = 32
QUERIES = 32
DOCS = 256
DOC_MOST = 512


def set_ends(values, stream_key, low, largest):
    longest = values.shape.index(max(values.shape))
    spots = []
    for shift in (0, 1):
        where = [jax.random.randint(jax.random.fold_in(stream_key, axis), (), 0, length) for axis, length in enumerate(values.shape)]
        where[longest] = (where[longest] + shift) % values.shape[longest]
        spots.append(tuple(where))
    return values.at[spots[0]].set(low).at[spots[1]].set(largest)


def steps_of(rng, shape, cuts, low, top_value):
    loudness = 1.0
    for dim, parts in cuts:
        steps = jax.random.uniform(jax.random.fold_in(jax.random.fold_in(rng, 6), dim), (parts,), jnp.float32, low / len(cuts), top_value / len(cuts))
        loudness = loudness * jnp.repeat(jnp.exp(steps), shape[dim] // parts).reshape((-1,) + (1,) * (len(shape) - 1 - dim))
    return loudness


def length_profile(count, total, bound, lean):
    loads = [(1 << 20) // math.isqrt(grade ** lean) + 1 for grade in range(2, count + 1)]
    surplus, holding = total - bound - (count - 1), [1] * (count - 1)
    while surplus > 0:
        movable = [i for i in range(count - 1) if holding[i] < bound]
        mass, budget = sum([loads[i] for i in movable]), surplus
        for i in movable:
            addition = min(bound - holding[i], max(1, budget * loads[i] // mass), surplus)
            holding[i] = holding[i] + addition
            surplus = surplus - addition
    return np.array([bound] + holding)


def uneven_parts(key, number_of, total, bound, slope):
    if number_of == 2:
        one = jax.random.randint(key, (), max(1, total - bound), min(bound, total - 1) + 1)
        return jnp.stack([one, total - one])
    sizes = jnp.asarray(length_profile(number_of, total, bound, slope), jnp.int32)
    couples = (number_of - 1) // 2
    donor, receiver = sizes[1:1 + 2 * couples:2], sizes[2:2 + 2 * couples:2]
    margin = jnp.minimum(donor - 1, bound - receiver)
    shifted = jax.random.randint(jax.random.fold_in(key, 1), (couples,), 0, 1 << 20) % (margin + 1)
    sizes = sizes.at[1:1 + 2 * couples:2].set(donor - shifted).at[2:2 + 2 * couples:2].set(receiver + shifted)
    return sizes[jax.random.permutation(jax.random.fold_in(key, 2), number_of)]


def scatter_about(key, dims, width, reach, cuts=(), kind=jnp.bfloat16):
    entries = jax.random.normal(key, dims, jnp.float32) * width
    if len(cuts) > 0:
        entries = steps_of(key, dims, cuts, -0.22, 0.18) * entries
    return jnp.clip(entries, min=-reach, max=reach).astype(kind)


def setup_inputs(seed: int = 0) -> dict:
    key_list = jax.random.split(jax.random.key(seed), 15)
    return {
        "doc_hidden": scatter_about(key_list[0], (ROWS, ROW_LEN, D), 1.0, 6.0, ((0, 32),)),
        "query_hidden": scatter_about(key_list[1], (QUERIES, SEARCH_TERM_SPAN, D), 1.0, 6.0, ((0, 32),)),
        "w_query": scatter_about(key_list[2], (D, D), (D // 2) ** -0.5, 0.25, ((0, 32),)),
        "w_key": scatter_about(key_list[3], (D, D), (D // 2) ** -0.5, 0.25, ((0, 32),)),
        "w_value": scatter_about(key_list[4], (D, D), D ** -0.5, 0.1875, ((0, 32),)),
        "w_out": scatter_about(key_list[5], (D, D), (D // 16) ** -0.5, 0.75, ((0, 32),)),
        "w_up": scatter_about(key_list[6], (D, FF), D ** -0.5, 0.1875, ((0, 32),)),
        "w_down": scatter_about(key_list[7], (FF, D), (FF // 2) ** -0.5, 0.125, ((0, 32),)),
        "w_proj": scatter_about(key_list[8], (D, P_SIZE), D ** -0.5, 0.1875, ((0, 32),)),
        "biases": scatter_about(key_list[9], (6, D), 0.3, 2.0, ((1, 32),)),
        "gains": jnp.clip(1.0 + 0.1 * jax.random.normal(key_list[10], (2, D), jnp.float32), 0.5, 1.5).astype(jnp.bfloat16),
        "up_bias": scatter_about(key_list[11], (FF,), 0.3, 2.0, ((0, 32),)),
        "seg_lengths": jax.vmap(lambda own: uneven_parts(own, DOCS_ROW + 1, ROW_LEN, DOC_MOST, 2))(jax.random.split(key_list[12], ROWS)).reshape((ROWS, DOCS_ROW + 1)).astype(jnp.int32),
        "positives": set_ends(jax.random.randint(key_list[13], (QUERIES,), 0, DOCS), jax.random.fold_in(key_list[13], 1), 0, DOCS - 1).astype(jnp.int32),
    }


@jax.custom_vjp
def low(v):
    return lax.optimization_barrier(v.astype(jnp.bfloat16)).astype(jnp.float32)

@jax.custom_vjp
def low_back(v):
    return v

def low_keep(v):
    return (low(v), None)

def low_pass(kept, grad):
    return (grad,)

def back_keep(v):
    return (v, None)

def back_low(kept, grad):
    return (low(grad),)
low.defvjp(low_keep, low_pass)
low_back.defvjp(back_keep, back_low)
softness = 0.1
sharpness_divisor = 0.2
norm_eps = 1e-05
unit_eps = 1e-06

def matmul_high(left, right):
    return jnp.dot(left, right, precision=lax.Precision.HIGHEST, preferred_element_type=jnp.float32)

def layer_norm(values, gain_row, bias_row):
    center = values - lax.optimization_barrier(jnp.mean(values, axis=-1, keepdims=True))
    spread = lax.optimization_barrier(jnp.mean(center * center, axis=-1, keepdims=True))
    return center * lax.rsqrt(spread + norm_eps) * gain_row + bias_row

def doc_attend(query_all, key_all, value_all, segment):
    length_rows = query_all.shape[0]
    query_h = query_all.reshape(length_rows, HEADS, HEAD_DIM).transpose(1, 0, 2)
    key_h = key_all.reshape(length_rows, HEADS, HEAD_DIM).transpose(1, 0, 2)
    value_h = value_all.reshape(length_rows, HEADS, HEAD_DIM).transpose(1, 0, 2)
    scores = low_back(jnp.einsum('hid,hjd->hij', query_h, key_h, precision=lax.Precision.HIGHEST) * 0.125)
    allowed = segment[:, None] == segment[None, :]
    scores = jnp.where(allowed[None, :, :], scores, -1e+30)
    attn_probs = low(jax.nn.softmax(scores, axis=-1))
    context = jnp.einsum('hij,hjd->hid', attn_probs, value_h, precision=lax.Precision.HIGHEST)
    return context.transpose(1, 0, 2).reshape(length_rows, D)

def query_attend(query_all, key_all, value_all):
    query_h = query_all.reshape(QUERIES, SEARCH_TERM_SPAN, HEADS, HEAD_DIM)
    key_h = key_all.reshape(QUERIES, SEARCH_TERM_SPAN, HEADS, HEAD_DIM)
    value_h = value_all.reshape(QUERIES, SEARCH_TERM_SPAN, HEADS, HEAD_DIM)
    scores = low_back(jnp.einsum('aihd,ajhd->ahij', query_h, key_h, precision=lax.Precision.HIGHEST) * 0.125)
    attn_probs = low(jax.nn.softmax(scores, axis=-1))
    context = jnp.einsum('ahij,ajhd->aihd', attn_probs, value_h, precision=lax.Precision.HIGHEST)
    return context.reshape(QUERIES * SEARCH_TERM_SPAN, D)

def encode(tokens, weights, attend):
    w_query, w_key, w_value, w_out, w_up, w_down, w_proj, biases, gains, up_bias = weights
    query_all = low(low_back(matmul_high(tokens, w_query) + biases[0]))
    key_all = low(low_back(matmul_high(tokens, w_key)))
    value_all = low(low_back(matmul_high(tokens, w_value) + biases[1]))
    context = low(low_back(attend(query_all, key_all, value_all)))
    attn_out = low_back(matmul_high(context, w_out) + biases[2])
    first = layer_norm(tokens + attn_out, gains[0], biases[3])
    up_pre = low_back(matmul_high(low(first), w_up) + up_bias)
    gelu_out = low(jax.nn.gelu(up_pre, approximate=False))
    ffn_out = low_back(matmul_high(gelu_out, w_down) + biases[4])
    second = layer_norm(first + ffn_out, gains[1], biases[5])
    return low(low_back(matmul_high(low(second), w_proj)))

def segment_ids(lengths_row):
    doc_ends = jnp.cumsum(lengths_row.astype(jnp.int32))
    places = jnp.arange(ROW_LEN, dtype=jnp.int32)
    return lax.optimization_barrier(jnp.sum((places[:, None] >= doc_ends[None, :]).astype(jnp.int32), axis=1))

def prefix_unit(vectors, level_width):
    part_cols = vectors[..., :level_width]
    return low(part_cols * lax.rsqrt(lax.optimization_barrier(jnp.sum(part_cols * part_cols, axis=-1, keepdims=True)) + unit_eps))

def row_logits(query_vectors, doc_vectors, segment):
    member = (segment[:, None] == jnp.arange(DOCS_ROW, dtype=jnp.int32)[None, :]).astype(jnp.float32)
    piled_entries = []
    for level_width in (P_SIZE, P_SIZE * 3 // 4, P_SIZE // 2):
        query_units = prefix_unit(query_vectors, level_width).reshape(QUERIES * SEARCH_TERM_SPAN, level_width)
        doc_units = prefix_unit(doc_vectors, level_width)
        scores = low_back(matmul_high(query_units, doc_units.T))
        doc_sums = matmul_high(jnp.exp(scores / softness), member)
        peak_match_score = lax.optimization_barrier(jnp.sum((softness * jnp.log(doc_sums)).reshape(QUERIES, SEARCH_TERM_SPAN, DOCS_ROW), axis=1))
        piled_entries.append(peak_match_score / (SEARCH_TERM_SPAN * sharpness_divisor))
    return jnp.stack(piled_entries, axis=1)

def reference(doc_hidden, query_hidden, w_query, w_key, w_value, w_out, w_up, w_down, w_proj, biases, gains, up_bias, seg_lengths, positives):
    floats = tuple((array.astype(jnp.float32) for array in (doc_hidden, query_hidden, w_query, w_key, w_value, w_out, w_up, w_down, w_proj, biases, gains, up_bias)))

    def loss_of(doc_in, query_in, *weights):
        query_vectors = encode(query_in.reshape(QUERIES * SEARCH_TERM_SPAN, D), weights, query_attend).reshape(QUERIES, SEARCH_TERM_SPAN, P_SIZE)

        def per_row(carry, row_pair):
            tokens, lengths_row = row_pair
            segment = segment_ids(lengths_row)
            vectors = encode(tokens, weights, partial(doc_attend, segment=segment))
            return (carry, row_logits(query_vectors, vectors, segment))
        unused, logits = lax.scan(jax.checkpoint(per_row), jnp.zeros((), jnp.float32), (doc_in, seg_lengths))
        logits = jnp.moveaxis(logits, 0, 2).reshape(QUERIES, 3, DOCS)
        totals = lax.optimization_barrier(jnp.sum(jnp.exp(logits), axis=-1))
        index_rows = jnp.broadcast_to(positives.astype(jnp.int32)[:, None, None], (QUERIES, 3, 1))
        picked = jnp.take_along_axis(logits, index_rows, axis=-1)[:, :, 0]
        return jnp.sum(jnp.log(totals) - picked) / QUERIES
    loss, backward = jax.vjp(loss_of, *floats)
    grads = backward(jnp.ones_like(loss))
    return (loss, grads[0], grads[1], grads[2], grads[3], grads[4], grads[5], grads[6], grads[7], grads[8], grads[9], grads[10], grads[11])
```

```python
from functools import partial

import jax
import jax.numpy as jnp
from jax import lax
from jax.experimental import pallas as pl
from jax.experimental.pallas import tpu as pltpu
from jax.sharding import PartitionSpec as P

softness = 0.1
sharpness_divisor = 0.2
norm_eps = 1e-05
unit_eps = 1e-06
head_width = 64
block_queries = 16
masked_score = -1e30
rate = 0.125 * 1.4426950408889634
q_rows = 256
k_rows = 256
f32 = jnp.float32
bf16 = jnp.bfloat16
AXES = ("dp", "fsdp")

def matmul_plain(left, right):
    return jnp.dot(left, right, preferred_element_type=jnp.float32)


def matmul_right_t(left, right):
    return lax.dot_general(
        left, right, (((1,), (1,)), ((), ())), preferred_element_type=jnp.float32
    )


def matmul_left_t(left, right):
    return lax.dot_general(
        left, right, (((0,), (0,)), ((), ())), preferred_element_type=jnp.float32
    )


def layer_norm_parts(values, gain_row, bias_row):
    center = values - jnp.mean(values, axis=-1, keepdims=True)
    spread = jnp.mean(center * center, axis=-1, keepdims=True)
    inv_scale = lax.rsqrt(spread + norm_eps)
    normed = center * inv_scale
    return (normed * gain_row + bias_row, normed, inv_scale)


def layer_norm_back(grad_out, normed, inv_scale, gain_row):
    grad_norm = grad_out * gain_row
    mean_grad = jnp.mean(grad_norm, axis=-1, keepdims=True)
    mean_proj = jnp.mean(grad_norm * normed, axis=-1, keepdims=True)
    grad_in = inv_scale * (grad_norm - mean_grad - normed * mean_proj)
    return (grad_in, jnp.sum(grad_out * normed, axis=0), jnp.sum(grad_out, axis=0))


def unit_prefix(vectors, level_width):
    part_cols = vectors[..., :level_width].astype(jnp.float32)
    inv_scale = lax.rsqrt(jnp.sum(part_cols * part_cols, axis=-1, keepdims=True) + unit_eps)
    return (part_cols * inv_scale, inv_scale)


def dot_nt(a,b): return lax.dot_general(a,b,(((1,),(1,)),((),())),preferred_element_type=f32)
def dot_nn(a,b): return jnp.dot(a,b,preferred_element_type=f32)

def stack_heads(block, first):
    zero=jnp.zeros_like(block)
    return jnp.concatenate([jnp.where(first,block,zero),jnp.where(first,zero,block)],axis=0)

def attend_forward(row_len, qb, kb, lanes, span, bounds, segrow, segcol, q_ref,k_ref,v_ref,ctx_ref,lse_ref,qlse_ref,vt_ref):
    units=lanes//128
    tokens=q_ref.shape[0]
    first_q=lax.broadcasted_iota(jnp.int32,(qb,128),1)<64
    top=lax.broadcasted_iota(jnp.int32,(128,qb),0)<64
    vt_ref[...]=v_ref[...].T
    def q_step(i,_):
        rows=pl.ds(pl.multiple_of(i*qb,qb),qb)
        own=segrow[pl.ds(i,1),:]
        stacked=[stack_heads(q_ref[rows,pl.ds(u*128,128)],first_q) for u in range(units)]
        def k_step(j,carry):
            keys=pl.ds(pl.multiple_of(j*kb,kb),kb)
            allowed=segcol[keys,:]==own
            out=[]
            for u in range(units):
                peak,total,acc=carry[u]
                s=jnp.where(allowed,dot_nt(k_ref[keys,pl.ds(u*128,128)],stacked[u]),masked_score)
                new=jnp.maximum(peak,jnp.max(s,axis=0,keepdims=True))
                p=jnp.exp2((s-new)*rate)
                fade=jnp.exp2((peak-new)*rate)
                total=total*fade+jnp.sum(p,axis=0,keepdims=True)
                acc=acc*fade+dot_nn(vt_ref[pl.ds(u*128,128),keys],p.astype(bf16))
                out.append((new,total,acc))
            return tuple(out)
        start=tuple((jnp.full((1,2*qb),masked_score,f32),jnp.zeros((1,2*qb),f32),jnp.zeros((128,2*qb),f32)) for u in range(units))
        res=lax.fori_loop(bounds[0,i],bounds[1,i],k_step,start)
        for u in range(units):
            peak,total,acc=res[u]
            acc=acc/total
            o=jnp.where(top,acc[:,:qb],acc[:,qb:])
            ctx_ref[rows,pl.ds(u*128,128)]=o.T.astype(bf16)
            lse_ref[u,pl.ds(i,1),:]=peak*rate+jnp.log2(total)
        return 0
    lax.fori_loop(0,row_len//qb,q_step,0)
    nq=tokens-row_len
    firstn=lax.broadcasted_iota(jnp.int32,(nq,128),1)<64
    own=lax.broadcasted_iota(jnp.int32,(nq,2*nq),0)//span
    other=(lax.broadcasted_iota(jnp.int32,(nq,2*nq),1)%nq)//span
    keep=own==other
    for u in range(units):
        cols=pl.ds(u*128,128)
        st=stack_heads(q_ref[row_len:,cols],firstn)
        s=jnp.where(keep,dot_nt(k_ref[row_len:,cols],st),masked_score)
        peak=jnp.max(s,axis=0,keepdims=True)
        p=jnp.exp2((s-peak)*rate)
        total=jnp.sum(p,axis=0,keepdims=True)
        p=(p/total).astype(bf16)
        acc=lax.dot_general(p,v_ref[row_len:,cols],(((0,),(0,)),((),())),preferred_element_type=f32)
        ctx_ref[row_len:,cols]=jnp.where(firstn,acc[:nq],acc[nq:]).astype(bf16)
        qlse_ref[u,:,:]=peak*rate+jnp.log2(total)

def attention_forward(qkv,segrow,segcol,bounds,row_len,span):
    tokens=qkv.shape[0]
    width=qkv.shape[1]//3
    qb,kb,lanes=q_rows,k_rows,width
    nq=tokens-row_len
    steps=width//lanes
    def spec(off): return pl.BlockSpec((tokens,lanes),lambda p,*_:(0,p+off))
    full=lambda a: pl.BlockSpec(a.shape,lambda p,*_:(0,)*a.ndim)
    return pl.pallas_call(
        partial(attend_forward,row_len,qb,kb,lanes,span),
        out_shape=(jax.ShapeDtypeStruct((tokens,width),bf16),jax.ShapeDtypeStruct((width//128,row_len//qb,2*qb),f32),jax.ShapeDtypeStruct((width//128,1,2*nq),f32)),
        grid_spec=pltpu.PrefetchScalarGridSpec(num_scalar_prefetch=1,grid=(steps,),
            in_specs=[full(segrow),full(segcol),spec(0),spec(steps),spec(2*steps)],
            out_specs=[pl.BlockSpec((tokens,lanes),lambda p,*_:(0,p)),pl.BlockSpec((lanes//128,row_len//qb,2*qb),lambda p,*_:(p,0,0)),pl.BlockSpec((lanes//128,1,2*nq),lambda p,*_:(p,0,0))],
            scratch_shapes=[pltpu.VMEM((lanes,tokens),bf16)]),
        compiler_params=pltpu.CompilerParams(vmem_limit_bytes=48<<20),
    )(bounds,segrow,segcol,qkv,qkv,qkv)

def attend_backward(row_len, qb, kb, lanes, span, bounds, segrow, segcol, q_ref,k_ref,v_ref,g_ref,o_ref,lse_ref,qlse_ref,out_ref,kt_ref,dka,dva):
    dq_ref=out_ref.at[:,:lanes]; dk_ref=out_ref.at[:,lanes:2*lanes]; dv_ref=out_ref.at[:,2*lanes:]
    units=lanes//128
    tokens=q_ref.shape[0]
    first_q=lax.broadcasted_iota(jnp.int32,(qb,128),1)<64
    top=lax.broadcasted_iota(jnp.int32,(128,qb),0)<64
    kt_ref[...]=k_ref[...].T
    dka[...]=jnp.zeros_like(dka); dva[...]=jnp.zeros_like(dva)
    def q_step(i,_):
        rows=pl.ds(pl.multiple_of(i*qb,qb),qb)
        own=segrow[pl.ds(i,1),:]
        sq=[];sg=[];dr=[];ls=[]
        for u in range(units):
            cols=pl.ds(u*128,128)
            g=g_ref[rows,cols]
            sq.append(stack_heads(q_ref[rows,cols],first_q)); sg.append(stack_heads(g,first_q))
            t=(g.astype(f32)*o_ref[rows,cols].astype(f32)).T
            dr.append(jnp.concatenate([jnp.sum(t[:64],axis=0,keepdims=True),jnp.sum(t[64:],axis=0,keepdims=True)],axis=1))
            ls.append(lse_ref[u,pl.ds(i,1),:])
        def k_step(j,carry):
            keys=pl.ds(pl.multiple_of(j*kb,kb),kb)
            allowed=segcol[keys,:]==own
            out=[]
            for u in range(units):
                cols=pl.ds(u*128,128)
                s=jnp.where(allowed,dot_nt(k_ref[keys,cols],sq[u]),masked_score)
                p=jnp.exp2(s*rate-ls[u])
                dp=dot_nt(v_ref[keys,cols],sg[u])
                ds=(p*(dp-dr[u])).astype(bf16)
                dva[keys,cols]+=dot_nn(p.astype(bf16),sg[u])
                dka[keys,cols]+=dot_nn(ds,sq[u])
                out.append(carry[u]+dot_nn(kt_ref[cols,keys],ds))
            return tuple(out)
        res=lax.fori_loop(bounds[0,i],bounds[1,i],k_step,tuple(jnp.zeros((128,2*qb),f32) for u in range(units)))
        for u in range(units):
            d=jnp.where(top,res[u][:,:qb],res[u][:,qb:])*0.125
            dq_ref[rows,pl.ds(u*128,128)]=d.T.astype(bf16)
        return 0
    lax.fori_loop(0,row_len//qb,q_step,0)
    dk_ref[:row_len,:]=(dka[...]*0.125).astype(bf16)
    dv_ref[:row_len,:]=dva[...].astype(bf16)
    nq=tokens-row_len
    firstn=lax.broadcasted_iota(jnp.int32,(nq,128),1)<64
    own=lax.broadcasted_iota(jnp.int32,(nq,2*nq),0)//span
    other=(lax.broadcasted_iota(jnp.int32,(nq,2*nq),1)%nq)//span
    keep=own==other
    for u in range(units):
        cols=pl.ds(u*128,128)
        q=q_ref[row_len:,cols]; k=k_ref[row_len:,cols]; v=v_ref[row_len:,cols]; g=g_ref[row_len:,cols]
        st=stack_heads(q,firstn); sg=stack_heads(g,firstn)
        s=jnp.where(keep,dot_nt(k,st),masked_score)
        p=jnp.exp2(s*rate-qlse_ref[u])
        dp=dot_nt(v,sg)
        ds=(p*(dp-jnp.sum(p*dp,axis=0,keepdims=True))).astype(bf16)
        dv_ref[row_len:,cols]=dot_nn(p.astype(bf16),sg).astype(bf16)
        dk_ref[row_len:,cols]=(dot_nn(ds,st)*0.125).astype(bf16)
        d=lax.dot_general(ds,k,(((0,),(0,)),((),())),preferred_element_type=f32)
        dq_ref[row_len:,cols]=(jnp.where(firstn,d[:nq],d[nq:])*0.125).astype(bf16)

def attention_backward(qkv,g,o,lse,qlse,segrow,segcol,bounds,row_len,span):
    tokens,width=g.shape
    qb,kb,lanes=q_rows,k_rows,width
    nq=tokens-row_len
    steps=width//lanes
    def spec(off): return pl.BlockSpec((tokens,lanes),lambda p,*_:(0,p+off))
    full=lambda a: pl.BlockSpec(a.shape,lambda p,*_:(0,)*a.ndim)
    sd=jax.ShapeDtypeStruct((tokens,3*width),bf16)
    return pl.pallas_call(
        partial(attend_backward,row_len,qb,kb,lanes,span),
        out_shape=sd,
        grid_spec=pltpu.PrefetchScalarGridSpec(num_scalar_prefetch=1,grid=(steps,),
            in_specs=[full(segrow),full(segcol)]+[spec(0),spec(1),spec(2),spec(0),spec(0)]+[pl.BlockSpec((lanes//128,row_len//qb,2*qb),lambda p,*_:(p,0,0)),pl.BlockSpec((lanes//128,1,2*nq),lambda p,*_:(p,0,0))],
            out_specs=pl.BlockSpec((tokens,3*lanes),lambda p,*_:(0,0)),
            scratch_shapes=[pltpu.VMEM((lanes,tokens),bf16),pltpu.VMEM((row_len,lanes),f32),pltpu.VMEM((row_len,lanes),f32)]),
        compiler_params=pltpu.CompilerParams(vmem_limit_bytes=56<<20),
    )(bounds,segrow,segcol,qkv,qkv,qkv,g,o,lse,qlse)


class Links:
    def __init__(self, dp, fsdp):
        self.dp, self.fsdp, self.count = dp, fsdp, dp * fsdp
        low = [1 << b for b in range(fsdp.bit_length() - 1)]
        high = [fsdp << b for b in range(dp.bit_length() - 1)]
        inner, rest = low[:1], low[1:]
        near, far = high[:1], high[1:][::-1]
        self.orders = (far + rest[::-1] + near + inner, far + near + rest[::-1] + inner)

    def swap(self, value, bit):
        return lax.ppermute(value, AXES, [(d, d ^ bit) for d in range(self.count)])

    def owners(self, order):
        slots = jnp.arange(self.count, dtype=jnp.int32)
        mixed = jnp.zeros_like(slots)
        for place, bit in enumerate(order):
            mixed = mixed + ((slots >> place) & 1) * bit
        return mixed ^ lax.axis_index(AXES)

    def places(self, order):
        other = jnp.arange(self.count, dtype=jnp.int32) ^ lax.axis_index(AXES)
        slots = jnp.zeros_like(other)
        for place, bit in enumerate(order):
            slots = slots + jnp.where((other & bit) != 0, 1 << place, 0)
        return slots

    def gather_slots(self, shard, order):
        held = shard[None]
        for bit in order:
            held = jnp.concatenate([held, self.swap(held, bit)], axis=0)
        return held

    def gather(self, shard, lane=0):
        order = self.orders[lane]
        return jnp.take(self.gather_slots(shard, order), self.places(order), axis=0)

    def scatter_sum(self, blocks, lane=0, wire=bf16):
        order = self.orders[lane]
        held = jnp.take(blocks.astype(wire), self.owners(order), axis=0)
        for bit in order[::-1]:
            half = held.shape[0] // 2
            arrived = self.swap(held[half:], bit)
            held = held[:half].astype(f32) + arrived.astype(f32)
            if half > 1:
                held = held.astype(wire)
        return held[0]

    def total(self, value):
        for bit in self.orders[0]:
            value = value + self.swap(value, bit)
        return value


class PlainLinks(Links):
    def gather(self, shard, lane=0):
        return lax.all_gather(shard, AXES, axis=0)

    def scatter_sum(self, blocks, lane=0, wire=bf16):
        return lax.psum_scatter(blocks, AXES, scatter_dimension=0, tiled=False)

    def total(self, value):
        return lax.psum(value, AXES)


def make_links(mesh):
    dp, fsdp = mesh.shape["dp"], mesh.shape["fsdp"]
    paired = (dp & (dp - 1)) == 0 and (fsdp & (fsdp - 1)) == 0 and dp * fsdp <= 64
    return (Links if paired else PlainLinks)(dp, fsdp)


def tables(lengths, row_len):
    ends = jnp.cumsum(lengths)
    starts = ends - lengths
    places = jnp.arange(row_len, dtype=jnp.int32)
    segment = jnp.sum((places[:, None] >= ends[None, :]).astype(jnp.int32), axis=1)
    rows = segment.reshape(row_len // q_rows, q_rows)
    ids = jnp.arange(lengths.shape[0])
    low = jnp.sum(jnp.where(rows[:, :1] == ids[None, :], starts[None, :], 0), axis=1)
    high = jnp.sum(jnp.where(rows[:, -1:] == ids[None, :], ends[None, :], 0), axis=1)
    bounds = jnp.stack([low // k_rows, (high + k_rows - 1) // k_rows]).astype(jnp.int32)
    return segment, jnp.concatenate([rows, rows], axis=1), segment[:, None], bounds


def body(
    links,
    doc_hidden,
    query_hidden,
    w_query,
    w_key,
    w_value,
    w_out,
    w_up,
    w_down,
    w_proj,
    biases,
    gains,
    up_bias,
    seg_lengths,
    positives,
):
    count = links.count
    row_len = doc_hidden.shape[1]
    model_width = doc_hidden.shape[2]
    query_count = query_hidden.shape[0]
    span = query_hidden.shape[1]
    doc_slots = seg_lengths.shape[1] - 1
    proj_width = w_proj.shape[1]
    ff = up_bias.shape[0] * count
    shard_cols = biases.shape[1]
    shard_rows = w_query.shape[0]
    part = model_width // 2
    small = jnp.concatenate(
        [biases.reshape(-1), gains.reshape(-1), up_bias.reshape(-1)], axis=0
    )[None]

    def rows_of(full):
        return full.reshape(full.shape[0] * full.shape[1], full.shape[2])

    small_full = links.gather(small, 0).reshape(count, -1)
    full_biases = (
        small_full[:, : 6 * shard_cols]
        .reshape(count, 6, shard_cols)
        .transpose(1, 0, 2)
        .reshape(6, model_width)
        .astype(f32)
    )
    full_gains = (
        small_full[:, 6 * shard_cols : 8 * shard_cols]
        .reshape(count, 2, shard_cols)
        .transpose(1, 0, 2)
        .reshape(2, model_width)
        .astype(f32)
    )
    full_upbias = small_full[:, 8 * shard_cols :].reshape(ff).astype(f32)

    full_qkv = []
    for side in range(2):
        cut = slice(side * part, (side + 1) * part)
        shard = jnp.concatenate([w_query[:, cut], w_key[:, cut], w_value[:, cut]], axis=1)
        full_qkv.append(rows_of(links.gather(shard, side)))
    out_proj = rows_of(links.gather(jnp.concatenate([w_out, w_proj], axis=1), 0))
    full_out, full_proj = out_proj[:, :model_width], out_proj[:, model_width:]
    full_up = rows_of(links.gather(w_up, 0))
    full_down = rows_of(links.gather(w_down, 1))

    tokens = jnp.concatenate(
        [doc_hidden[0], query_hidden.reshape(query_count * span, model_width)], axis=0
    )
    segment, segrow, segcol, bounds = tables(seg_lengths[0], row_len)
    slot_ids = jnp.arange(doc_slots, dtype=jnp.int32)
    member = (segment[:, None] == slot_ids[None, :]).astype(f32)
    member_t = (slot_ids[:, None] == segment[None, :]).astype(f32)
    zero_row = jnp.zeros((part,), f32)
    qkv, contexts, saved = [], [], []
    for side in range(2):
        cut = slice(side * part, (side + 1) * part)
        bias = jnp.concatenate([full_biases[0, cut], zero_row, full_biases[1, cut]])
        qkv.append((matmul_plain(tokens, full_qkv[side]) + bias).astype(bf16))
        context, lse, query_lse = attention_forward(
            qkv[side], segrow, segcol, bounds, row_len, span
        )
        contexts.append(context)
        saved.append((lse, query_lse))
    attn_out = (
        matmul_plain(contexts[0], full_out[:part])
        + matmul_plain(contexts[1], full_out[part:])
        + full_biases[2]
    )
    first_out, first_normed, first_scale = layer_norm_parts(
        tokens.astype(f32) + attn_out, full_gains[0], full_biases[3]
    )
    first_low = first_out.astype(bf16)
    up_pre = matmul_plain(first_low, full_up) + full_upbias
    gelu_out = jax.nn.gelu(up_pre, approximate=False).astype(bf16)
    ffn_out = matmul_plain(gelu_out, full_down) + full_biases[4]
    second_out, second_normed, second_scale = layer_norm_parts(
        first_out + ffn_out, full_gains[1], full_biases[5]
    )
    second_low = second_out.astype(bf16)
    vectors = matmul_plain(second_low, full_proj).astype(bf16)
    doc_vectors = vectors[:row_len]
    query_vectors = vectors[row_len:].reshape(query_count * span, proj_width)
    every_query = links.gather(query_vectors).reshape(count * query_count, span, proj_width)
    query_total = every_query.shape[0]
    block_count = query_total // block_queries
    levels = (proj_width, proj_width * 3 // 4, proj_width // 2)
    doc_prefix = tuple((unit_prefix(doc_vectors, level_width) for level_width in levels))
    doc_lows = tuple((prefix_pair[0].astype(bf16) for prefix_pair in doc_prefix))

    def block_logits(one_block):
        row_total = one_block.shape[0] * span
        piled_entries = []
        for position in range(3):
            level_width = levels[position]
            unit_rows = (
                unit_prefix(one_block, level_width)[0].astype(bf16).reshape(row_total, level_width)
            )
            scores = matmul_right_t(unit_rows, doc_lows[position])
            doc_sums = jnp.dot(jnp.exp(scores / softness), member, precision=lax.Precision.HIGHEST)
            peak_match_score = jnp.sum(
                (softness * jnp.log(doc_sums)).reshape(one_block.shape[0], span, doc_slots),
                axis=1,
            )
            piled_entries.append(peak_match_score / (span * sharpness_divisor))
        return jnp.stack(piled_entries, axis=1)

    blocks = every_query.reshape(block_count, block_queries, span, proj_width)
    logits = lax.map(block_logits, blocks).reshape(query_total, 3, doc_slots)
    powers = jnp.exp(logits)
    local_sum = jnp.sum(powers, axis=-1)
    my_row = lax.axis_index(AXES)
    chosen = ((positives - my_row * doc_slots)[:, None] == slot_ids[None, :]).astype(f32)
    local_pick = jnp.sum(logits * chosen[:, None, :], axis=-1)
    both = links.total(jnp.concatenate([local_sum, local_pick], axis=1))
    all_sums, picked = both[:, :3], both[:, 3:]
    loss = jnp.sum(jnp.log(all_sums) - picked) / query_total
    score_derivative = (powers / all_sums[:, :, None] - chosen[:, None, :]) / query_total
    peak_match_derivative = score_derivative / (span * sharpness_divisor)

    def block_back(carry, inputs):
        one_block, grad_block = inputs
        block_size = one_block.shape[0]
        row_total = block_size * span
        grad_vectors = jnp.zeros((block_size, span, proj_width), f32)
        new_carry = []
        for position in range(3):
            level_width = levels[position]
            unit_full, inv_scale = unit_prefix(one_block, level_width)
            unit_rows = unit_full.astype(bf16).reshape(row_total, level_width)
            scores = matmul_right_t(unit_rows, doc_lows[position])
            score_powers = jnp.exp(scores / softness)
            doc_sums = jnp.dot(score_powers, member, precision=lax.Precision.HIGHEST)
            grad_rows = jnp.broadcast_to(
                grad_block[:, None, position, :], (block_size, span, doc_slots)
            ).reshape(row_total, doc_slots)
            spread_rows = jnp.dot(grad_rows / doc_sums, member_t, precision=lax.Precision.HIGHEST)
            grad_scores = (score_powers * spread_rows).astype(bf16)
            grad_unit = matmul_plain(grad_scores, doc_lows[position]).reshape(
                block_size, span, level_width
            )
            new_carry.append(carry[position] + matmul_left_t(grad_scores, unit_rows))
            grad_part = inv_scale * (
                grad_unit - unit_full * jnp.sum(grad_unit * unit_full, axis=-1, keepdims=True)
            )
            grad_vectors = grad_vectors + jnp.pad(
                grad_part, ((0, 0), (0, 0), (0, proj_width - level_width))
            )
        return (tuple(new_carry), grad_vectors)

    start_carry = tuple((jnp.zeros((row_len, level_width), f32) for level_width in levels))
    grad_blocks = peak_match_derivative.reshape(block_count, block_queries, 3, doc_slots)
    doc_unit_grads, query_terms = lax.scan(block_back, start_carry, (blocks, grad_blocks))
    query_terms = query_terms.reshape(count, query_count * span, proj_width)
    query_vec_grad = links.scatter_sum(query_terms, wire=f32)
    doc_vec_grad = jnp.zeros((row_len, proj_width), f32)
    for position in range(3):
        unit_full, inv_scale = doc_prefix[position]
        grad_unit = doc_unit_grads[position]
        grad_part = inv_scale * (
            grad_unit - unit_full * jnp.sum(grad_unit * unit_full, axis=-1, keepdims=True)
        )
        doc_vec_grad = doc_vec_grad + jnp.pad(
            grad_part, ((0, 0), (0, proj_width - levels[position]))
        )
    grad_vectors = jnp.concatenate([doc_vec_grad, query_vec_grad], axis=0).astype(bf16)

    def spread_rows_of(full):
        return full.reshape(count, full.shape[0] // count, full.shape[1])

    proj_grad = matmul_left_t(second_low, grad_vectors)
    grad_second = matmul_right_t(grad_vectors, full_proj)
    grad_mid, gain_two, bias_two = layer_norm_back(
        grad_second, second_normed, second_scale, full_gains[1]
    )
    grad_ffn = grad_mid.astype(bf16)
    down_grad = matmul_left_t(gelu_out, grad_ffn)
    down_shard = links.scatter_sum(spread_rows_of(down_grad), 1)
    down_bias = jnp.sum(grad_ffn, axis=0, dtype=f32)
    grad_gelu = matmul_right_t(grad_ffn, full_down)
    gelu_back = jax.vjp(lambda pre_act: jax.nn.gelu(pre_act, approximate=False), up_pre)[1]
    grad_up = gelu_back(grad_gelu)[0].astype(bf16)
    upbias_grad = jnp.sum(grad_up, axis=0, dtype=f32)
    up_grad = matmul_left_t(first_low, grad_up)
    up_shard = links.scatter_sum(spread_rows_of(up_grad), 0)
    grad_first = grad_mid + matmul_right_t(grad_up, full_up)
    grad_res, gain_one, bias_one = layer_norm_back(
        grad_first, first_normed, first_scale, full_gains[0]
    )
    grad_attn = grad_res.astype(bf16)
    out_bias = jnp.sum(grad_attn, axis=0, dtype=f32)
    out_grad = jnp.concatenate([matmul_left_t(c, grad_attn) for c in contexts], axis=0)
    out_proj_shard = links.scatter_sum(
        spread_rows_of(jnp.concatenate([out_grad, proj_grad], axis=1)), 0
    )
    input_grad = grad_res
    query_bias, value_bias, qkv_shards = [], [], []
    for side in range(2):
        grad_context = matmul_right_t(
            grad_attn, full_out[side * part : (side + 1) * part]
        ).astype(bf16)
        grad_qkv = attention_backward(
            qkv[side], grad_context, contexts[side], *saved[side], segrow, segcol, bounds,
            row_len, span,
        )
        query_bias.append(jnp.sum(grad_qkv[:, :part], axis=0, dtype=f32))
        value_bias.append(jnp.sum(grad_qkv[:, 2 * part :], axis=0, dtype=f32))
        qkv_grad = matmul_left_t(tokens, grad_qkv)
        qkv_shards.append(links.scatter_sum(spread_rows_of(qkv_grad), side))
        input_grad = input_grad + matmul_right_t(grad_qkv, full_qkv[side])
    bias_grads = jnp.stack(
        [
            jnp.concatenate(query_bias),
            jnp.concatenate(value_bias),
            out_bias,
            bias_one,
            down_bias,
            bias_two,
            gain_one,
            gain_two,
        ],
        axis=0,
    )
    small_grads = jnp.concatenate(
        [
            bias_grads.reshape(8, count, shard_cols).transpose(1, 0, 2).reshape(count, -1),
            upbias_grad.reshape(count, -1),
        ],
        axis=1,
    )
    small_shard = links.scatter_sum(small_grads[:, None, :], 0, wire=f32)[0]
    shards = [
        jnp.concatenate([s[:, i * part : (i + 1) * part] for s in qkv_shards], axis=1)
        for i in range(3)
    ]
    return (
        loss,
        input_grad[:row_len].reshape(1, row_len, model_width),
        input_grad[row_len:].reshape(query_count, span, model_width),
        shards[0],
        shards[1],
        shards[2],
        out_proj_shard[:, :model_width],
        up_shard,
        down_shard,
        out_proj_shard[:, model_width:],
        small_shard[: 6 * shard_cols].reshape(6, shard_cols),
        small_shard[6 * shard_cols : 8 * shard_cols].reshape(2, shard_cols),
        small_shard[8 * shard_cols :],
    )


def solution(mesh):
    return jax.shard_map(
        partial(body, make_links(mesh)),
        mesh=mesh,
        in_specs=(
            P(("dp", "fsdp"), None, None),
            P(("dp", "fsdp"), None, None),
            P(("dp", "fsdp"), None),
            P(("dp", "fsdp"), None),
            P(("dp", "fsdp"), None),
            P(("dp", "fsdp"), None),
            P(("dp", "fsdp"), None),
            P(("dp", "fsdp"), None),
            P(("dp", "fsdp"), None),
            P(None, ("dp", "fsdp")),
            P(None, ("dp", "fsdp")),
            P(("dp", "fsdp")),
            P(("dp", "fsdp"), None),
            P(),
        ),
        out_specs=(
            P(),
            P(("dp", "fsdp"), None, None),
            P(("dp", "fsdp"), None, None),
            P(("dp", "fsdp"), None),
            P(("dp", "fsdp"), None),
            P(("dp", "fsdp"), None),
            P(("dp", "fsdp"), None),
            P(("dp", "fsdp"), None),
            P(("dp", "fsdp"), None),
            P(("dp", "fsdp"), None),
            P(None, ("dp", "fsdp")),
            P(None, ("dp", "fsdp")),
            P(("dp", "fsdp")),
        ),
        check_vma=False,
    )
```

```python
from functools import partial

import jax
import jax.numpy as jnp
from jax import lax
from jax.experimental import pallas as pl
from jax.experimental.pallas import tpu as pltpu
from jax.sharding import PartitionSpec as P

softness = 0.1
sharpness_divisor = 0.2
norm_eps = 1e-05
unit_eps = 1e-06
root_half = 0.7071067811865476
density_peak = 0.3989422804014327
head_width = 64
block_queries = 16
masked_score = -1e30
rate = 0.125 * 1.4426950408889634
q_rows = 256
k_rows = 256
f32 = jnp.float32
bf16 = jnp.bfloat16
AXES = ("dp", "fsdp")

def matmul_plain(left, right):
    return jnp.dot(left, right, preferred_element_type=jnp.float32)


def matmul_right_t(left, right):
    return lax.dot_general(
        left, right, (((1,), (1,)), ((), ())), preferred_element_type=jnp.float32
    )


def matmul_left_t(left, right):
    return lax.dot_general(
        left, right, (((0,), (0,)), ((), ())), preferred_element_type=jnp.float32
    )


def layer_norm_parts(values, gain_row, bias_row):
    center = values - jnp.mean(values, axis=-1, keepdims=True)
    spread = jnp.mean(center * center, axis=-1, keepdims=True)
    inv_scale = lax.rsqrt(spread + norm_eps)
    normed = center * inv_scale
    return (normed * gain_row + bias_row, normed, inv_scale)


def layer_norm_back(grad_out, normed, inv_scale, gain_row):
    grad_norm = grad_out * gain_row
    mean_grad = jnp.mean(grad_norm, axis=-1, keepdims=True)
    mean_proj = jnp.mean(grad_norm * normed, axis=-1, keepdims=True)
    grad_in = inv_scale * (grad_norm - mean_grad - normed * mean_proj)
    return (grad_in, jnp.sum(grad_out * normed, axis=0), jnp.sum(grad_out, axis=0))


def unit_prefix(vectors, level_width):
    part_cols = vectors[..., :level_width].astype(jnp.float32)
    inv_scale = lax.rsqrt(jnp.sum(part_cols * part_cols, axis=-1, keepdims=True) + unit_eps)
    return (part_cols * inv_scale, inv_scale)


def dot_nt(a,b): return lax.dot_general(a,b,(((1,),(1,)),((),())),preferred_element_type=f32)
def dot_nn(a,b): return jnp.dot(a,b,preferred_element_type=f32)

def stack_heads(block, first):
    zero=jnp.zeros_like(block)
    return jnp.concatenate([jnp.where(first,block,zero),jnp.where(first,zero,block)],axis=0)

def attend_forward(row_len, qb, kb, lanes, span, bounds, segrow, segcol, q_ref,k_ref,v_ref,ctx_ref,lse_ref,qlse_ref,vt_ref):
    units=lanes//128
    tokens=q_ref.shape[0]
    first_q=lax.broadcasted_iota(jnp.int32,(qb,128),1)<64
    top=lax.broadcasted_iota(jnp.int32,(128,qb),0)<64
    vt_ref[...]=v_ref[...].T
    def q_step(i,_):
        rows=pl.ds(pl.multiple_of(i*qb,qb),qb)
        own=segrow[pl.ds(i,1),:]
        stacked=[stack_heads(q_ref[rows,pl.ds(u*128,128)],first_q) for u in range(units)]
        def k_step(j,carry):
            keys=pl.ds(pl.multiple_of(j*kb,kb),kb)
            allowed=segcol[keys,:]==own
            out=[]
            for u in range(units):
                peak,total,acc=carry[u]
                s=jnp.where(allowed,dot_nt(k_ref[keys,pl.ds(u*128,128)],stacked[u]),masked_score)
                new=jnp.maximum(peak,jnp.max(s,axis=0,keepdims=True))
                p=jnp.exp2((s-new)*rate)
                fade=jnp.exp2((peak-new)*rate)
                total=total*fade+jnp.sum(p,axis=0,keepdims=True)
                acc=acc*fade+dot_nn(vt_ref[pl.ds(u*128,128),keys],p.astype(bf16))
                out.append((new,total,acc))
            return tuple(out)
        start=tuple((jnp.full((1,2*qb),masked_score,f32),jnp.zeros((1,2*qb),f32),jnp.zeros((128,2*qb),f32)) for u in range(units))
        res=lax.fori_loop(bounds[0,i],bounds[1,i],k_step,start)
        for u in range(units):
            peak,total,acc=res[u]
            acc=acc/total
            o=jnp.where(top,acc[:,:qb],acc[:,qb:])
            ctx_ref[rows,pl.ds(u*128,128)]=o.T.astype(bf16)
            lse_ref[u,pl.ds(i,1),:]=peak*rate+jnp.log2(total)
        return 0
    lax.fori_loop(0,row_len//qb,q_step,0)
    nq=tokens-row_len
    firstn=lax.broadcasted_iota(jnp.int32,(nq,128),1)<64
    own=lax.broadcasted_iota(jnp.int32,(nq,2*nq),0)//span
    other=(lax.broadcasted_iota(jnp.int32,(nq,2*nq),1)%nq)//span
    keep=own==other
    for u in range(units):
        cols=pl.ds(u*128,128)
        st=stack_heads(q_ref[row_len:,cols],firstn)
        s=jnp.where(keep,dot_nt(k_ref[row_len:,cols],st),masked_score)
        peak=jnp.max(s,axis=0,keepdims=True)
        p=jnp.exp2((s-peak)*rate)
        total=jnp.sum(p,axis=0,keepdims=True)
        p=(p/total).astype(bf16)
        acc=lax.dot_general(p,v_ref[row_len:,cols],(((0,),(0,)),((),())),preferred_element_type=f32)
        ctx_ref[row_len:,cols]=jnp.where(firstn,acc[:nq],acc[nq:]).astype(bf16)
        qlse_ref[u,:,:]=peak*rate+jnp.log2(total)

def attention_forward(qkv,segrow,segcol,bounds,row_len,span):
    tokens=qkv.shape[0]
    width=qkv.shape[1]//3
    qb,kb,lanes=q_rows,k_rows,width
    nq=tokens-row_len
    steps=width//lanes
    def spec(off): return pl.BlockSpec((tokens,lanes),lambda p,*_:(0,p+off))
    full=lambda a: pl.BlockSpec(a.shape,lambda p,*_:(0,)*a.ndim)
    return pl.pallas_call(
        partial(attend_forward,row_len,qb,kb,lanes,span),
        out_shape=(jax.ShapeDtypeStruct((tokens,width),bf16),jax.ShapeDtypeStruct((width//128,row_len//qb,2*qb),f32),jax.ShapeDtypeStruct((width//128,1,2*nq),f32)),
        grid_spec=pltpu.PrefetchScalarGridSpec(num_scalar_prefetch=1,grid=(steps,),
            in_specs=[full(segrow),full(segcol),spec(0),spec(steps),spec(2*steps)],
            out_specs=[pl.BlockSpec((tokens,lanes),lambda p,*_:(0,p)),pl.BlockSpec((lanes//128,row_len//qb,2*qb),lambda p,*_:(p,0,0)),pl.BlockSpec((lanes//128,1,2*nq),lambda p,*_:(p,0,0))],
            scratch_shapes=[pltpu.VMEM((lanes,tokens),bf16)]),
        compiler_params=pltpu.CompilerParams(vmem_limit_bytes=48<<20),
    )(bounds,segrow,segcol,qkv,qkv,qkv)

def attend_backward(row_len, qb, kb, lanes, span, bounds, segrow, segcol, q_ref,k_ref,v_ref,g_ref,o_ref,lse_ref,qlse_ref,out_ref,kt_ref,dka,dva):
    dq_ref=out_ref.at[:,:lanes]; dk_ref=out_ref.at[:,lanes:2*lanes]; dv_ref=out_ref.at[:,2*lanes:]
    units=lanes//128
    tokens=q_ref.shape[0]
    first_q=lax.broadcasted_iota(jnp.int32,(qb,128),1)<64
    top=lax.broadcasted_iota(jnp.int32,(128,qb),0)<64
    kt_ref[...]=k_ref[...].T
    dka[...]=jnp.zeros_like(dka); dva[...]=jnp.zeros_like(dva)
    def q_step(i,_):
        rows=pl.ds(pl.multiple_of(i*qb,qb),qb)
        own=segrow[pl.ds(i,1),:]
        sq=[];sg=[];dr=[];ls=[]
        for u in range(units):
            cols=pl.ds(u*128,128)
            g=g_ref[rows,cols]
            sq.append(stack_heads(q_ref[rows,cols],first_q)); sg.append(stack_heads(g,first_q))
            t=(g.astype(f32)*o_ref[rows,cols].astype(f32)).T
            dr.append(jnp.concatenate([jnp.sum(t[:64],axis=0,keepdims=True),jnp.sum(t[64:],axis=0,keepdims=True)],axis=1))
            ls.append(lse_ref[u,pl.ds(i,1),:])
        def k_step(j,carry):
            keys=pl.ds(pl.multiple_of(j*kb,kb),kb)
            allowed=segcol[keys,:]==own
            out=[]
            for u in range(units):
                cols=pl.ds(u*128,128)
                s=jnp.where(allowed,dot_nt(k_ref[keys,cols],sq[u]),masked_score)
                p=jnp.exp2(s*rate-ls[u])
                dp=dot_nt(v_ref[keys,cols],sg[u])
                ds=(p*(dp-dr[u])).astype(bf16)
                dva[keys,cols]+=dot_nn(p.astype(bf16),sg[u])
                dka[keys,cols]+=dot_nn(ds,sq[u])
                out.append(carry[u]+dot_nn(kt_ref[cols,keys],ds))
            return tuple(out)
        res=lax.fori_loop(bounds[0,i],bounds[1,i],k_step,tuple(jnp.zeros((128,2*qb),f32) for u in range(units)))
        for u in range(units):
            d=jnp.where(top,res[u][:,:qb],res[u][:,qb:])*0.125
            dq_ref[rows,pl.ds(u*128,128)]=d.T.astype(bf16)
        return 0
    lax.fori_loop(0,row_len//qb,q_step,0)
    dk_ref[:row_len,:]=(dka[...]*0.125).astype(bf16)
    dv_ref[:row_len,:]=dva[...].astype(bf16)
    nq=tokens-row_len
    firstn=lax.broadcasted_iota(jnp.int32,(nq,128),1)<64
    own=lax.broadcasted_iota(jnp.int32,(nq,2*nq),0)//span
    other=(lax.broadcasted_iota(jnp.int32,(nq,2*nq),1)%nq)//span
    keep=own==other
    for u in range(units):
        cols=pl.ds(u*128,128)
        q=q_ref[row_len:,cols]; k=k_ref[row_len:,cols]; v=v_ref[row_len:,cols]; g=g_ref[row_len:,cols]
        st=stack_heads(q,firstn); sg=stack_heads(g,firstn)
        s=jnp.where(keep,dot_nt(k,st),masked_score)
        p=jnp.exp2(s*rate-qlse_ref[u])
        dp=dot_nt(v,sg)
        ds=(p*(dp-jnp.sum(p*dp,axis=0,keepdims=True))).astype(bf16)
        dv_ref[row_len:,cols]=dot_nn(p.astype(bf16),sg).astype(bf16)
        dk_ref[row_len:,cols]=(dot_nn(ds,st)*0.125).astype(bf16)
        d=lax.dot_general(ds,k,(((0,),(0,)),((),())),preferred_element_type=f32)
        dq_ref[row_len:,cols]=(jnp.where(firstn,d[:nq],d[nq:])*0.125).astype(bf16)

def attention_backward(qkv,g,o,lse,qlse,segrow,segcol,bounds,row_len,span):
    tokens,width=g.shape
    qb,kb,lanes=q_rows,k_rows,width
    nq=tokens-row_len
    steps=width//lanes
    def spec(off): return pl.BlockSpec((tokens,lanes),lambda p,*_:(0,p+off))
    full=lambda a: pl.BlockSpec(a.shape,lambda p,*_:(0,)*a.ndim)
    sd=jax.ShapeDtypeStruct((tokens,3*width),bf16)
    return pl.pallas_call(
        partial(attend_backward,row_len,qb,kb,lanes,span),
        out_shape=sd,
        grid_spec=pltpu.PrefetchScalarGridSpec(num_scalar_prefetch=1,grid=(steps,),
            in_specs=[full(segrow),full(segcol)]+[spec(0),spec(1),spec(2),spec(0),spec(0)]+[pl.BlockSpec((lanes//128,row_len//qb,2*qb),lambda p,*_:(p,0,0)),pl.BlockSpec((lanes//128,1,2*nq),lambda p,*_:(p,0,0))],
            out_specs=pl.BlockSpec((tokens,3*lanes),lambda p,*_:(0,0)),
            scratch_shapes=[pltpu.VMEM((lanes,tokens),bf16),pltpu.VMEM((row_len,lanes),f32),pltpu.VMEM((row_len,lanes),f32)]),
        compiler_params=pltpu.CompilerParams(vmem_limit_bytes=56<<20),
    )(bounds,segrow,segcol,qkv,qkv,qkv,g,o,lse,qlse)


def after(value, *earlier):
    return lax.optimization_barrier((value, *earlier))[0]


class Growing:
    def __init__(self, links, shard, lane):
        self.links, self.order, self.block = links, list(links.orders[lane]), shard.shape
        self.held = shard.reshape((1,) * links.bits + shard.shape)

    def wait(self, *earlier):
        self.held = after(self.held, *earlier)

    def step(self):
        place = self.order.pop(0)
        axis = self.links.bits - 1 - place
        mine = self.links.side(place)
        held = self.held
        arrived = self.links.swap(held, 1 << place)
        both = jnp.zeros(held.shape[:axis] + (2,) + held.shape[axis + 1 :], held.dtype)
        both = lax.dynamic_update_slice_in_dim(both, held, mine, axis)
        self.held = lax.dynamic_update_slice_in_dim(both, arrived, 1 - mine, axis)

    def full(self):
        while self.order:
            self.step()
        return self.held.reshape((self.links.count,) + self.block)


class Shrinking:
    def __init__(self, links, blocks, lane, wire):
        self.links, self.order, self.block = links, list(links.orders[lane]), blocks.shape[1:]
        self.wire = wire
        self.held = blocks.astype(wire).reshape((2,) * links.bits + self.block)

    def wait(self, *earlier):
        self.held = after(self.held, *earlier)

    def step(self):
        place = self.order.pop()
        axis = self.links.bits - 1 - place
        mine = self.links.side(place)
        leaving = lax.dynamic_slice_in_dim(self.held, 1 - mine, 1, axis)
        kept = lax.dynamic_slice_in_dim(self.held, mine, 1, axis)
        total = kept.astype(f32) + self.links.swap(leaving, 1 << place).astype(f32)
        self.held = total.astype(self.wire) if self.order else total

    def mine(self):
        while self.order:
            self.step()
        return self.held.reshape(self.block)


class Links:
    def __init__(self, dp, fsdp):
        self.dp, self.fsdp, self.count = dp, fsdp, dp * fsdp
        self.bits = self.count.bit_length() - 1
        inner_bits = fsdp.bit_length() - 1
        low, high = list(range(inner_bits)), list(range(inner_bits, self.bits))
        inner, rest = low[:1], low[1:]
        near, far = high[:1], high[1:][::-1]
        self.orders = (far + rest[::-1] + near + inner, far + near + rest[::-1] + inner)

    def side(self, place):
        return (lax.axis_index(AXES) >> place) & 1

    def swap(self, value, bit):
        return lax.ppermute(value, AXES, [(d, d ^ bit) for d in range(self.count)])

    def growing(self, shard, lane=0):
        return Growing(self, shard, lane)

    def shrinking(self, blocks, lane=0, wire=bf16):
        return Shrinking(self, blocks, lane, wire)

    def total(self, value):
        for place in self.orders[0]:
            value = value + self.swap(value, 1 << place)
        return value


class Whole:
    def __init__(self, value):
        self.held = value

    def wait(self, *earlier):
        pass

    def step(self):
        pass

    def full(self):
        return self.held

    def mine(self):
        return self.held


class PlainLinks(Links):
    def growing(self, shard, lane=0):
        return Whole(lax.all_gather(shard, AXES, axis=0))

    def shrinking(self, blocks, lane=0, wire=bf16):
        return Whole(lax.psum_scatter(blocks, AXES, scatter_dimension=0, tiled=False))

    def total(self, value):
        return lax.psum(value, AXES)


def make_links(mesh):
    dp, fsdp = mesh.shape["dp"], mesh.shape["fsdp"]
    paired = (dp & (dp - 1)) == 0 and (fsdp & (fsdp - 1)) == 0 and dp * fsdp <= 64
    return (Links if paired else PlainLinks)(dp, fsdp)


def tables(lengths, row_len):
    ends = jnp.cumsum(lengths)
    starts = ends - lengths
    places = jnp.arange(row_len, dtype=jnp.int32)
    segment = jnp.sum((places[:, None] >= ends[None, :]).astype(jnp.int32), axis=1)
    rows = segment.reshape(row_len // q_rows, q_rows)
    ids = jnp.arange(lengths.shape[0])
    low = jnp.sum(jnp.where(rows[:, :1] == ids[None, :], starts[None, :], 0), axis=1)
    high = jnp.sum(jnp.where(rows[:, -1:] == ids[None, :], ends[None, :], 0), axis=1)
    bounds = jnp.stack([low // k_rows, (high + k_rows - 1) // k_rows]).astype(jnp.int32)
    return segment, jnp.concatenate([rows, rows], axis=1), segment[:, None], bounds


def body(
    links,
    doc_hidden,
    query_hidden,
    w_query,
    w_key,
    w_value,
    w_out,
    w_up,
    w_down,
    w_proj,
    biases,
    gains,
    up_bias,
    seg_lengths,
    positives,
):
    count = links.count
    row_len = doc_hidden.shape[1]
    model_width = doc_hidden.shape[2]
    query_count = query_hidden.shape[0]
    span = query_hidden.shape[1]
    doc_slots = seg_lengths.shape[1] - 1
    proj_width = w_proj.shape[1]
    ff = up_bias.shape[0] * count
    shard_cols = biases.shape[1]
    shard_rows = w_query.shape[0]
    part = model_width // 2
    small = jnp.concatenate(
        [biases.reshape(-1), gains.reshape(-1), up_bias.reshape(-1)], axis=0
    )[None]

    def rows_of(full):
        return full.reshape(full.shape[0] * full.shape[1], full.shape[2])

    sides = []
    for side in range(2):
        cut = slice(side * part, (side + 1) * part)
        shard = jnp.concatenate([w_query[:, cut], w_key[:, cut], w_value[:, cut]], axis=1)
        sides.append(links.growing(shard, side))
    small_part = links.growing(small, 0)
    out_part = links.growing(jnp.concatenate([w_out, w_proj], axis=1), 0)
    up_part = links.growing(w_up, 0)
    down_part = links.growing(w_down, 1)
    for hop in range(4):
        for one in sides + [small_part]:
            one.step()
        for one in (out_part, up_part, down_part):
            one.wait(sides[0].held, sides[1].held)
            if hop < 3:
                one.step()
    for one in sides + [small_part]:
        one.step()
        one.wait(up_part.held, down_part.held)
    for one in (out_part, up_part, down_part):
        one.step()
    small_full = small_part.full().reshape(count, -1)
    full_qkv = [rows_of(one.full()) for one in sides]
    full_biases = (
        small_full[:, : 6 * shard_cols]
        .reshape(count, 6, shard_cols)
        .transpose(1, 0, 2)
        .reshape(6, model_width)
        .astype(f32)
    )
    full_gains = (
        small_full[:, 6 * shard_cols : 8 * shard_cols]
        .reshape(count, 2, shard_cols)
        .transpose(1, 0, 2)
        .reshape(2, model_width)
        .astype(f32)
    )
    full_upbias = small_full[:, 8 * shard_cols :].reshape(ff).astype(f32)

    tokens = jnp.concatenate(
        [doc_hidden[0], query_hidden.reshape(query_count * span, model_width)], axis=0
    )
    segment, segrow, segcol, bounds = tables(seg_lengths[0], row_len)
    slot_ids = jnp.arange(doc_slots, dtype=jnp.int32)
    member = (segment[:, None] == slot_ids[None, :]).astype(f32)
    member_t = (slot_ids[:, None] == segment[None, :]).astype(f32)
    zero_row = jnp.zeros((part,), f32)
    qkv, contexts, saved = [], [], []
    for side in range(2):
        cut = slice(side * part, (side + 1) * part)
        bias = jnp.concatenate([full_biases[0, cut], zero_row, full_biases[1, cut]])
        qkv.append((matmul_plain(tokens, full_qkv[side]) + bias).astype(bf16))
        context, lse, query_lse = attention_forward(
            qkv[side], segrow, segcol, bounds, row_len, span
        )
        contexts.append(context)
        saved.append((lse, query_lse))
    contexts[1] = after(contexts[1], up_part.held, down_part.held)
    out_proj = rows_of(out_part.full())
    full_out, full_proj = out_proj[:, :model_width], out_proj[:, model_width:]
    full_up = rows_of(up_part.full())
    full_down = rows_of(down_part.full())
    attn_out = (
        matmul_plain(contexts[0], full_out[:part])
        + matmul_plain(contexts[1], full_out[part:])
        + full_biases[2]
    )
    first_out, first_normed, first_scale = layer_norm_parts(
        tokens.astype(f32) + attn_out, full_gains[0], full_biases[3]
    )
    first_low = first_out.astype(bf16)
    up_pre = matmul_plain(first_low, full_up) + full_upbias
    share = 0.5 * (1.0 + lax.erf(up_pre * root_half))
    gelu_out = (up_pre * share).astype(bf16)
    density = jnp.exp(-0.5 * up_pre * up_pre) * density_peak
    slope = (share + up_pre * density).astype(bf16)
    gelu_out, slope = lax.optimization_barrier((gelu_out, slope))
    ffn_out = matmul_plain(gelu_out, full_down) + full_biases[4]
    second_out, second_normed, second_scale = layer_norm_parts(
        first_out + ffn_out, full_gains[1], full_biases[5]
    )
    second_low = second_out.astype(bf16)
    vectors = matmul_plain(second_low, full_proj).astype(bf16)
    doc_vectors = vectors[:row_len]
    query_vectors = vectors[row_len:].reshape(query_count * span, proj_width)
    every_query = links.growing(query_vectors).full().reshape(count * query_count, span, proj_width)
    query_total = every_query.shape[0]
    block_count = query_total // block_queries
    levels = (proj_width, proj_width * 3 // 4, proj_width // 2)
    doc_prefix = tuple((unit_prefix(doc_vectors, level_width) for level_width in levels))
    doc_lows = tuple((prefix_pair[0].astype(bf16) for prefix_pair in doc_prefix))

    def block_logits(one_block):
        row_total = one_block.shape[0] * span
        piled_entries = []
        for position in range(3):
            level_width = levels[position]
            unit_rows = (
                unit_prefix(one_block, level_width)[0].astype(bf16).reshape(row_total, level_width)
            )
            scores = matmul_right_t(unit_rows, doc_lows[position])
            doc_sums = jnp.dot(jnp.exp(scores / softness), member, precision=lax.Precision.HIGHEST)
            peak_match_score = jnp.sum(
                (softness * jnp.log(doc_sums)).reshape(one_block.shape[0], span, doc_slots),
                axis=1,
            )
            piled_entries.append(peak_match_score / (span * sharpness_divisor))
        return jnp.stack(piled_entries, axis=1)

    blocks = every_query.reshape(block_count, block_queries, span, proj_width)
    logits = lax.map(block_logits, blocks).reshape(query_total, 3, doc_slots)
    powers = jnp.exp(logits)
    local_sum = jnp.sum(powers, axis=-1)
    my_row = lax.axis_index(AXES)
    chosen = ((positives - my_row * doc_slots)[:, None] == slot_ids[None, :]).astype(f32)
    local_pick = jnp.sum(logits * chosen[:, None, :], axis=-1)
    both = links.total(jnp.concatenate([local_sum, local_pick], axis=1))
    all_sums, picked = both[:, :3], both[:, 3:]
    loss = jnp.sum(jnp.log(all_sums) - picked) / query_total
    score_derivative = (powers / all_sums[:, :, None] - chosen[:, None, :]) / query_total
    peak_match_derivative = score_derivative / (span * sharpness_divisor)

    def block_back(carry, inputs):
        one_block, grad_block = inputs
        block_size = one_block.shape[0]
        row_total = block_size * span
        grad_vectors = jnp.zeros((block_size, span, proj_width), f32)
        new_carry = []
        for position in range(3):
            level_width = levels[position]
            unit_full, inv_scale = unit_prefix(one_block, level_width)
            unit_rows = unit_full.astype(bf16).reshape(row_total, level_width)
            scores = matmul_right_t(unit_rows, doc_lows[position])
            score_powers = jnp.exp(scores / softness)
            doc_sums = jnp.dot(score_powers, member, precision=lax.Precision.HIGHEST)
            grad_rows = jnp.broadcast_to(
                grad_block[:, None, position, :], (block_size, span, doc_slots)
            ).reshape(row_total, doc_slots)
            spread_rows = jnp.dot(grad_rows / doc_sums, member_t, precision=lax.Precision.HIGHEST)
            grad_scores = (score_powers * spread_rows).astype(bf16)
            grad_unit = matmul_plain(grad_scores, doc_lows[position]).reshape(
                block_size, span, level_width
            )
            new_carry.append(carry[position] + matmul_left_t(grad_scores, unit_rows))
            grad_part = inv_scale * (
                grad_unit - unit_full * jnp.sum(grad_unit * unit_full, axis=-1, keepdims=True)
            )
            grad_vectors = grad_vectors + jnp.pad(
                grad_part, ((0, 0), (0, 0), (0, proj_width - level_width))
            )
        return (tuple(new_carry), grad_vectors)

    start_carry = tuple((jnp.zeros((row_len, level_width), f32) for level_width in levels))
    grad_blocks = peak_match_derivative.reshape(block_count, block_queries, 3, doc_slots)
    doc_unit_grads, query_terms = lax.scan(block_back, start_carry, (blocks, grad_blocks))
    query_terms = query_terms.reshape(count, query_count * span, proj_width)
    query_vec_grad = links.shrinking(query_terms, wire=f32).mine()
    doc_vec_grad = jnp.zeros((row_len, proj_width), f32)
    for position in range(3):
        unit_full, inv_scale = doc_prefix[position]
        grad_unit = doc_unit_grads[position]
        grad_part = inv_scale * (
            grad_unit - unit_full * jnp.sum(grad_unit * unit_full, axis=-1, keepdims=True)
        )
        doc_vec_grad = doc_vec_grad + jnp.pad(
            grad_part, ((0, 0), (0, proj_width - levels[position]))
        )
    grad_vectors = jnp.concatenate([doc_vec_grad, query_vec_grad], axis=0).astype(bf16)

    def spread_rows_of(full):
        return full.reshape(count, full.shape[0] // count, full.shape[1])

    proj_grad = matmul_left_t(second_low, grad_vectors)
    grad_second = matmul_right_t(grad_vectors, full_proj)
    grad_mid, gain_two, bias_two = layer_norm_back(
        grad_second, second_normed, second_scale, full_gains[1]
    )
    grad_ffn = grad_mid.astype(bf16)
    down_grad = matmul_left_t(gelu_out, grad_ffn)
    down_sum = links.shrinking(spread_rows_of(down_grad), 1)
    down_sum.step()
    down_bias = jnp.sum(grad_ffn, axis=0, dtype=f32)
    grad_gelu = matmul_right_t(grad_ffn, full_down)
    grad_up = (grad_gelu * slope.astype(f32)).astype(bf16)
    upbias_grad = jnp.sum(grad_up, axis=0, dtype=f32)
    up_grad = matmul_left_t(first_low, grad_up)
    up_sum = links.shrinking(spread_rows_of(up_grad), 0)
    up_sum.step()
    grad_first = grad_mid + matmul_right_t(after(grad_up, down_sum.held), full_up)
    down_sum.step()
    grad_res, gain_one, bias_one = layer_norm_back(
        grad_first, first_normed, first_scale, full_gains[0]
    )
    grad_attn = after(grad_res.astype(bf16), up_sum.held)
    up_sum.step()
    out_bias = jnp.sum(grad_attn, axis=0, dtype=f32)
    out_grad = jnp.concatenate([matmul_left_t(c, grad_attn) for c in contexts], axis=0)
    out_sum = links.shrinking(spread_rows_of(jnp.concatenate([out_grad, proj_grad], axis=1)), 0)
    out_sum.step()
    input_grad = grad_res
    query_bias, value_bias, qkv_sums = [], [], []
    earlier = (out_sum.held,)
    for side in range(2):
        grad_context = matmul_right_t(
            grad_attn, full_out[side * part : (side + 1) * part]
        ).astype(bf16)
        grad_qkv = attention_backward(
            qkv[side], after(grad_context, *earlier), contexts[side], *saved[side], segrow, segcol,
            bounds, row_len, span,
        )
        if side == 0:
            out_sum.step()
        else:
            grad_qkv = after(grad_qkv, up_sum.held, out_sum.held, qkv_sums[0].held)
            up_sum.step()
            qkv_sums[0].step()
        query_bias.append(jnp.sum(grad_qkv[:, :part], axis=0, dtype=f32))
        value_bias.append(jnp.sum(grad_qkv[:, 2 * part :], axis=0, dtype=f32))
        qkv_grad = matmul_left_t(tokens, grad_qkv)
        qkv_sums.append(links.shrinking(spread_rows_of(qkv_grad), side))
        qkv_sums[side].step()
        earlier = (down_sum.held, qkv_sums[0].held)
        if side == 0:
            down_sum.step()
            qkv_sums[0].step()
        input_grad = input_grad + matmul_right_t(grad_qkv, full_qkv[side])
    down_shard, up_shard, out_proj_shard = down_sum.mine(), up_sum.mine(), out_sum.mine()
    qkv_shards = [one.mine() for one in qkv_sums]
    bias_grads = jnp.stack(
        [
            jnp.concatenate(query_bias),
            jnp.concatenate(value_bias),
            out_bias,
            bias_one,
            down_bias,
            bias_two,
            gain_one,
            gain_two,
        ],
        axis=0,
    )
    small_grads = jnp.concatenate(
        [
            bias_grads.reshape(8, count, shard_cols).transpose(1, 0, 2).reshape(count, -1),
            upbias_grad.reshape(count, -1),
        ],
        axis=1,
    )
    small_shard = links.shrinking(small_grads[:, None, :], 0, wire=f32).mine()[0]
    shards = [
        jnp.concatenate([s[:, i * part : (i + 1) * part] for s in qkv_shards], axis=1)
        for i in range(3)
    ]
    return (
        loss,
        input_grad[:row_len].reshape(1, row_len, model_width),
        input_grad[row_len:].reshape(query_count, span, model_width),
        shards[0],
        shards[1],
        shards[2],
        out_proj_shard[:, :model_width],
        up_shard,
        down_shard,
        out_proj_shard[:, model_width:],
        small_shard[: 6 * shard_cols].reshape(6, shard_cols),
        small_shard[6 * shard_cols : 8 * shard_cols].reshape(2, shard_cols),
        small_shard[8 * shard_cols :],
    )


def solution(mesh):
    return jax.shard_map(
        partial(body, make_links(mesh)),
        mesh=mesh,
        in_specs=(
            P(("dp", "fsdp"), None, None),
            P(("dp", "fsdp"), None, None),
            P(("dp", "fsdp"), None),
            P(("dp", "fsdp"), None),
            P(("dp", "fsdp"), None),
            P(("dp", "fsdp"), None),
            P(("dp", "fsdp"), None),
            P(("dp", "fsdp"), None),
            P(("dp", "fsdp"), None),
            P(None, ("dp", "fsdp")),
            P(None, ("dp", "fsdp")),
            P(("dp", "fsdp")),
            P(("dp", "fsdp"), None),
            P(),
        ),
        out_specs=(
            P(),
            P(("dp", "fsdp"), None, None),
            P(("dp", "fsdp"), None, None),
            P(("dp", "fsdp"), None),
            P(("dp", "fsdp"), None),
            P(("dp", "fsdp"), None),
            P(("dp", "fsdp"), None),
            P(("dp", "fsdp"), None),
            P(("dp", "fsdp"), None),
            P(("dp", "fsdp"), None),
            P(None, ("dp", "fsdp")),
            P(None, ("dp", "fsdp")),
            P(("dp", "fsdp")),
        ),
        check_vma=False,
    )
```

```python
from functools import partial

import jax
import jax.numpy as jnp
from jax import lax
from jax.experimental import pallas as pl
from jax.experimental.pallas import tpu as pltpu
from jax.sharding import PartitionSpec as P

softness = 0.1
sharpness_divisor = 0.2
norm_eps = 1e-05
unit_eps = 1e-06
root_half = 0.7071067811865476
density_peak = 0.3989422804014327
head_width = 64
block_queries = 16
masked_score = -1e30
rate = 0.125 * 1.4426950408889634
q_rows = 256
k_rows = 256
f32 = jnp.float32
bf16 = jnp.bfloat16
AXES = ("dp", "fsdp")

def matmul_plain(left, right):
    return jnp.dot(left, right, preferred_element_type=jnp.float32)


def matmul_right_t(left, right):
    return lax.dot_general(
        left, right, (((1,), (1,)), ((), ())), preferred_element_type=jnp.float32
    )


def matmul_left_t(left, right):
    return lax.dot_general(
        left, right, (((0,), (0,)), ((), ())), preferred_element_type=jnp.float32
    )


def layer_norm_parts(values, gain_row, bias_row):
    center = values - jnp.mean(values, axis=-1, keepdims=True)
    spread = jnp.mean(center * center, axis=-1, keepdims=True)
    inv_scale = lax.rsqrt(spread + norm_eps)
    normed = center * inv_scale
    return (normed * gain_row + bias_row, normed, inv_scale)


def layer_norm_back(grad_out, normed, inv_scale, gain_row):
    grad_norm = grad_out * gain_row
    mean_grad = jnp.mean(grad_norm, axis=-1, keepdims=True)
    mean_proj = jnp.mean(grad_norm * normed, axis=-1, keepdims=True)
    grad_in = inv_scale * (grad_norm - mean_grad - normed * mean_proj)
    return (grad_in, jnp.sum(grad_out * normed, axis=0), jnp.sum(grad_out, axis=0))


def unit_prefix(vectors, level_width):
    part_cols = vectors[..., :level_width].astype(jnp.float32)
    inv_scale = lax.rsqrt(jnp.sum(part_cols * part_cols, axis=-1, keepdims=True) + unit_eps)
    return (part_cols * inv_scale, inv_scale)


def dot_nt(a,b): return lax.dot_general(a,b,(((1,),(1,)),((),())),preferred_element_type=f32)
def dot_nn(a,b): return jnp.dot(a,b,preferred_element_type=f32)

def stack_heads(block, first):
    zero=jnp.zeros_like(block)
    return jnp.concatenate([jnp.where(first,block,zero),jnp.where(first,zero,block)],axis=0)

def attend_forward(row_len, qb, kb, lanes, span, bounds, segrow, segcol, q_ref,k_ref,v_ref,ctx_ref,lse_ref,qlse_ref,vt_ref):
    units=lanes//128
    tokens=q_ref.shape[0]
    first_q=lax.broadcasted_iota(jnp.int32,(qb,128),1)<64
    top=lax.broadcasted_iota(jnp.int32,(128,qb),0)<64
    vt_ref[...]=v_ref[...].T
    def q_step(i,_):
        rows=pl.ds(pl.multiple_of(i*qb,qb),qb)
        own=segrow[pl.ds(i,1),:]
        stacked=[stack_heads(q_ref[rows,pl.ds(u*128,128)],first_q) for u in range(units)]
        def k_step(j,carry):
            keys=pl.ds(pl.multiple_of(j*kb,kb),kb)
            allowed=segcol[keys,:]==own
            out=[]
            for u in range(units):
                peak,total,acc=carry[u]
                s=jnp.where(allowed,dot_nt(k_ref[keys,pl.ds(u*128,128)],stacked[u]),masked_score)
                new=jnp.maximum(peak,jnp.max(s,axis=0,keepdims=True))
                p=jnp.exp2((s-new)*rate)
                fade=jnp.exp2((peak-new)*rate)
                total=total*fade+jnp.sum(p,axis=0,keepdims=True)
                acc=acc*fade+dot_nn(vt_ref[pl.ds(u*128,128),keys],p.astype(bf16))
                out.append((new,total,acc))
            return tuple(out)
        start=tuple((jnp.full((1,2*qb),masked_score,f32),jnp.zeros((1,2*qb),f32),jnp.zeros((128,2*qb),f32)) for u in range(units))
        res=lax.fori_loop(bounds[0,i],bounds[1,i],k_step,start)
        for u in range(units):
            peak,total,acc=res[u]
            acc=acc/total
            o=jnp.where(top,acc[:,:qb],acc[:,qb:])
            ctx_ref[rows,pl.ds(u*128,128)]=o.T.astype(bf16)
            lse_ref[u,pl.ds(i,1),:]=peak*rate+jnp.log2(total)
        return 0
    lax.fori_loop(0,row_len//qb,q_step,0)
    nq=tokens-row_len
    firstn=lax.broadcasted_iota(jnp.int32,(nq,128),1)<64
    own=lax.broadcasted_iota(jnp.int32,(nq,2*nq),0)//span
    other=(lax.broadcasted_iota(jnp.int32,(nq,2*nq),1)%nq)//span
    keep=own==other
    for u in range(units):
        cols=pl.ds(u*128,128)
        st=stack_heads(q_ref[row_len:,cols],firstn)
        s=jnp.where(keep,dot_nt(k_ref[row_len:,cols],st),masked_score)
        peak=jnp.max(s,axis=0,keepdims=True)
        p=jnp.exp2((s-peak)*rate)
        total=jnp.sum(p,axis=0,keepdims=True)
        p=(p/total).astype(bf16)
        acc=lax.dot_general(p,v_ref[row_len:,cols],(((0,),(0,)),((),())),preferred_element_type=f32)
        ctx_ref[row_len:,cols]=jnp.where(firstn,acc[:nq],acc[nq:]).astype(bf16)
        qlse_ref[u,:,:]=peak*rate+jnp.log2(total)

def attention_forward(qkv,segrow,segcol,bounds,row_len,span):
    tokens=qkv.shape[0]
    width=qkv.shape[1]//3
    qb,kb,lanes=q_rows,k_rows,width
    nq=tokens-row_len
    steps=width//lanes
    def spec(off): return pl.BlockSpec((tokens,lanes),lambda p,*_:(0,p+off))
    full=lambda a: pl.BlockSpec(a.shape,lambda p,*_:(0,)*a.ndim)
    return pl.pallas_call(
        partial(attend_forward,row_len,qb,kb,lanes,span),
        out_shape=(jax.ShapeDtypeStruct((tokens,width),bf16),jax.ShapeDtypeStruct((width//128,row_len//qb,2*qb),f32),jax.ShapeDtypeStruct((width//128,1,2*nq),f32)),
        grid_spec=pltpu.PrefetchScalarGridSpec(num_scalar_prefetch=1,grid=(steps,),
            in_specs=[full(segrow),full(segcol),spec(0),spec(steps),spec(2*steps)],
            out_specs=[pl.BlockSpec((tokens,lanes),lambda p,*_:(0,p)),pl.BlockSpec((lanes//128,row_len//qb,2*qb),lambda p,*_:(p,0,0)),pl.BlockSpec((lanes//128,1,2*nq),lambda p,*_:(p,0,0))],
            scratch_shapes=[pltpu.VMEM((lanes,tokens),bf16)]),
        compiler_params=pltpu.CompilerParams(vmem_limit_bytes=48<<20),
    )(bounds,segrow,segcol,qkv,qkv,qkv)

def attend_backward(row_len, qb, kb, lanes, span, bounds, segrow, segcol, q_ref,k_ref,v_ref,g_ref,o_ref,lse_ref,qlse_ref,out_ref,kt_ref,dka,dva):
    dq_ref=out_ref.at[:,:lanes]; dk_ref=out_ref.at[:,lanes:2*lanes]; dv_ref=out_ref.at[:,2*lanes:]
    units=lanes//128
    tokens=q_ref.shape[0]
    first_q=lax.broadcasted_iota(jnp.int32,(qb,128),1)<64
    top=lax.broadcasted_iota(jnp.int32,(128,qb),0)<64
    kt_ref[...]=k_ref[...].T
    dka[...]=jnp.zeros_like(dka); dva[...]=jnp.zeros_like(dva)
    def q_step(i,_):
        rows=pl.ds(pl.multiple_of(i*qb,qb),qb)
        own=segrow[pl.ds(i,1),:]
        sq=[];sg=[];dr=[];ls=[]
        for u in range(units):
            cols=pl.ds(u*128,128)
            g=g_ref[rows,cols]
            sq.append(stack_heads(q_ref[rows,cols],first_q)); sg.append(stack_heads(g,first_q))
            t=(g.astype(f32)*o_ref[rows,cols].astype(f32)).T
            dr.append(jnp.concatenate([jnp.sum(t[:64],axis=0,keepdims=True),jnp.sum(t[64:],axis=0,keepdims=True)],axis=1))
            ls.append(lse_ref[u,pl.ds(i,1),:])
        def k_step(j,carry):
            keys=pl.ds(pl.multiple_of(j*kb,kb),kb)
            allowed=segcol[keys,:]==own
            out=[]
            for u in range(units):
                cols=pl.ds(u*128,128)
                s=jnp.where(allowed,dot_nt(k_ref[keys,cols],sq[u]),masked_score)
                p=jnp.exp2(s*rate-ls[u])
                dp=dot_nt(v_ref[keys,cols],sg[u])
                ds=(p*(dp-dr[u])).astype(bf16)
                dva[keys,cols]+=dot_nn(p.astype(bf16),sg[u])
                dka[keys,cols]+=dot_nn(ds,sq[u])
                out.append(carry[u]+dot_nn(kt_ref[cols,keys],ds))
            return tuple(out)
        res=lax.fori_loop(bounds[0,i],bounds[1,i],k_step,tuple(jnp.zeros((128,2*qb),f32) for u in range(units)))
        for u in range(units):
            d=jnp.where(top,res[u][:,:qb],res[u][:,qb:])*0.125
            dq_ref[rows,pl.ds(u*128,128)]=d.T.astype(bf16)
        return 0
    lax.fori_loop(0,row_len//qb,q_step,0)
    dk_ref[:row_len,:]=(dka[...]*0.125).astype(bf16)
    dv_ref[:row_len,:]=dva[...].astype(bf16)
    nq=tokens-row_len
    firstn=lax.broadcasted_iota(jnp.int32,(nq,128),1)<64
    own=lax.broadcasted_iota(jnp.int32,(nq,2*nq),0)//span
    other=(lax.broadcasted_iota(jnp.int32,(nq,2*nq),1)%nq)//span
    keep=own==other
    for u in range(units):
        cols=pl.ds(u*128,128)
        q=q_ref[row_len:,cols]; k=k_ref[row_len:,cols]; v=v_ref[row_len:,cols]; g=g_ref[row_len:,cols]
        st=stack_heads(q,firstn); sg=stack_heads(g,firstn)
        s=jnp.where(keep,dot_nt(k,st),masked_score)
        p=jnp.exp2(s*rate-qlse_ref[u])
        dp=dot_nt(v,sg)
        ds=(p*(dp-jnp.sum(p*dp,axis=0,keepdims=True))).astype(bf16)
        dv_ref[row_len:,cols]=dot_nn(p.astype(bf16),sg).astype(bf16)
        dk_ref[row_len:,cols]=(dot_nn(ds,st)*0.125).astype(bf16)
        d=lax.dot_general(ds,k,(((0,),(0,)),((),())),preferred_element_type=f32)
        dq_ref[row_len:,cols]=(jnp.where(firstn,d[:nq],d[nq:])*0.125).astype(bf16)

def attention_backward(qkv,g,o,lse,qlse,segrow,segcol,bounds,row_len,span):
    tokens,width=g.shape
    qb,kb,lanes=q_rows,k_rows,width
    nq=tokens-row_len
    steps=width//lanes
    def spec(off): return pl.BlockSpec((tokens,lanes),lambda p,*_:(0,p+off))
    full=lambda a: pl.BlockSpec(a.shape,lambda p,*_:(0,)*a.ndim)
    sd=jax.ShapeDtypeStruct((tokens,3*width),bf16)
    return pl.pallas_call(
        partial(attend_backward,row_len,qb,kb,lanes,span),
        out_shape=sd,
        grid_spec=pltpu.PrefetchScalarGridSpec(num_scalar_prefetch=1,grid=(steps,),
            in_specs=[full(segrow),full(segcol)]+[spec(0),spec(1),spec(2),spec(0),spec(0)]+[pl.BlockSpec((lanes//128,row_len//qb,2*qb),lambda p,*_:(p,0,0)),pl.BlockSpec((lanes//128,1,2*nq),lambda p,*_:(p,0,0))],
            out_specs=pl.BlockSpec((tokens,3*lanes),lambda p,*_:(0,0)),
            scratch_shapes=[pltpu.VMEM((lanes,tokens),bf16),pltpu.VMEM((row_len,lanes),f32),pltpu.VMEM((row_len,lanes),f32)]),
        compiler_params=pltpu.CompilerParams(vmem_limit_bytes=56<<20),
    )(bounds,segrow,segcol,qkv,qkv,qkv,g,o,lse,qlse)


def after(value, *earlier):
    return lax.optimization_barrier((value, *earlier))[0]


class Growing:
    def __init__(self, links, shard, lane):
        self.links, self.order, self.block = links, list(links.orders[lane]), shard.shape
        self.held = shard.reshape((1,) * links.bits + shard.shape)

    def wait(self, *earlier):
        self.held = after(self.held, *earlier)

    def launch(self):
        self.place = self.order.pop(0)
        self.before = self.held
        self.arrived = self.links.swap(self.held, 1 << self.place)

    def merge(self, *earlier):
        axis = self.links.bits - 1 - self.place
        mine = self.links.side(self.place)
        held = self.held
        arrived = after(self.arrived, *earlier) if earlier else self.arrived
        both = jnp.zeros(held.shape[:axis] + (2,) + held.shape[axis + 1 :], held.dtype)
        both = lax.dynamic_update_slice_in_dim(both, held, mine, axis)
        self.held = lax.dynamic_update_slice_in_dim(both, arrived, 1 - mine, axis)

    def full(self):
        while self.order:
            self.launch()
            self.merge()
        return self.held.reshape((self.links.count,) + self.block)


class Shrinking:
    def __init__(self, links, blocks, lane, wire):
        self.links, self.order, self.block = links, list(links.orders[lane]), blocks.shape[1:]
        self.wire = wire
        self.held = blocks.astype(wire).reshape((2,) * links.bits + self.block)

    def wait(self, *earlier):
        self.held = after(self.held, *earlier)

    def launch(self):
        self.place = self.order.pop()
        axis = self.links.bits - 1 - self.place
        self.leaving = lax.dynamic_slice_in_dim(
            self.held, 1 - self.links.side(self.place), 1, axis
        )
        self.arrived = self.links.swap(self.leaving, 1 << self.place)

    def merge(self, *earlier):
        axis = self.links.bits - 1 - self.place
        kept = lax.dynamic_slice_in_dim(self.held, self.links.side(self.place), 1, axis)
        arrived = after(self.arrived, *earlier) if earlier else self.arrived
        total = kept.astype(f32) + arrived.astype(f32)
        self.held = total.astype(self.wire) if self.order else total

    def mine(self):
        while self.order:
            self.launch()
            self.merge()
        return self.held.reshape(self.block)


class Links:
    def __init__(self, dp, fsdp):
        self.dp, self.fsdp, self.count = dp, fsdp, dp * fsdp
        self.bits = self.count.bit_length() - 1
        inner_bits = fsdp.bit_length() - 1
        low, high = list(range(inner_bits)), list(range(inner_bits, self.bits))
        inner, rest = low[:1], low[1:]
        near, far = high[:1], high[1:][::-1]
        self.orders = (far + rest[::-1] + near + inner, far + near + rest[::-1] + inner)

    def side(self, place):
        return (lax.axis_index(AXES) >> place) & 1

    def swap(self, value, bit):
        return lax.ppermute(value, AXES, [(d, d ^ bit) for d in range(self.count)])

    def growing(self, shard, lane=0):
        return Growing(self, shard, lane)

    def shrinking(self, blocks, lane=0, wire=bf16):
        return Shrinking(self, blocks, lane, wire)

    def total(self, value):
        for place in self.orders[0]:
            value = value + self.swap(value, 1 << place)
        return value


class Whole:
    def __init__(self, value):
        self.held = self.before = self.leaving = value

    def wait(self, *earlier):
        pass

    def launch(self):
        pass

    def merge(self, *earlier):
        pass

    def full(self):
        return self.held

    def mine(self):
        return self.held


class PlainLinks(Links):
    def growing(self, shard, lane=0):
        return Whole(lax.all_gather(shard, AXES, axis=0))

    def shrinking(self, blocks, lane=0, wire=bf16):
        return Whole(lax.psum_scatter(blocks, AXES, scatter_dimension=0, tiled=False))

    def total(self, value):
        return lax.psum(value, AXES)


def make_links(mesh):
    dp, fsdp = mesh.shape["dp"], mesh.shape["fsdp"]
    paired = (dp & (dp - 1)) == 0 and (fsdp & (fsdp - 1)) == 0 and dp * fsdp <= 64
    return (Links if paired else PlainLinks)(dp, fsdp)


def tables(lengths, row_len):
    ends = jnp.cumsum(lengths)
    starts = ends - lengths
    places = jnp.arange(row_len, dtype=jnp.int32)
    segment = jnp.sum((places[:, None] >= ends[None, :]).astype(jnp.int32), axis=1)
    rows = segment.reshape(row_len // q_rows, q_rows)
    ids = jnp.arange(lengths.shape[0])
    low = jnp.sum(jnp.where(rows[:, :1] == ids[None, :], starts[None, :], 0), axis=1)
    high = jnp.sum(jnp.where(rows[:, -1:] == ids[None, :], ends[None, :], 0), axis=1)
    bounds = jnp.stack([low // k_rows, (high + k_rows - 1) // k_rows]).astype(jnp.int32)
    return segment, jnp.concatenate([rows, rows], axis=1), segment[:, None], bounds


def body(
    links,
    doc_hidden,
    query_hidden,
    w_query,
    w_key,
    w_value,
    w_out,
    w_up,
    w_down,
    w_proj,
    biases,
    gains,
    up_bias,
    seg_lengths,
    positives,
):
    count = links.count
    row_len = doc_hidden.shape[1]
    model_width = doc_hidden.shape[2]
    query_count = query_hidden.shape[0]
    span = query_hidden.shape[1]
    doc_slots = seg_lengths.shape[1] - 1
    proj_width = w_proj.shape[1]
    ff = up_bias.shape[0] * count
    shard_cols = biases.shape[1]
    shard_rows = w_query.shape[0]
    part = model_width // 2
    small = jnp.concatenate(
        [biases.reshape(-1), gains.reshape(-1), up_bias.reshape(-1)], axis=0
    )[None]

    def rows_of(full):
        return full.reshape(full.shape[0] * full.shape[1], full.shape[2])

    sides = []
    for side in range(2):
        cut = slice(side * part, (side + 1) * part)
        shard = jnp.concatenate([w_query[:, cut], w_key[:, cut], w_value[:, cut]], axis=1)
        sides.append(links.growing(shard, side))
    small_part = links.growing(small, 0)
    out_part = links.growing(jnp.concatenate([w_out, w_proj], axis=1), 0)
    up_part = links.growing(w_up, 0)
    down_part = links.growing(w_down, 1)
    rest = (out_part, up_part, down_part)
    for hop in range(5):
        for one in sides:
            one.launch()
        if hop > 0:
            small_part.wait(sides[0].before, sides[1].before)
        small_part.launch()
        for one in sides:
            one.merge()
        first = (sides[0].held, sides[1].held)
        small_part.merge(*first)
        if hop > 0 and hop < 4:
            for one in rest:
                one.merge(*first)
        if hop < 4:
            for one in rest:
                one.wait(*first)
                one.launch()
    small_full = small_part.full().reshape(count, -1)
    full_qkv = [rows_of(one.full()) for one in sides]
    full_biases = (
        small_full[:, : 6 * shard_cols]
        .reshape(count, 6, shard_cols)
        .transpose(1, 0, 2)
        .reshape(6, model_width)
        .astype(f32)
    )
    full_gains = (
        small_full[:, 6 * shard_cols : 8 * shard_cols]
        .reshape(count, 2, shard_cols)
        .transpose(1, 0, 2)
        .reshape(2, model_width)
        .astype(f32)
    )
    full_upbias = small_full[:, 8 * shard_cols :].reshape(ff).astype(f32)

    tokens = jnp.concatenate(
        [doc_hidden[0], query_hidden.reshape(query_count * span, model_width)], axis=0
    )
    segment, segrow, segcol, bounds = tables(seg_lengths[0], row_len)
    slot_ids = jnp.arange(doc_slots, dtype=jnp.int32)
    member = (segment[:, None] == slot_ids[None, :]).astype(f32)
    member_t = (slot_ids[:, None] == segment[None, :]).astype(f32)
    zero_row = jnp.zeros((part,), f32)
    qkv, contexts, saved = [], [], []
    for side in range(2):
        cut = slice(side * part, (side + 1) * part)
        bias = jnp.concatenate([full_biases[0, cut], zero_row, full_biases[1, cut]])
        qkv.append((matmul_plain(tokens, full_qkv[side]) + bias).astype(bf16))
        context, lse, query_lse = attention_forward(
            qkv[side], segrow, segcol, bounds, row_len, span
        )
        if side == 0:
            out_part.merge(context)
            out_part.launch()
        contexts.append(context)
        saved.append((lse, query_lse))
    for one in (up_part, down_part):
        one.merge(*contexts)
        one.launch()
    contexts[1] = after(contexts[1], up_part.before, down_part.before)
    out_part.merge()
    out_proj = rows_of(out_part.full())
    full_out, full_proj = out_proj[:, :model_width], out_proj[:, model_width:]
    up_part.merge()
    down_part.merge()
    full_up = rows_of(up_part.full())
    full_down = rows_of(down_part.full())
    attn_out = (
        matmul_plain(contexts[0], full_out[:part])
        + matmul_plain(contexts[1], full_out[part:])
        + full_biases[2]
    )
    first_out, first_normed, first_scale = layer_norm_parts(
        tokens.astype(f32) + attn_out, full_gains[0], full_biases[3]
    )
    first_low = first_out.astype(bf16)
    up_pre = matmul_plain(first_low, full_up) + full_upbias
    share = 0.5 * (1.0 + lax.erf(up_pre * root_half))
    gelu_out = (up_pre * share).astype(bf16)
    density = jnp.exp(-0.5 * up_pre * up_pre) * density_peak
    slope = (share + up_pre * density).astype(bf16)
    gelu_out, slope = lax.optimization_barrier((gelu_out, slope))
    ffn_out = matmul_plain(gelu_out, full_down) + full_biases[4]
    second_out, second_normed, second_scale = layer_norm_parts(
        first_out + ffn_out, full_gains[1], full_biases[5]
    )
    second_low = second_out.astype(bf16)
    vectors = matmul_plain(second_low, full_proj).astype(bf16)
    doc_vectors = vectors[:row_len]
    query_vectors = vectors[row_len:].reshape(query_count * span, proj_width)
    every_query = links.growing(query_vectors).full().reshape(count * query_count, span, proj_width)
    query_total = every_query.shape[0]
    block_count = query_total // block_queries
    levels = (proj_width, proj_width * 3 // 4, proj_width // 2)
    doc_prefix = tuple((unit_prefix(doc_vectors, level_width) for level_width in levels))
    doc_lows = tuple((prefix_pair[0].astype(bf16) for prefix_pair in doc_prefix))

    def block_logits(one_block):
        row_total = one_block.shape[0] * span
        piled_entries = []
        for position in range(3):
            level_width = levels[position]
            unit_rows = (
                unit_prefix(one_block, level_width)[0].astype(bf16).reshape(row_total, level_width)
            )
            scores = matmul_right_t(unit_rows, doc_lows[position])
            doc_sums = jnp.dot(jnp.exp(scores / softness), member, precision=lax.Precision.HIGHEST)
            peak_match_score = jnp.sum(
                (softness * jnp.log(doc_sums)).reshape(one_block.shape[0], span, doc_slots),
                axis=1,
            )
            piled_entries.append(peak_match_score / (span * sharpness_divisor))
        return jnp.stack(piled_entries, axis=1)

    blocks = every_query.reshape(block_count, block_queries, span, proj_width)
    logits = lax.map(block_logits, blocks).reshape(query_total, 3, doc_slots)
    powers = jnp.exp(logits)
    local_sum = jnp.sum(powers, axis=-1)
    my_row = lax.axis_index(AXES)
    chosen = ((positives - my_row * doc_slots)[:, None] == slot_ids[None, :]).astype(f32)
    local_pick = jnp.sum(logits * chosen[:, None, :], axis=-1)
    both = links.total(jnp.concatenate([local_sum, local_pick], axis=1))
    all_sums, picked = both[:, :3], both[:, 3:]
    loss = jnp.sum(jnp.log(all_sums) - picked) / query_total
    score_derivative = (powers / all_sums[:, :, None] - chosen[:, None, :]) / query_total
    peak_match_derivative = score_derivative / (span * sharpness_divisor)

    def block_back(carry, inputs):
        one_block, grad_block = inputs
        block_size = one_block.shape[0]
        row_total = block_size * span
        grad_vectors = jnp.zeros((block_size, span, proj_width), f32)
        new_carry = []
        for position in range(3):
            level_width = levels[position]
            unit_full, inv_scale = unit_prefix(one_block, level_width)
            unit_rows = unit_full.astype(bf16).reshape(row_total, level_width)
            scores = matmul_right_t(unit_rows, doc_lows[position])
            score_powers = jnp.exp(scores / softness)
            doc_sums = jnp.dot(score_powers, member, precision=lax.Precision.HIGHEST)
            grad_rows = jnp.broadcast_to(
                grad_block[:, None, position, :], (block_size, span, doc_slots)
            ).reshape(row_total, doc_slots)
            spread_rows = jnp.dot(grad_rows / doc_sums, member_t, precision=lax.Precision.HIGHEST)
            grad_scores = (score_powers * spread_rows).astype(bf16)
            grad_unit = matmul_plain(grad_scores, doc_lows[position]).reshape(
                block_size, span, level_width
            )
            new_carry.append(carry[position] + matmul_left_t(grad_scores, unit_rows))
            grad_part = inv_scale * (
                grad_unit - unit_full * jnp.sum(grad_unit * unit_full, axis=-1, keepdims=True)
            )
            grad_vectors = grad_vectors + jnp.pad(
                grad_part, ((0, 0), (0, 0), (0, proj_width - level_width))
            )
        return (tuple(new_carry), grad_vectors)

    start_carry = tuple((jnp.zeros((row_len, level_width), f32) for level_width in levels))
    grad_blocks = peak_match_derivative.reshape(block_count, block_queries, 3, doc_slots)
    doc_unit_grads, query_terms = lax.scan(block_back, start_carry, (blocks, grad_blocks))
    query_terms = query_terms.reshape(count, query_count * span, proj_width)
    query_vec_grad = links.shrinking(query_terms, wire=f32).mine()
    doc_vec_grad = jnp.zeros((row_len, proj_width), f32)
    for position in range(3):
        unit_full, inv_scale = doc_prefix[position]
        grad_unit = doc_unit_grads[position]
        grad_part = inv_scale * (
            grad_unit - unit_full * jnp.sum(grad_unit * unit_full, axis=-1, keepdims=True)
        )
        doc_vec_grad = doc_vec_grad + jnp.pad(
            grad_part, ((0, 0), (0, proj_width - levels[position]))
        )
    grad_vectors = jnp.concatenate([doc_vec_grad, query_vec_grad], axis=0).astype(bf16)

    def spread_rows_of(full):
        return full.reshape(count, full.shape[0] // count, full.shape[1])

    proj_grad = matmul_left_t(second_low, grad_vectors)
    grad_second = matmul_right_t(grad_vectors, full_proj)
    grad_mid, gain_two, bias_two = layer_norm_back(
        grad_second, second_normed, second_scale, full_gains[1]
    )
    grad_ffn = grad_mid.astype(bf16)
    down_grad = matmul_left_t(gelu_out, grad_ffn)
    down_sum = links.shrinking(spread_rows_of(down_grad), 1)
    down_sum.launch()
    down_bias = jnp.sum(grad_ffn, axis=0, dtype=f32)
    grad_gelu = matmul_right_t(after(grad_ffn, down_sum.leaving), full_down)
    grad_up = (grad_gelu * slope.astype(f32)).astype(bf16)
    upbias_grad = jnp.sum(grad_up, axis=0, dtype=f32)
    up_grad = matmul_left_t(first_low, grad_up)
    up_sum = links.shrinking(spread_rows_of(up_grad), 0)
    up_sum.launch()
    down_sum.merge(up_sum.leaving)
    down_sum.launch()
    grad_first = grad_mid + matmul_right_t(after(grad_up, down_sum.leaving), full_up)
    grad_res, gain_one, bias_one = layer_norm_back(
        grad_first, first_normed, first_scale, full_gains[0]
    )
    up_sum.merge(grad_res)
    up_sum.launch()
    grad_attn = after(grad_res.astype(bf16), up_sum.leaving)
    out_bias = jnp.sum(grad_attn, axis=0, dtype=f32)
    out_grad = jnp.concatenate([matmul_left_t(c, grad_attn) for c in contexts], axis=0)
    out_sum = links.shrinking(spread_rows_of(jnp.concatenate([out_grad, proj_grad], axis=1)), 0)
    out_sum.launch()
    input_grad = grad_res
    query_bias, value_bias, qkv_sums = [], [], []
    grad_contexts = [
        matmul_right_t(grad_attn, full_out[side * part : (side + 1) * part]).astype(bf16)
        for side in range(2)
    ]
    down_sum.merge(*grad_contexts)
    down_sum.launch()
    earlier = (out_sum.leaving, down_sum.leaving)
    for side in range(2):
        grad_qkv = attention_backward(
            qkv[side], after(grad_contexts[side], *earlier), contexts[side], *saved[side], segrow,
            segcol, bounds, row_len, span,
        )
        if side == 1:
            up_sum.merge(grad_qkv)
            up_sum.launch()
            down_sum.merge(grad_qkv)
            down_sum.launch()
            qkv_sums[0].merge(grad_qkv)
            qkv_sums[0].launch()
            grad_qkv = after(grad_qkv, up_sum.leaving, down_sum.leaving, qkv_sums[0].leaving)
        query_bias.append(jnp.sum(grad_qkv[:, :part], axis=0, dtype=f32))
        value_bias.append(jnp.sum(grad_qkv[:, 2 * part :], axis=0, dtype=f32))
        qkv_grad = matmul_left_t(tokens, grad_qkv)
        if side == 0:
            qkv_sums.append(links.shrinking(spread_rows_of(qkv_grad), side))
        else:
            wide = qkv_grad.shape[1] // 2
            for lane in range(2):
                piece = qkv_grad[:, lane * wide : (lane + 1) * wide]
                qkv_sums.append(links.shrinking(spread_rows_of(piece), lane))
        for one in qkv_sums[side:]:
            one.launch()
        if side == 0:
            out_sum.merge(qkv_sums[0].leaving)
            out_sum.launch()
            earlier = (qkv_sums[0].leaving, out_sum.leaving)
        grad_qkv = after(grad_qkv, *[one.leaving for one in qkv_sums[side:]])
        input_grad = input_grad + matmul_right_t(grad_qkv, full_qkv[side])
    last = [one.leaving for one in qkv_sums[1:]]
    for one in (out_sum, up_sum, down_sum, qkv_sums[0]):
        one.merge(*last)
    for one in qkv_sums[1:]:
        one.merge()
    down_shard, up_shard, out_proj_shard = down_sum.mine(), up_sum.mine(), out_sum.mine()
    qkv_shards = [one.mine() for one in qkv_sums]
    qkv_shards = [qkv_shards[0], jnp.concatenate(qkv_shards[1:], axis=-1)]
    bias_grads = jnp.stack(
        [
            jnp.concatenate(query_bias),
            jnp.concatenate(value_bias),
            out_bias,
            bias_one,
            down_bias,
            bias_two,
            gain_one,
            gain_two,
        ],
        axis=0,
    )
    small_grads = jnp.concatenate(
        [
            bias_grads.reshape(8, count, shard_cols).transpose(1, 0, 2).reshape(count, -1),
            upbias_grad.reshape(count, -1),
        ],
        axis=1,
    )
    small_shard = links.shrinking(small_grads[:, None, :], 0, wire=f32).mine()[0]
    shards = [
        jnp.concatenate([s[:, i * part : (i + 1) * part] for s in qkv_shards], axis=1)
        for i in range(3)
    ]
    return (
        loss,
        input_grad[:row_len].reshape(1, row_len, model_width),
        input_grad[row_len:].reshape(query_count, span, model_width),
        shards[0],
        shards[1],
        shards[2],
        out_proj_shard[:, :model_width],
        up_shard,
        down_shard,
        out_proj_shard[:, model_width:],
        small_shard[: 6 * shard_cols].reshape(6, shard_cols),
        small_shard[6 * shard_cols : 8 * shard_cols].reshape(2, shard_cols),
        small_shard[8 * shard_cols :],
    )


def solution(mesh):
    return jax.shard_map(
        partial(body, make_links(mesh)),
        mesh=mesh,
        in_specs=(
            P(("dp", "fsdp"), None, None),
            P(("dp", "fsdp"), None, None),
            P(("dp", "fsdp"), None),
            P(("dp", "fsdp"), None),
            P(("dp", "fsdp"), None),
            P(("dp", "fsdp"), None),
            P(("dp", "fsdp"), None),
            P(("dp", "fsdp"), None),
            P(("dp", "fsdp"), None),
            P(None, ("dp", "fsdp")),
            P(None, ("dp", "fsdp")),
            P(("dp", "fsdp")),
            P(("dp", "fsdp"), None),
            P(),
        ),
        out_specs=(
            P(),
            P(("dp", "fsdp"), None, None),
            P(("dp", "fsdp"), None, None),
            P(("dp", "fsdp"), None),
            P(("dp", "fsdp"), None),
            P(("dp", "fsdp"), None),
            P(("dp", "fsdp"), None),
            P(("dp", "fsdp"), None),
            P(("dp", "fsdp"), None),
            P(("dp", "fsdp"), None),
            P(None, ("dp", "fsdp")),
            P(None, ("dp", "fsdp")),
            P(("dp", "fsdp")),
        ),
        check_vma=False,
    )
```

```python
from functools import partial

import jax
import jax.numpy as jnp
from jax import lax
from jax.experimental import pallas as pl
from jax.experimental.pallas import tpu as pltpu
from jax.sharding import PartitionSpec as P

softness = 0.1
sharpness_divisor = 0.2
norm_eps = 1e-05
unit_eps = 1e-06
root_half = 0.7071067811865476
density_peak = 0.3989422804014327
head_width = 64
block_queries = 8
masked_score = -1e30
rate = 0.125 * 1.4426950408889634
q_rows = 256
k_rows = 256
f32 = jnp.float32
bf16 = jnp.bfloat16
AXES = ("dp", "fsdp")

def matmul_plain(left, right):
    return jnp.dot(left, right, preferred_element_type=jnp.float32)


def matmul_right_t(left, right):
    return lax.dot_general(
        left, right, (((1,), (1,)), ((), ())), preferred_element_type=jnp.float32
    )


def matmul_left_t(left, right):
    return lax.dot_general(
        left, right, (((0,), (0,)), ((), ())), preferred_element_type=jnp.float32
    )


def layer_norm_parts(values, gain_row, bias_row):
    center = values - jnp.mean(values, axis=-1, keepdims=True)
    spread = jnp.mean(center * center, axis=-1, keepdims=True)
    inv_scale = lax.rsqrt(spread + norm_eps)
    normed = center * inv_scale
    return (normed * gain_row + bias_row, normed, inv_scale)


def layer_norm_back(grad_out, normed, inv_scale, gain_row):
    grad_norm = grad_out * gain_row
    mean_grad = jnp.mean(grad_norm, axis=-1, keepdims=True)
    mean_proj = jnp.mean(grad_norm * normed, axis=-1, keepdims=True)
    grad_in = inv_scale * (grad_norm - mean_grad - normed * mean_proj)
    return (grad_in, jnp.sum(grad_out * normed, axis=0), jnp.sum(grad_out, axis=0))


def dot_nt(a,b): return lax.dot_general(a,b,(((1,),(1,)),((),())),preferred_element_type=f32)
def dot_nn(a,b): return jnp.dot(a,b,preferred_element_type=f32)

def stack_heads(block, first):
    zero=jnp.zeros_like(block)
    return jnp.concatenate([jnp.where(first,block,zero),jnp.where(first,zero,block)],axis=0)

def attend_forward(row_len, qb, kb, lanes, span, bounds, segrow, segcol, q_ref,k_ref,v_ref,ctx_ref,lse_ref,qlse_ref,vt_ref):
    units=lanes//128
    tokens=q_ref.shape[0]
    first_q=lax.broadcasted_iota(jnp.int32,(qb,128),1)<64
    top=lax.broadcasted_iota(jnp.int32,(128,qb),0)<64
    vt_ref[...]=v_ref[...].T
    def q_step(i,_):
        rows=pl.ds(pl.multiple_of(i*qb,qb),qb)
        own=segrow[pl.ds(i,1),:]
        stacked=[stack_heads(q_ref[rows,pl.ds(u*128,128)],first_q) for u in range(units)]
        def k_step(j,carry):
            keys=pl.ds(pl.multiple_of(j*kb,kb),kb)
            allowed=segcol[keys,:]==own
            out=[]
            for u in range(units):
                peak,total,acc=carry[u]
                s=jnp.where(allowed,dot_nt(k_ref[keys,pl.ds(u*128,128)],stacked[u]),masked_score)
                new=jnp.maximum(peak,jnp.max(s,axis=0,keepdims=True))
                p=jnp.exp2((s-new)*rate)
                fade=jnp.exp2((peak-new)*rate)
                total=total*fade+jnp.sum(p,axis=0,keepdims=True)
                acc=acc*fade+dot_nn(vt_ref[pl.ds(u*128,128),keys],p.astype(bf16))
                out.append((new,total,acc))
            return tuple(out)
        start=tuple((jnp.full((1,2*qb),masked_score,f32),jnp.zeros((1,2*qb),f32),jnp.zeros((128,2*qb),f32)) for u in range(units))
        res=lax.fori_loop(bounds[0,i],bounds[1,i],k_step,start)
        for u in range(units):
            peak,total,acc=res[u]
            acc=acc/total
            o=jnp.where(top,acc[:,:qb],acc[:,qb:])
            ctx_ref[rows,pl.ds(u*128,128)]=o.T.astype(bf16)
            lse_ref[u,pl.ds(i,1),:]=peak*rate+jnp.log2(total)
        return 0
    lax.fori_loop(0,row_len//qb,q_step,0)
    nq=tokens-row_len
    firstn=lax.broadcasted_iota(jnp.int32,(nq,128),1)<64
    own=lax.broadcasted_iota(jnp.int32,(nq,2*nq),0)//span
    other=(lax.broadcasted_iota(jnp.int32,(nq,2*nq),1)%nq)//span
    keep=own==other
    for u in range(units):
        cols=pl.ds(u*128,128)
        st=stack_heads(q_ref[row_len:,cols],firstn)
        s=jnp.where(keep,dot_nt(k_ref[row_len:,cols],st),masked_score)
        peak=jnp.max(s,axis=0,keepdims=True)
        p=jnp.exp2((s-peak)*rate)
        total=jnp.sum(p,axis=0,keepdims=True)
        p=(p/total).astype(bf16)
        acc=lax.dot_general(p,v_ref[row_len:,cols],(((0,),(0,)),((),())),preferred_element_type=f32)
        ctx_ref[row_len:,cols]=jnp.where(firstn,acc[:nq],acc[nq:]).astype(bf16)
        qlse_ref[u,:,:]=peak*rate+jnp.log2(total)

def attention_forward(qkv,segrow,segcol,bounds,row_len,span):
    tokens=qkv.shape[0]
    width=qkv.shape[1]//3
    qb,kb,lanes=q_rows,k_rows,width
    nq=tokens-row_len
    steps=width//lanes
    def spec(off): return pl.BlockSpec((tokens,lanes),lambda p,*_:(0,p+off))
    full=lambda a: pl.BlockSpec(a.shape,lambda p,*_:(0,)*a.ndim)
    return pl.pallas_call(
        partial(attend_forward,row_len,qb,kb,lanes,span),
        out_shape=(jax.ShapeDtypeStruct((tokens,width),bf16),jax.ShapeDtypeStruct((width//128,row_len//qb,2*qb),f32),jax.ShapeDtypeStruct((width//128,1,2*nq),f32)),
        grid_spec=pltpu.PrefetchScalarGridSpec(num_scalar_prefetch=1,grid=(steps,),
            in_specs=[full(segrow),full(segcol),spec(0),spec(steps),spec(2*steps)],
            out_specs=[pl.BlockSpec((tokens,lanes),lambda p,*_:(0,p)),pl.BlockSpec((lanes//128,row_len//qb,2*qb),lambda p,*_:(p,0,0)),pl.BlockSpec((lanes//128,1,2*nq),lambda p,*_:(p,0,0))],
            scratch_shapes=[pltpu.VMEM((lanes,tokens),bf16)]),
        compiler_params=pltpu.CompilerParams(vmem_limit_bytes=48<<20),
    )(bounds,segrow,segcol,qkv,qkv,qkv)

def attend_backward(row_len, qb, kb, lanes, span, bounds, segrow, segcol, q_ref,k_ref,v_ref,g_ref,o_ref,lse_ref,qlse_ref,out_ref,kt_ref,dka,dva):
    dq_ref=out_ref.at[:,:lanes]; dk_ref=out_ref.at[:,lanes:2*lanes]; dv_ref=out_ref.at[:,2*lanes:]
    units=lanes//128
    tokens=q_ref.shape[0]
    first_q=lax.broadcasted_iota(jnp.int32,(qb,128),1)<64
    top=lax.broadcasted_iota(jnp.int32,(128,qb),0)<64
    kt_ref[...]=k_ref[...].T
    dka[...]=jnp.zeros_like(dka); dva[...]=jnp.zeros_like(dva)
    def q_step(i,_):
        rows=pl.ds(pl.multiple_of(i*qb,qb),qb)
        own=segrow[pl.ds(i,1),:]
        sq=[];sg=[];dr=[];ls=[]
        for u in range(units):
            cols=pl.ds(u*128,128)
            g=g_ref[rows,cols]
            sq.append(stack_heads(q_ref[rows,cols],first_q)); sg.append(stack_heads(g,first_q))
            t=(g.astype(f32)*o_ref[rows,cols].astype(f32)).T
            dr.append(jnp.concatenate([jnp.sum(t[:64],axis=0,keepdims=True),jnp.sum(t[64:],axis=0,keepdims=True)],axis=1))
            ls.append(lse_ref[u,pl.ds(i,1),:])
        def k_step(j,carry):
            keys=pl.ds(pl.multiple_of(j*kb,kb),kb)
            allowed=segcol[keys,:]==own
            out=[]
            for u in range(units):
                cols=pl.ds(u*128,128)
                s=jnp.where(allowed,dot_nt(k_ref[keys,cols],sq[u]),masked_score)
                p=jnp.exp2(s*rate-ls[u])
                dp=dot_nt(v_ref[keys,cols],sg[u])
                ds=(p*(dp-dr[u])).astype(bf16)
                dva[keys,cols]+=dot_nn(p.astype(bf16),sg[u])
                dka[keys,cols]+=dot_nn(ds,sq[u])
                out.append(carry[u]+dot_nn(kt_ref[cols,keys],ds))
            return tuple(out)
        res=lax.fori_loop(bounds[0,i],bounds[1,i],k_step,tuple(jnp.zeros((128,2*qb),f32) for u in range(units)))
        for u in range(units):
            d=jnp.where(top,res[u][:,:qb],res[u][:,qb:])*0.125
            dq_ref[rows,pl.ds(u*128,128)]=d.T.astype(bf16)
        return 0
    lax.fori_loop(0,row_len//qb,q_step,0)
    dk_ref[:row_len,:]=(dka[...]*0.125).astype(bf16)
    dv_ref[:row_len,:]=dva[...].astype(bf16)
    nq=tokens-row_len
    firstn=lax.broadcasted_iota(jnp.int32,(nq,128),1)<64
    own=lax.broadcasted_iota(jnp.int32,(nq,2*nq),0)//span
    other=(lax.broadcasted_iota(jnp.int32,(nq,2*nq),1)%nq)//span
    keep=own==other
    for u in range(units):
        cols=pl.ds(u*128,128)
        q=q_ref[row_len:,cols]; k=k_ref[row_len:,cols]; v=v_ref[row_len:,cols]; g=g_ref[row_len:,cols]
        st=stack_heads(q,firstn); sg=stack_heads(g,firstn)
        s=jnp.where(keep,dot_nt(k,st),masked_score)
        p=jnp.exp2(s*rate-qlse_ref[u])
        dp=dot_nt(v,sg)
        ds=(p*(dp-jnp.sum(p*dp,axis=0,keepdims=True))).astype(bf16)
        dv_ref[row_len:,cols]=dot_nn(p.astype(bf16),sg).astype(bf16)
        dk_ref[row_len:,cols]=(dot_nn(ds,st)*0.125).astype(bf16)
        d=lax.dot_general(ds,k,(((0,),(0,)),((),())),preferred_element_type=f32)
        dq_ref[row_len:,cols]=(jnp.where(firstn,d[:nq],d[nq:])*0.125).astype(bf16)

def attention_backward(qkv,g,o,lse,qlse,segrow,segcol,bounds,row_len,span):
    tokens,width=g.shape
    qb,kb,lanes=q_rows,k_rows,width
    nq=tokens-row_len
    steps=width//lanes
    def spec(off): return pl.BlockSpec((tokens,lanes),lambda p,*_:(0,p+off))
    full=lambda a: pl.BlockSpec(a.shape,lambda p,*_:(0,)*a.ndim)
    sd=jax.ShapeDtypeStruct((tokens,3*width),bf16)
    return pl.pallas_call(
        partial(attend_backward,row_len,qb,kb,lanes,span),
        out_shape=sd,
        grid_spec=pltpu.PrefetchScalarGridSpec(num_scalar_prefetch=1,grid=(steps,),
            in_specs=[full(segrow),full(segcol)]+[spec(0),spec(1),spec(2),spec(0),spec(0)]+[pl.BlockSpec((lanes//128,row_len//qb,2*qb),lambda p,*_:(p,0,0)),pl.BlockSpec((lanes//128,1,2*nq),lambda p,*_:(p,0,0))],
            out_specs=pl.BlockSpec((tokens,3*lanes),lambda p,*_:(0,0)),
            scratch_shapes=[pltpu.VMEM((lanes,tokens),bf16),pltpu.VMEM((row_len,lanes),f32),pltpu.VMEM((row_len,lanes),f32)]),
        compiler_params=pltpu.CompilerParams(vmem_limit_bytes=56<<20),
    )(bounds,segrow,segcol,qkv,qkv,qkv,g,o,lse,qlse)


def level_units(values, width):
    lanes = lax.broadcasted_iota(jnp.int32, values.shape, 1)
    part_cols = jnp.where(lanes < width, values, 0.0)
    inv_scale = lax.rsqrt(jnp.sum(part_cols * part_cols, axis=-1, keepdims=True) + unit_eps)
    return part_cols * inv_scale, inv_scale


def three_parts(values):
    top = values.astype(bf16)
    rest = values - top.astype(f32)
    middle = rest.astype(bf16)
    return top, middle, (rest - middle.astype(f32)).astype(bf16)


def exact_dot(values, marks):
    return sum(dot_nn(part, marks) for part in three_parts(values))


def keep_doc_units(levels, doc_ref, low_ref):
    @pl.when(pl.program_id(0) == 0)
    def _():
        docs = doc_ref[...].astype(f32)
        for position, width in enumerate(levels):
            low_ref[position] = level_units(docs, width)[0].astype(bf16)


def interact_forward(levels, span, doc_ref, member_ref, query_ref, logit_ref, sums_ref, low_ref):
    keep_doc_units(levels, doc_ref, low_ref)
    queries = query_ref[...].astype(f32)
    member = member_ref[...]
    for position, width in enumerate(levels):
        unit_rows = level_units(queries, width)[0].astype(bf16)
        powers = jnp.exp(dot_nt(unit_rows, low_ref[position]) / softness)
        doc_sums = exact_dot(powers, member)
        sums_ref[position] = doc_sums
        logs = (softness * jnp.log(doc_sums)).reshape(-1, span, doc_sums.shape[1])
        logit_ref[position] = jnp.sum(logs, axis=1) / (span * sharpness_divisor)


def interact_backward(
    levels, span, doc_ref, member_t_ref, query_ref, sums_ref, grad_ref, query_grad_ref,
    doc_grad_ref, low_ref, held_ref,
):
    keep_doc_units(levels, doc_ref, low_ref)

    @pl.when(pl.program_id(0) == 0)
    def _():
        held_ref[...] = jnp.zeros_like(held_ref)

    queries = query_ref[...].astype(f32)
    member_t = member_t_ref[...]
    total = jnp.zeros(queries.shape, f32)
    for position, width in enumerate(levels):
        unit_full, inv_scale = level_units(queries, width)
        unit_rows = unit_full.astype(bf16)
        powers = jnp.exp(dot_nt(unit_rows, low_ref[position]) / softness)
        grads = grad_ref[position]
        rows = jnp.broadcast_to(grads[:, None, :], (grads.shape[0], span, grads.shape[1]))
        rows = rows.reshape(-1, grads.shape[1]) / sums_ref[position]
        grad_scores = (powers * exact_dot(rows, member_t)).astype(bf16)
        grad_unit = dot_nn(grad_scores, low_ref[position])
        held_ref[position] += matmul_left_t(grad_scores, unit_rows)
        total = total + inv_scale * (
            grad_unit - unit_full * jnp.sum(grad_unit * unit_full, axis=-1, keepdims=True)
        )
    query_grad_ref[...] = total

    @pl.when(pl.program_id(0) == pl.num_programs(0) - 1)
    def _():
        docs = doc_ref[...].astype(f32)
        doc_total = jnp.zeros(docs.shape, f32)
        for position, width in enumerate(levels):
            unit_full, inv_scale = level_units(docs, width)
            grad_unit = held_ref[position]
            doc_total = doc_total + inv_scale * (
                grad_unit - unit_full * jnp.sum(grad_unit * unit_full, axis=-1, keepdims=True)
            )
        doc_grad_ref[...] = doc_total


def interaction_logits(levels, span, docs, member, queries):
    tokens, width = queries.shape
    row_len, slots = member.shape
    rows = block_queries * span
    return pl.pallas_call(
        partial(interact_forward, levels, span),
        grid=(tokens // rows,),
        out_shape=(
            jax.ShapeDtypeStruct((3, tokens // span, slots), f32),
            jax.ShapeDtypeStruct((3, tokens, slots), f32),
        ),
        in_specs=[
            pl.BlockSpec((row_len, width), lambda i: (0, 0)),
            pl.BlockSpec((row_len, slots), lambda i: (0, 0)),
            pl.BlockSpec((rows, width), lambda i: (i, 0)),
        ],
        out_specs=(
            pl.BlockSpec((3, block_queries, slots), lambda i: (0, i, 0)),
            pl.BlockSpec((3, rows, slots), lambda i: (0, i, 0)),
        ),
        scratch_shapes=[pltpu.VMEM((3, row_len, width), bf16)],
        compiler_params=pltpu.CompilerParams(vmem_limit_bytes=40 << 20),
    )(docs, member, queries)


def interaction_grads(levels, span, docs, member_t, queries, sums, grads):
    tokens, width = queries.shape
    slots, row_len = member_t.shape
    rows = block_queries * span
    return pl.pallas_call(
        partial(interact_backward, levels, span),
        grid=(tokens // rows,),
        out_shape=(
            jax.ShapeDtypeStruct((tokens, width), f32),
            jax.ShapeDtypeStruct((row_len, width), f32),
        ),
        in_specs=[
            pl.BlockSpec((row_len, width), lambda i: (0, 0)),
            pl.BlockSpec((slots, row_len), lambda i: (0, 0)),
            pl.BlockSpec((rows, width), lambda i: (i, 0)),
            pl.BlockSpec((3, rows, slots), lambda i: (0, i, 0)),
            pl.BlockSpec((3, block_queries, slots), lambda i: (0, i, 0)),
        ],
        out_specs=(
            pl.BlockSpec((rows, width), lambda i: (i, 0)),
            pl.BlockSpec((row_len, width), lambda i: (0, 0)),
        ),
        scratch_shapes=[
            pltpu.VMEM((3, row_len, width), bf16),
            pltpu.VMEM((3, row_len, width), f32),
        ],
        compiler_params=pltpu.CompilerParams(vmem_limit_bytes=40 << 20),
    )(docs, member_t, queries, sums, grads)


def after(value, *earlier):
    return lax.optimization_barrier((value, *earlier))[0]


class Growing:
    def __init__(self, links, shard, lane):
        self.links, self.order, self.block = links, list(links.orders[lane]), shard.shape
        self.held = shard.reshape((1,) * links.bits + shard.shape)

    def wait(self, *earlier):
        self.held = after(self.held, *earlier)

    def launch(self):
        self.place = self.order.pop(0)
        self.before = self.held
        self.arrived = self.links.swap(self.held, 1 << self.place)

    def merge(self, *earlier):
        axis = self.links.bits - 1 - self.place
        mine = self.links.side(self.place)
        held = self.held
        arrived = after(self.arrived, *earlier) if earlier else self.arrived
        shape = held.shape[:axis] + (2,) + held.shape[axis + 1 :]
        own = lax.broadcasted_iota(jnp.int32, shape, axis) == mine
        self.held = jnp.where(own, held, arrived)

    def full(self):
        while self.order:
            self.launch()
            self.merge()
        return self.held.reshape((self.links.count,) + self.block)


class Shrinking:
    def __init__(self, links, blocks, lane, wire):
        self.links, self.order, self.block = links, list(links.orders[lane]), blocks.shape[1:]
        self.wire = wire
        self.held = blocks.astype(wire).reshape((2,) * links.bits + self.block)

    def wait(self, *earlier):
        self.held = after(self.held, *earlier)

    def launch(self):
        if not self.order:
            return
        self.place = self.order.pop()
        axis = self.links.bits - 1 - self.place
        self.leaving = lax.dynamic_slice_in_dim(
            self.held, 1 - self.links.side(self.place), 1, axis
        )
        self.arrived = self.links.swap(self.leaving, 1 << self.place)

    def merge(self, *earlier):
        if self.arrived is None:
            return
        axis = self.links.bits - 1 - self.place
        kept = lax.dynamic_slice_in_dim(self.held, self.links.side(self.place), 1, axis)
        arrived = after(self.arrived, *earlier) if earlier else self.arrived
        total = kept.astype(f32) + arrived.astype(f32)
        self.held = total.astype(self.wire) if self.order else total
        self.arrived = None

    def mine(self):
        while self.order:
            self.launch()
            self.merge()
        return self.held.reshape(self.block)


class Links:
    def __init__(self, dp, fsdp):
        self.dp, self.fsdp, self.count = dp, fsdp, dp * fsdp
        self.bits = self.count.bit_length() - 1
        inner_bits = fsdp.bit_length() - 1
        low, high = list(range(inner_bits)), list(range(inner_bits, self.bits))
        inner, rest = low[:1], low[1:]
        near, far = high[:1], high[1:][::-1]
        self.orders = (far + rest[::-1] + near + inner, far + near + rest[::-1] + inner)

    def side(self, place):
        return (lax.axis_index(AXES) >> place) & 1

    def swap(self, value, bit):
        return lax.ppermute(value, AXES, [(d, d ^ bit) for d in range(self.count)])

    def growing(self, shard, lane=0):
        return Growing(self, shard, lane)

    def shrinking(self, blocks, lane=0, wire=bf16):
        return Shrinking(self, blocks, lane, wire)

    def total(self, value):
        for place in self.orders[0]:
            value = value + self.swap(value, 1 << place)
        return value


class Whole:
    def __init__(self, value):
        self.held = self.before = self.leaving = value

    def wait(self, *earlier):
        pass

    def launch(self):
        pass

    def merge(self, *earlier):
        pass

    def full(self):
        return self.held

    def mine(self):
        return self.held


class PlainLinks(Links):
    def growing(self, shard, lane=0):
        return Whole(lax.all_gather(shard, AXES, axis=0))

    def shrinking(self, blocks, lane=0, wire=bf16):
        return Whole(lax.psum_scatter(blocks, AXES, scatter_dimension=0, tiled=False))

    def total(self, value):
        return lax.psum(value, AXES)


def make_links(mesh):
    dp, fsdp = mesh.shape["dp"], mesh.shape["fsdp"]
    paired = (dp & (dp - 1)) == 0 and (fsdp & (fsdp - 1)) == 0 and dp * fsdp <= 64
    return (Links if paired else PlainLinks)(dp, fsdp)


def tables(lengths, row_len):
    ends = jnp.cumsum(lengths)
    starts = ends - lengths
    places = jnp.arange(row_len, dtype=jnp.int32)
    segment = jnp.sum((places[:, None] >= ends[None, :]).astype(jnp.int32), axis=1)
    rows = segment.reshape(row_len // q_rows, q_rows)
    ids = jnp.arange(lengths.shape[0])
    low = jnp.sum(jnp.where(rows[:, :1] == ids[None, :], starts[None, :], 0), axis=1)
    high = jnp.sum(jnp.where(rows[:, -1:] == ids[None, :], ends[None, :], 0), axis=1)
    bounds = jnp.stack([low // k_rows, (high + k_rows - 1) // k_rows]).astype(jnp.int32)
    return segment, jnp.concatenate([rows, rows], axis=1), segment[:, None], bounds


def body(
    links,
    doc_hidden,
    query_hidden,
    w_query,
    w_key,
    w_value,
    w_out,
    w_up,
    w_down,
    w_proj,
    biases,
    gains,
    up_bias,
    seg_lengths,
    positives,
):
    count = links.count
    row_len = doc_hidden.shape[1]
    model_width = doc_hidden.shape[2]
    query_count = query_hidden.shape[0]
    span = query_hidden.shape[1]
    doc_slots = seg_lengths.shape[1] - 1
    proj_width = w_proj.shape[1]
    ff = up_bias.shape[0] * count
    shard_cols = biases.shape[1]
    shard_rows = w_query.shape[0]
    part = model_width // 2
    small = jnp.concatenate(
        [biases.reshape(-1), gains.reshape(-1), up_bias.reshape(-1)], axis=0
    )[None]

    def rows_of(full):
        return full.reshape(full.shape[0] * full.shape[1], full.shape[2])

    sides = []
    for side in range(2):
        cut = slice(side * part, (side + 1) * part)
        shard = jnp.concatenate([w_query[:, cut], w_key[:, cut], w_value[:, cut]], axis=1)
        sides.append(links.growing(shard, side))
    small_part = links.growing(small, 0)
    out_part = links.growing(jnp.concatenate([w_out, w_proj], axis=1), 0)
    up_part = links.growing(w_up, 0)
    down_part = links.growing(w_down, 1)
    rest = (out_part, up_part, down_part)
    for hop in range(5):
        for one in sides:
            one.launch()
        if hop > 0:
            small_part.wait(sides[0].before, sides[1].before)
        small_part.launch()
        for one in sides:
            one.merge()
        first = (sides[0].held, sides[1].held)
        small_part.merge(*first)
        if hop > 0 and hop < 4:
            for one in rest:
                one.merge(*first)
        if hop < 4:
            for one in rest:
                one.wait(*first)
                one.launch()
    small_full = small_part.full().reshape(count, -1)
    full_qkv = [rows_of(one.full()) for one in sides]
    full_biases = (
        small_full[:, : 6 * shard_cols]
        .reshape(count, 6, shard_cols)
        .transpose(1, 0, 2)
        .reshape(6, model_width)
        .astype(f32)
    )
    full_gains = (
        small_full[:, 6 * shard_cols : 8 * shard_cols]
        .reshape(count, 2, shard_cols)
        .transpose(1, 0, 2)
        .reshape(2, model_width)
        .astype(f32)
    )
    full_upbias = small_full[:, 8 * shard_cols :].reshape(ff).astype(f32)

    tokens = jnp.concatenate(
        [doc_hidden[0], query_hidden.reshape(query_count * span, model_width)], axis=0
    )
    segment, segrow, segcol, bounds = tables(seg_lengths[0], row_len)
    slot_ids = jnp.arange(doc_slots, dtype=jnp.int32)
    member = (segment[:, None] == slot_ids[None, :]).astype(f32)
    member_t = (slot_ids[:, None] == segment[None, :]).astype(f32)
    zero_row = jnp.zeros((part,), f32)
    qkv, contexts, saved = [], [], []
    for side in range(2):
        cut = slice(side * part, (side + 1) * part)
        bias = jnp.concatenate([full_biases[0, cut], zero_row, full_biases[1, cut]])
        qkv.append((matmul_plain(tokens, full_qkv[side]) + bias).astype(bf16))
        context, lse, query_lse = attention_forward(
            qkv[side], segrow, segcol, bounds, row_len, span
        )
        if side == 0:
            out_part.merge(context)
            out_part.launch()
        contexts.append(context)
        saved.append((lse, query_lse))
    for one in (up_part, down_part):
        one.merge(*contexts)
        one.launch()
    contexts[1] = after(contexts[1], up_part.before, down_part.before)
    out_part.merge()
    out_proj = rows_of(out_part.full())
    full_out, full_proj = out_proj[:, :model_width], out_proj[:, model_width:]
    up_part.merge()
    down_part.merge()
    full_up = rows_of(up_part.full())
    full_down = rows_of(down_part.full())
    attn_out = (
        matmul_plain(contexts[0], full_out[:part])
        + matmul_plain(contexts[1], full_out[part:])
        + full_biases[2]
    )
    first_out, first_normed, first_scale = layer_norm_parts(
        tokens.astype(f32) + attn_out, full_gains[0], full_biases[3]
    )
    first_low = first_out.astype(bf16)
    up_pre = matmul_plain(first_low, full_up) + full_upbias
    share = 0.5 * (1.0 + lax.erf(up_pre * root_half))
    gelu_out = (up_pre * share).astype(bf16)
    density = jnp.exp(-0.5 * up_pre * up_pre) * density_peak
    slope = (share + up_pre * density).astype(bf16)
    gelu_out, slope = lax.optimization_barrier((gelu_out, slope))
    ffn_out = matmul_plain(gelu_out, full_down) + full_biases[4]
    second_out, second_normed, second_scale = layer_norm_parts(
        first_out + ffn_out, full_gains[1], full_biases[5]
    )
    second_low = second_out.astype(bf16)
    vectors = matmul_plain(second_low, full_proj).astype(bf16)
    doc_vectors = vectors[:row_len]
    query_vectors = vectors[row_len:].reshape(query_count * span, proj_width)
    every_query = links.growing(query_vectors).full().reshape(count * query_count * span, proj_width)
    query_total = count * query_count
    levels = (proj_width, proj_width * 3 // 4, proj_width // 2)
    logits, doc_sums = interaction_logits(levels, span, doc_vectors, member.astype(bf16), every_query)
    logits = logits.transpose(1, 0, 2)
    powers = jnp.exp(logits)
    local_sum = jnp.sum(powers, axis=-1)
    my_row = lax.axis_index(AXES)
    chosen = ((positives - my_row * doc_slots)[:, None] == slot_ids[None, :]).astype(f32)
    local_pick = jnp.sum(logits * chosen[:, None, :], axis=-1)
    both = links.total(jnp.concatenate([local_sum, local_pick], axis=1))
    all_sums, picked = both[:, :3], both[:, 3:]
    loss = jnp.sum(jnp.log(all_sums) - picked) / query_total
    score_derivative = (powers / all_sums[:, :, None] - chosen[:, None, :]) / query_total
    peak_match_derivative = score_derivative / (span * sharpness_divisor)

    query_terms, doc_vec_grad = interaction_grads(
        levels, span, doc_vectors, member_t.astype(bf16), every_query, doc_sums,
        peak_match_derivative.transpose(1, 0, 2),
    )
    query_terms = query_terms.reshape(count, query_count * span, proj_width)
    query_vec_grad = links.shrinking(query_terms, wire=f32).mine()
    grad_vectors = jnp.concatenate([doc_vec_grad, query_vec_grad], axis=0).astype(bf16)

    def spread_rows_of(full):
        return full.reshape(count, full.shape[0] // count, full.shape[1])

    proj_grad = matmul_left_t(second_low, grad_vectors)
    grad_second = matmul_right_t(grad_vectors, full_proj)
    grad_mid, gain_two, bias_two = layer_norm_back(
        grad_second, second_normed, second_scale, full_gains[1]
    )
    grad_ffn = grad_mid.astype(bf16)
    down_grad = matmul_left_t(gelu_out, grad_ffn)
    down_sum = links.shrinking(spread_rows_of(down_grad), 1)
    down_sum.launch()
    down_bias = jnp.sum(grad_ffn, axis=0, dtype=f32)
    grad_gelu = matmul_right_t(after(grad_ffn, down_sum.leaving), full_down)
    grad_up = (grad_gelu * slope.astype(f32)).astype(bf16)
    upbias_grad = jnp.sum(grad_up, axis=0, dtype=f32)
    up_grad = matmul_left_t(first_low, grad_up)
    up_sum = links.shrinking(spread_rows_of(up_grad), 0)
    up_sum.launch()
    down_sum.merge(up_sum.leaving)
    down_sum.launch()
    grad_first = grad_mid + matmul_right_t(after(grad_up, down_sum.leaving), full_up)
    grad_res, gain_one, bias_one = layer_norm_back(
        grad_first, first_normed, first_scale, full_gains[0]
    )
    up_sum.merge(grad_res)
    up_sum.launch()
    grad_attn = after(grad_res.astype(bf16), up_sum.leaving)
    out_bias = jnp.sum(grad_attn, axis=0, dtype=f32)
    out_grad = jnp.concatenate([matmul_left_t(c, grad_attn) for c in contexts], axis=0)
    out_sum = links.shrinking(spread_rows_of(jnp.concatenate([out_grad, proj_grad], axis=1)), 0)
    out_sum.launch()
    input_grad = grad_res
    query_bias, value_bias, qkv_sums = [], [], []
    grad_contexts = [
        matmul_right_t(grad_attn, full_out[side * part : (side + 1) * part]).astype(bf16)
        for side in range(2)
    ]
    down_sum.merge(*grad_contexts)
    down_sum.launch()
    earlier = (out_sum.leaving, down_sum.leaving)
    for side in range(2):
        grad_qkv = attention_backward(
            qkv[side], after(grad_contexts[side], *earlier), contexts[side], *saved[side], segrow,
            segcol, bounds, row_len, span,
        )
        if side == 1:
            up_sum.merge(grad_qkv)
            up_sum.launch()
            down_sum.merge(grad_qkv)
            down_sum.launch()
            qkv_sums[0].merge(grad_qkv)
            qkv_sums[0].launch()
            grad_qkv = after(grad_qkv, up_sum.leaving, down_sum.leaving, qkv_sums[0].leaving)
        query_bias.append(jnp.sum(grad_qkv[:, :part], axis=0, dtype=f32))
        value_bias.append(jnp.sum(grad_qkv[:, 2 * part :], axis=0, dtype=f32))
        qkv_grad = matmul_left_t(tokens, grad_qkv)
        if side == 0:
            qkv_sums.append(links.shrinking(spread_rows_of(qkv_grad), side))
        else:
            wide = qkv_grad.shape[1] // 2
            for lane in range(2):
                piece = qkv_grad[:, lane * wide : (lane + 1) * wide]
                qkv_sums.append(links.shrinking(spread_rows_of(piece), lane))
        for one in qkv_sums[side:]:
            one.launch()
        if side == 0:
            out_sum.merge(qkv_sums[0].leaving)
            out_sum.launch()
            up_sum.merge(qkv_sums[0].leaving)
            up_sum.launch()
            earlier = (qkv_sums[0].leaving, out_sum.leaving, up_sum.leaving)
        grad_qkv = after(grad_qkv, *[one.leaving for one in qkv_sums[side:]])
        input_grad = input_grad + matmul_right_t(grad_qkv, full_qkv[side])
    bias_grads = jnp.stack(
        [
            jnp.concatenate(query_bias),
            jnp.concatenate(value_bias),
            out_bias,
            bias_one,
            down_bias,
            bias_two,
            gain_one,
            gain_two,
        ],
        axis=0,
    )
    small_grads = jnp.concatenate(
        [
            bias_grads.reshape(8, count, shard_cols).transpose(1, 0, 2).reshape(count, -1),
            upbias_grad.reshape(count, -1),
        ],
        axis=1,
    )
    small_sum = links.shrinking(small_grads[:, None, :], 0, wire=f32)
    small_sum.launch()
    first, others = qkv_sums[1:], [small_sum, qkv_sums[0], out_sum, up_sum, down_sum]
    last = [one.leaving for one in first]
    for hop in range(links.bits):
        for one in first:
            one.merge()
        for one in others:
            one.merge(*last)
        for one in first + others:
            one.launch()
        last = [one.leaving for one in first]
    down_shard, up_shard, out_proj_shard = down_sum.mine(), up_sum.mine(), out_sum.mine()
    qkv_shards = [one.mine() for one in qkv_sums]
    qkv_shards = [qkv_shards[0], jnp.concatenate(qkv_shards[1:], axis=-1)]
    small_shard = small_sum.mine()[0]
    shards = [
        jnp.concatenate([s[:, i * part : (i + 1) * part] for s in qkv_shards], axis=1)
        for i in range(3)
    ]
    return (
        loss,
        input_grad[:row_len].reshape(1, row_len, model_width),
        input_grad[row_len:].reshape(query_count, span, model_width),
        shards[0],
        shards[1],
        shards[2],
        out_proj_shard[:, :model_width],
        up_shard,
        down_shard,
        out_proj_shard[:, model_width:],
        small_shard[: 6 * shard_cols].reshape(6, shard_cols),
        small_shard[6 * shard_cols : 8 * shard_cols].reshape(2, shard_cols),
        small_shard[8 * shard_cols :],
    )


def solution(mesh):
    return jax.shard_map(
        partial(body, make_links(mesh)),
        mesh=mesh,
        in_specs=(
            P(("dp", "fsdp"), None, None),
            P(("dp", "fsdp"), None, None),
            P(("dp", "fsdp"), None),
            P(("dp", "fsdp"), None),
            P(("dp", "fsdp"), None),
            P(("dp", "fsdp"), None),
            P(("dp", "fsdp"), None),
            P(("dp", "fsdp"), None),
            P(("dp", "fsdp"), None),
            P(None, ("dp", "fsdp")),
            P(None, ("dp", "fsdp")),
            P(("dp", "fsdp")),
            P(("dp", "fsdp"), None),
            P(),
        ),
        out_specs=(
            P(),
            P(("dp", "fsdp"), None, None),
            P(("dp", "fsdp"), None, None),
            P(("dp", "fsdp"), None),
            P(("dp", "fsdp"), None),
            P(("dp", "fsdp"), None),
            P(("dp", "fsdp"), None),
            P(("dp", "fsdp"), None),
            P(("dp", "fsdp"), None),
            P(("dp", "fsdp"), None),
            P(None, ("dp", "fsdp")),
            P(None, ("dp", "fsdp")),
            P(("dp", "fsdp")),
        ),
        check_vma=False,
    )
```

```python
from functools import partial

import jax
import jax.numpy as jnp
from jax import lax
from jax.experimental import pallas as pl
from jax.experimental.pallas import tpu as pltpu
from jax.sharding import PartitionSpec as P

softness = 0.1
sharpness_divisor = 0.2
norm_eps = 1e-05
unit_eps = 1e-06
root_half = 0.7071067811865476
density_peak = 0.3989422804014327
head_width = 64
block_queries = 8
masked_score = -1e30
rate = 0.125 * 1.4426950408889634
q_rows = 256
k_rows = 256
f32 = jnp.float32
bf16 = jnp.bfloat16
AXES = ("dp", "fsdp")

def matmul_plain(left, right):
    return jnp.dot(left, right, preferred_element_type=jnp.float32)


def matmul_right_t(left, right):
    return lax.dot_general(
        left, right, (((1,), (1,)), ((), ())), preferred_element_type=jnp.float32
    )


def matmul_left_t(left, right):
    return lax.dot_general(
        left, right, (((0,), (0,)), ((), ())), preferred_element_type=jnp.float32
    )


def layer_norm_parts(values, gain_row, bias_row):
    center = values - jnp.mean(values, axis=-1, keepdims=True)
    spread = jnp.mean(center * center, axis=-1, keepdims=True)
    inv_scale = lax.rsqrt(spread + norm_eps)
    normed = center * inv_scale
    return (normed * gain_row + bias_row, normed, inv_scale)


def layer_norm_back(grad_out, normed, inv_scale, gain_row):
    grad_norm = grad_out * gain_row
    mean_grad = jnp.mean(grad_norm, axis=-1, keepdims=True)
    mean_proj = jnp.mean(grad_norm * normed, axis=-1, keepdims=True)
    grad_in = inv_scale * (grad_norm - mean_grad - normed * mean_proj)
    return (grad_in, jnp.sum(grad_out * normed, axis=0), jnp.sum(grad_out, axis=0))


def dot_nt(a,b): return lax.dot_general(a,b,(((1,),(1,)),((),())),preferred_element_type=f32)
def dot_nn(a,b): return jnp.dot(a,b,preferred_element_type=f32)

def stack_heads(block, first):
    zero=jnp.zeros_like(block)
    return jnp.concatenate([jnp.where(first,block,zero),jnp.where(first,zero,block)],axis=0)

def attend_forward(row_len, qb, kb, lanes, span, bounds, segrow, segcol, q_ref,k_ref,v_ref,ctx_ref,lse_ref,qlse_ref,vt_ref):
    units=lanes//128
    tokens=q_ref.shape[0]
    first_q=lax.broadcasted_iota(jnp.int32,(qb,128),1)<64
    top=lax.broadcasted_iota(jnp.int32,(128,qb),0)<64
    vt_ref[...]=v_ref[...].T
    def q_step(i,_):
        rows=pl.ds(pl.multiple_of(i*qb,qb),qb)
        own=segrow[pl.ds(i,1),:]
        stacked=[stack_heads(q_ref[rows,pl.ds(u*128,128)],first_q) for u in range(units)]
        def k_step(j,carry):
            keys=pl.ds(pl.multiple_of(j*kb,kb),kb)
            allowed=segcol[keys,:]==own
            out=[]
            for u in range(units):
                peak,total,acc=carry[u]
                s=jnp.where(allowed,dot_nt(k_ref[keys,pl.ds(u*128,128)],stacked[u]),masked_score)
                new=jnp.maximum(peak,jnp.max(s,axis=0,keepdims=True))
                p=jnp.exp2((s-new)*rate)
                fade=jnp.exp2((peak-new)*rate)
                total=total*fade+jnp.sum(p,axis=0,keepdims=True)
                acc=acc*fade+dot_nn(vt_ref[pl.ds(u*128,128),keys],p.astype(bf16))
                out.append((new,total,acc))
            return tuple(out)
        start=tuple((jnp.full((1,2*qb),masked_score,f32),jnp.zeros((1,2*qb),f32),jnp.zeros((128,2*qb),f32)) for u in range(units))
        res=lax.fori_loop(bounds[0,i],bounds[1,i],k_step,start)
        for u in range(units):
            peak,total,acc=res[u]
            acc=acc/total
            o=jnp.where(top,acc[:,:qb],acc[:,qb:])
            ctx_ref[rows,pl.ds(u*128,128)]=o.T.astype(bf16)
            lse_ref[u,pl.ds(i,1),:]=peak*rate+jnp.log2(total)
        return 0
    lax.fori_loop(0,row_len//qb,q_step,0)
    nq=tokens-row_len
    firstn=lax.broadcasted_iota(jnp.int32,(nq,128),1)<64
    own=lax.broadcasted_iota(jnp.int32,(nq,2*nq),0)//span
    other=(lax.broadcasted_iota(jnp.int32,(nq,2*nq),1)%nq)//span
    keep=own==other
    for u in range(units):
        cols=pl.ds(u*128,128)
        st=stack_heads(q_ref[row_len:,cols],firstn)
        s=jnp.where(keep,dot_nt(k_ref[row_len:,cols],st),masked_score)
        peak=jnp.max(s,axis=0,keepdims=True)
        p=jnp.exp2((s-peak)*rate)
        total=jnp.sum(p,axis=0,keepdims=True)
        p=(p/total).astype(bf16)
        acc=lax.dot_general(p,v_ref[row_len:,cols],(((0,),(0,)),((),())),preferred_element_type=f32)
        ctx_ref[row_len:,cols]=jnp.where(firstn,acc[:nq],acc[nq:]).astype(bf16)
        qlse_ref[u,:,:]=peak*rate+jnp.log2(total)

def attention_forward(qkv,segrow,segcol,bounds,row_len,span):
    tokens=qkv.shape[0]
    width=qkv.shape[1]//3
    qb,kb,lanes=q_rows,k_rows,width
    nq=tokens-row_len
    steps=width//lanes
    def spec(off): return pl.BlockSpec((tokens,lanes),lambda p,*_:(0,p+off))
    full=lambda a: pl.BlockSpec(a.shape,lambda p,*_:(0,)*a.ndim)
    return pl.pallas_call(
        partial(attend_forward,row_len,qb,kb,lanes,span),
        out_shape=(jax.ShapeDtypeStruct((tokens,width),bf16),jax.ShapeDtypeStruct((width//128,row_len//qb,2*qb),f32),jax.ShapeDtypeStruct((width//128,1,2*nq),f32)),
        grid_spec=pltpu.PrefetchScalarGridSpec(num_scalar_prefetch=1,grid=(steps,),
            in_specs=[full(segrow),full(segcol),spec(0),spec(steps),spec(2*steps)],
            out_specs=[pl.BlockSpec((tokens,lanes),lambda p,*_:(0,p)),pl.BlockSpec((lanes//128,row_len//qb,2*qb),lambda p,*_:(p,0,0)),pl.BlockSpec((lanes//128,1,2*nq),lambda p,*_:(p,0,0))],
            scratch_shapes=[pltpu.VMEM((lanes,tokens),bf16)]),
        compiler_params=pltpu.CompilerParams(vmem_limit_bytes=48<<20),
    )(bounds,segrow,segcol,qkv,qkv,qkv)

def attend_backward(row_len, qb, kb, lanes, span, bounds, segrow, segcol, q_ref,k_ref,v_ref,g_ref,o_ref,lse_ref,qlse_ref,out_ref,kt_ref,dka,dva):
    dq_ref=out_ref.at[:,:lanes]; dk_ref=out_ref.at[:,lanes:2*lanes]; dv_ref=out_ref.at[:,2*lanes:]
    units=lanes//128
    tokens=q_ref.shape[0]
    first_q=lax.broadcasted_iota(jnp.int32,(qb,128),1)<64
    top=lax.broadcasted_iota(jnp.int32,(128,qb),0)<64
    kt_ref[...]=k_ref[...].T
    dka[...]=jnp.zeros_like(dka); dva[...]=jnp.zeros_like(dva)
    def q_step(i,_):
        rows=pl.ds(pl.multiple_of(i*qb,qb),qb)
        own=segrow[pl.ds(i,1),:]
        sq=[];sg=[];dr=[];ls=[]
        for u in range(units):
            cols=pl.ds(u*128,128)
            g=g_ref[rows,cols]
            sq.append(stack_heads(q_ref[rows,cols],first_q)); sg.append(stack_heads(g,first_q))
            t=(g.astype(f32)*o_ref[rows,cols].astype(f32)).T
            dr.append(jnp.concatenate([jnp.sum(t[:64],axis=0,keepdims=True),jnp.sum(t[64:],axis=0,keepdims=True)],axis=1))
            ls.append(lse_ref[u,pl.ds(i,1),:])
        def k_step(j,carry):
            keys=pl.ds(pl.multiple_of(j*kb,kb),kb)
            allowed=segcol[keys,:]==own
            out=[]
            for u in range(units):
                cols=pl.ds(u*128,128)
                s=jnp.where(allowed,dot_nt(k_ref[keys,cols],sq[u]),masked_score)
                p=jnp.exp2(s*rate-ls[u])
                dp=dot_nt(v_ref[keys,cols],sg[u])
                ds=(p*(dp-dr[u])).astype(bf16)
                dva[keys,cols]+=dot_nn(p.astype(bf16),sg[u])
                dka[keys,cols]+=dot_nn(ds,sq[u])
                out.append(carry[u]+dot_nn(kt_ref[cols,keys],ds))
            return tuple(out)
        res=lax.fori_loop(bounds[0,i],bounds[1,i],k_step,tuple(jnp.zeros((128,2*qb),f32) for u in range(units)))
        for u in range(units):
            d=jnp.where(top,res[u][:,:qb],res[u][:,qb:])*0.125
            dq_ref[rows,pl.ds(u*128,128)]=d.T.astype(bf16)
        return 0
    lax.fori_loop(0,row_len//qb,q_step,0)
    dk_ref[:row_len,:]=(dka[...]*0.125).astype(bf16)
    dv_ref[:row_len,:]=dva[...].astype(bf16)
    nq=tokens-row_len
    firstn=lax.broadcasted_iota(jnp.int32,(nq,128),1)<64
    own=lax.broadcasted_iota(jnp.int32,(nq,2*nq),0)//span
    other=(lax.broadcasted_iota(jnp.int32,(nq,2*nq),1)%nq)//span
    keep=own==other
    for u in range(units):
        cols=pl.ds(u*128,128)
        q=q_ref[row_len:,cols]; k=k_ref[row_len:,cols]; v=v_ref[row_len:,cols]; g=g_ref[row_len:,cols]
        st=stack_heads(q,firstn); sg=stack_heads(g,firstn)
        s=jnp.where(keep,dot_nt(k,st),masked_score)
        p=jnp.exp2(s*rate-qlse_ref[u])
        dp=dot_nt(v,sg)
        ds=(p*(dp-jnp.sum(p*dp,axis=0,keepdims=True))).astype(bf16)
        dv_ref[row_len:,cols]=dot_nn(p.astype(bf16),sg).astype(bf16)
        dk_ref[row_len:,cols]=(dot_nn(ds,st)*0.125).astype(bf16)
        d=lax.dot_general(ds,k,(((0,),(0,)),((),())),preferred_element_type=f32)
        dq_ref[row_len:,cols]=(jnp.where(firstn,d[:nq],d[nq:])*0.125).astype(bf16)

def attention_backward(qkv,g,o,lse,qlse,segrow,segcol,bounds,row_len,span):
    tokens,width=g.shape
    qb,kb,lanes=q_rows,k_rows,width
    nq=tokens-row_len
    steps=width//lanes
    def spec(off): return pl.BlockSpec((tokens,lanes),lambda p,*_:(0,p+off))
    full=lambda a: pl.BlockSpec(a.shape,lambda p,*_:(0,)*a.ndim)
    sd=jax.ShapeDtypeStruct((tokens,3*width),bf16)
    return pl.pallas_call(
        partial(attend_backward,row_len,qb,kb,lanes,span),
        out_shape=sd,
        grid_spec=pltpu.PrefetchScalarGridSpec(num_scalar_prefetch=1,grid=(steps,),
            in_specs=[full(segrow),full(segcol)]+[spec(0),spec(1),spec(2),spec(0),spec(0)]+[pl.BlockSpec((lanes//128,row_len//qb,2*qb),lambda p,*_:(p,0,0)),pl.BlockSpec((lanes//128,1,2*nq),lambda p,*_:(p,0,0))],
            out_specs=pl.BlockSpec((tokens,3*lanes),lambda p,*_:(0,0)),
            scratch_shapes=[pltpu.VMEM((lanes,tokens),bf16),pltpu.VMEM((row_len,lanes),f32),pltpu.VMEM((row_len,lanes),f32)]),
        compiler_params=pltpu.CompilerParams(vmem_limit_bytes=56<<20),
    )(bounds,segrow,segcol,qkv,qkv,qkv,g,o,lse,qlse)


def level_units(values, width):
    lanes = lax.broadcasted_iota(jnp.int32, values.shape, 1)
    part_cols = jnp.where(lanes < width, values, 0.0)
    inv_scale = lax.rsqrt(jnp.sum(part_cols * part_cols, axis=-1, keepdims=True) + unit_eps)
    return part_cols * inv_scale, inv_scale


def three_parts(values):
    top = values.astype(bf16)
    rest = values - top.astype(f32)
    middle = rest.astype(bf16)
    return top, middle, (rest - middle.astype(f32)).astype(bf16)


def exact_dot(values, marks):
    return sum(dot_nn(part, marks) for part in three_parts(values))


def keep_doc_units(levels, doc_ref, low_ref):
    @pl.when(pl.program_id(0) == 0)
    def _():
        docs = doc_ref[...].astype(f32)
        for position, width in enumerate(levels):
            low_ref[position] = level_units(docs, width)[0].astype(bf16)


def interact_forward(levels, span, doc_ref, member_ref, query_ref, logit_ref, sums_ref, low_ref):
    keep_doc_units(levels, doc_ref, low_ref)
    queries = query_ref[...].astype(f32)
    member = member_ref[...]
    for position, width in enumerate(levels):
        unit_rows = level_units(queries, width)[0].astype(bf16)
        powers = jnp.exp(dot_nt(unit_rows, low_ref[position]) / softness)
        doc_sums = exact_dot(powers, member)
        sums_ref[position] = doc_sums
        logs = (softness * jnp.log(doc_sums)).reshape(-1, span, doc_sums.shape[1])
        logit_ref[position] = jnp.sum(logs, axis=1) / (span * sharpness_divisor)


def interact_backward(
    levels, span, doc_ref, member_t_ref, query_ref, sums_ref, grad_ref, query_grad_ref,
    doc_grad_ref, low_ref, held_ref,
):
    keep_doc_units(levels, doc_ref, low_ref)

    @pl.when(pl.program_id(0) == 0)
    def _():
        held_ref[...] = jnp.zeros_like(held_ref)

    queries = query_ref[...].astype(f32)
    member_t = member_t_ref[...]
    total = jnp.zeros(queries.shape, f32)
    for position, width in enumerate(levels):
        unit_full, inv_scale = level_units(queries, width)
        unit_rows = unit_full.astype(bf16)
        powers = jnp.exp(dot_nt(unit_rows, low_ref[position]) / softness)
        grads = grad_ref[position]
        rows = jnp.broadcast_to(grads[:, None, :], (grads.shape[0], span, grads.shape[1]))
        rows = rows.reshape(-1, grads.shape[1]) / sums_ref[position]
        grad_scores = (powers * exact_dot(rows, member_t)).astype(bf16)
        grad_unit = dot_nn(grad_scores, low_ref[position])
        held_ref[position] += matmul_left_t(grad_scores, unit_rows)
        total = total + inv_scale * (
            grad_unit - unit_full * jnp.sum(grad_unit * unit_full, axis=-1, keepdims=True)
        )
    query_grad_ref[...] = total

    @pl.when(pl.program_id(0) == pl.num_programs(0) - 1)
    def _():
        docs = doc_ref[...].astype(f32)
        doc_total = jnp.zeros(docs.shape, f32)
        for position, width in enumerate(levels):
            unit_full, inv_scale = level_units(docs, width)
            grad_unit = held_ref[position]
            doc_total = doc_total + inv_scale * (
                grad_unit - unit_full * jnp.sum(grad_unit * unit_full, axis=-1, keepdims=True)
            )
        doc_grad_ref[...] = doc_total


def interaction_logits(levels, span, docs, member, queries):
    tokens, width = queries.shape
    row_len, slots = member.shape
    rows = block_queries * span
    return pl.pallas_call(
        partial(interact_forward, levels, span),
        grid=(tokens // rows,),
        out_shape=(
            jax.ShapeDtypeStruct((3, tokens // span, slots), f32),
            jax.ShapeDtypeStruct((3, tokens, slots), f32),
        ),
        in_specs=[
            pl.BlockSpec((row_len, width), lambda i: (0, 0)),
            pl.BlockSpec((row_len, slots), lambda i: (0, 0)),
            pl.BlockSpec((rows, width), lambda i: (i, 0)),
        ],
        out_specs=(
            pl.BlockSpec((3, block_queries, slots), lambda i: (0, i, 0)),
            pl.BlockSpec((3, rows, slots), lambda i: (0, i, 0)),
        ),
        scratch_shapes=[pltpu.VMEM((3, row_len, width), bf16)],
        compiler_params=pltpu.CompilerParams(vmem_limit_bytes=40 << 20),
    )(docs, member, queries)


def interaction_grads(levels, span, docs, member_t, queries, sums, grads):
    tokens, width = queries.shape
    slots, row_len = member_t.shape
    rows = block_queries * span
    return pl.pallas_call(
        partial(interact_backward, levels, span),
        grid=(tokens // rows,),
        out_shape=(
            jax.ShapeDtypeStruct((tokens, width), f32),
            jax.ShapeDtypeStruct((row_len, width), f32),
        ),
        in_specs=[
            pl.BlockSpec((row_len, width), lambda i: (0, 0)),
            pl.BlockSpec((slots, row_len), lambda i: (0, 0)),
            pl.BlockSpec((rows, width), lambda i: (i, 0)),
            pl.BlockSpec((3, rows, slots), lambda i: (0, i, 0)),
            pl.BlockSpec((3, block_queries, slots), lambda i: (0, i, 0)),
        ],
        out_specs=(
            pl.BlockSpec((rows, width), lambda i: (i, 0)),
            pl.BlockSpec((row_len, width), lambda i: (0, 0)),
        ),
        scratch_shapes=[
            pltpu.VMEM((3, row_len, width), bf16),
            pltpu.VMEM((3, row_len, width), f32),
        ],
        compiler_params=pltpu.CompilerParams(vmem_limit_bytes=40 << 20),
    )(docs, member_t, queries, sums, grads)


def after(value, *earlier):
    return lax.optimization_barrier((value, *earlier))[0]


class Growing:
    def __init__(self, links, shard, lane):
        self.links, self.order, self.block = links, list(links.orders[lane]), shard.shape
        self.held = shard.reshape((1,) * links.bits + shard.shape)

    def wait(self, *earlier):
        self.held = after(self.held, *earlier)

    def launch(self):
        self.place = self.order.pop(0)
        self.before = self.held
        self.arrived = self.links.swap(self.held, 1 << self.place)

    def merge(self, *earlier):
        axis = self.links.bits - 1 - self.place
        mine = self.links.side(self.place)
        held = self.held
        arrived = after(self.arrived, *earlier) if earlier else self.arrived
        shape = held.shape[:axis] + (2,) + held.shape[axis + 1 :]
        own = lax.broadcasted_iota(jnp.int32, shape, axis) == mine
        self.held = jnp.where(own, held, arrived)

    def full(self):
        while self.order:
            self.launch()
            self.merge()
        return self.held.reshape((self.links.count,) + self.block)


class Shrinking:
    def __init__(self, links, blocks, lane, wire):
        self.links, self.order, self.block = links, list(links.orders[lane]), blocks.shape[1:]
        self.wire = wire
        self.held = blocks.astype(wire).reshape((2,) * links.bits + self.block)

    def wait(self, *earlier):
        self.held = after(self.held, *earlier)

    def launch(self):
        if not self.order:
            return
        self.place = self.order.pop()
        axis = self.links.bits - 1 - self.place
        self.leaving = lax.dynamic_slice_in_dim(
            self.held, 1 - self.links.side(self.place), 1, axis
        )
        self.arrived = self.links.swap(self.leaving, 1 << self.place)

    def merge(self, *earlier):
        if self.arrived is None:
            return
        axis = self.links.bits - 1 - self.place
        kept = lax.dynamic_slice_in_dim(self.held, self.links.side(self.place), 1, axis)
        arrived = after(self.arrived, *earlier) if earlier else self.arrived
        total = kept.astype(f32) + arrived.astype(f32)
        self.held = total.astype(self.wire) if self.order else total
        self.arrived = None

    def mine(self):
        while self.order:
            self.launch()
            self.merge()
        return self.held.reshape(self.block)


class Links:
    def __init__(self, dp, fsdp):
        self.dp, self.fsdp, self.count = dp, fsdp, dp * fsdp
        self.bits = self.count.bit_length() - 1
        inner_bits = fsdp.bit_length() - 1
        low, high = list(range(inner_bits)), list(range(inner_bits, self.bits))
        inner, rest = low[:1], low[1:]
        near, far = high[:1], high[1:][::-1]
        self.orders = (far + rest[::-1] + near + inner, far + near + rest[::-1] + inner)

    def side(self, place):
        return (lax.axis_index(AXES) >> place) & 1

    def swap(self, value, bit):
        return lax.ppermute(value, AXES, [(d, d ^ bit) for d in range(self.count)])

    def growing(self, shard, lane=0):
        return Growing(self, shard, lane)

    def shrinking(self, blocks, lane=0, wire=bf16):
        return Shrinking(self, blocks, lane, wire)

    def total(self, value):
        for place in self.orders[0]:
            value = value + self.swap(value, 1 << place)
        return value


class Whole:
    def __init__(self, value):
        self.held = self.before = self.leaving = value

    def wait(self, *earlier):
        pass

    def launch(self):
        pass

    def merge(self, *earlier):
        pass

    def full(self):
        return self.held

    def mine(self):
        return self.held


class PlainLinks(Links):
    def growing(self, shard, lane=0):
        return Whole(lax.all_gather(shard, AXES, axis=0))

    def shrinking(self, blocks, lane=0, wire=bf16):
        return Whole(lax.psum_scatter(blocks, AXES, scatter_dimension=0, tiled=False))

    def total(self, value):
        return lax.psum(value, AXES)


def make_links(mesh):
    dp, fsdp = mesh.shape["dp"], mesh.shape["fsdp"]
    paired = (dp & (dp - 1)) == 0 and (fsdp & (fsdp - 1)) == 0 and dp * fsdp <= 64
    return (Links if paired else PlainLinks)(dp, fsdp)


def tables(lengths, row_len):
    ends = jnp.cumsum(lengths)
    starts = ends - lengths
    places = jnp.arange(row_len, dtype=jnp.int32)
    segment = jnp.sum((places[:, None] >= ends[None, :]).astype(jnp.int32), axis=1)
    rows = segment.reshape(row_len // q_rows, q_rows)
    ids = jnp.arange(lengths.shape[0])
    low = jnp.sum(jnp.where(rows[:, :1] == ids[None, :], starts[None, :], 0), axis=1)
    high = jnp.sum(jnp.where(rows[:, -1:] == ids[None, :], ends[None, :], 0), axis=1)
    bounds = jnp.stack([low // k_rows, (high + k_rows - 1) // k_rows]).astype(jnp.int32)
    return segment, jnp.concatenate([rows, rows], axis=1), segment[:, None], bounds


def body(
    links,
    doc_hidden,
    query_hidden,
    w_query,
    w_key,
    w_value,
    w_out,
    w_up,
    w_down,
    w_proj,
    biases,
    gains,
    up_bias,
    seg_lengths,
    positives,
):
    count = links.count
    row_len = doc_hidden.shape[1]
    model_width = doc_hidden.shape[2]
    query_count = query_hidden.shape[0]
    span = query_hidden.shape[1]
    doc_slots = seg_lengths.shape[1] - 1
    proj_width = w_proj.shape[1]
    ff = up_bias.shape[0] * count
    shard_cols = biases.shape[1]
    shard_rows = w_query.shape[0]
    part = model_width // 2
    small = jnp.concatenate(
        [biases.reshape(-1), gains.reshape(-1), up_bias.reshape(-1)], axis=0
    )[None]

    def rows_of(full):
        return full.reshape(full.shape[0] * full.shape[1], full.shape[2])

    sides = []
    for side in range(2):
        cut = slice(side * part, (side + 1) * part)
        shard = jnp.concatenate([w_query[:, cut], w_key[:, cut], w_value[:, cut]], axis=1)
        sides.append(links.growing(shard, side))
    small_part = links.growing(small, 0)
    out_part = links.growing(jnp.concatenate([w_out, w_proj], axis=1), 0)
    up_part = links.growing(w_up, 0)
    down_part = links.growing(w_down, 1)
    rest = (out_part, up_part, down_part)
    for hop in range(5):
        for one in sides:
            one.launch()
        if hop > 0:
            small_part.wait(sides[0].before, sides[1].before)
        small_part.launch()
        for one in sides:
            one.merge()
        first = (sides[0].held, sides[1].held)
        small_part.merge(*first)
        for one in rest:
            if hop == 0:
                one.wait(*first)
                one.launch()
            if hop == 2 or hop == 3:
                one.merge(*first)
                one.launch()
    small_full = small_part.full().reshape(count, -1)
    full_qkv = [rows_of(one.full()) for one in sides]
    full_biases = (
        small_full[:, : 6 * shard_cols]
        .reshape(count, 6, shard_cols)
        .transpose(1, 0, 2)
        .reshape(6, model_width)
        .astype(f32)
    )
    full_gains = (
        small_full[:, 6 * shard_cols : 8 * shard_cols]
        .reshape(count, 2, shard_cols)
        .transpose(1, 0, 2)
        .reshape(2, model_width)
        .astype(f32)
    )
    full_upbias = small_full[:, 8 * shard_cols :].reshape(ff).astype(f32)

    tokens = jnp.concatenate(
        [doc_hidden[0], query_hidden.reshape(query_count * span, model_width)], axis=0
    )
    segment, segrow, segcol, bounds = tables(seg_lengths[0], row_len)
    slot_ids = jnp.arange(doc_slots, dtype=jnp.int32)
    member = (segment[:, None] == slot_ids[None, :]).astype(f32)
    member_t = (slot_ids[:, None] == segment[None, :]).astype(f32)
    zero_row = jnp.zeros((part,), f32)
    qkv, contexts, saved = [], [], []
    for side in range(2):
        cut = slice(side * part, (side + 1) * part)
        bias = jnp.concatenate([full_biases[0, cut], zero_row, full_biases[1, cut]])
        qkv.append((matmul_plain(tokens, full_qkv[side]) + bias).astype(bf16))
    for one in rest:
        one.merge(*qkv)
        one.launch()
    for side in range(2):
        qkv[side] = after(qkv[side], *[one.before for one in rest])
        context, lse, query_lse = attention_forward(
            qkv[side], segrow, segcol, bounds, row_len, span
        )
        if side == 0:
            out_part.merge(context)
            out_part.launch()
        contexts.append(context)
        saved.append((lse, query_lse))
    for one in (up_part, down_part):
        one.merge(*contexts)
        one.launch()
    contexts[1] = after(contexts[1], up_part.before, down_part.before)
    out_part.merge()
    out_proj = rows_of(out_part.full())
    full_out, full_proj = out_proj[:, :model_width], out_proj[:, model_width:]
    up_part.merge()
    down_part.merge()
    full_up = rows_of(up_part.full())
    full_down = rows_of(down_part.full())
    attn_out = (
        matmul_plain(contexts[0], full_out[:part])
        + matmul_plain(contexts[1], full_out[part:])
        + full_biases[2]
    )
    first_out, first_normed, first_scale = layer_norm_parts(
        tokens.astype(f32) + attn_out, full_gains[0], full_biases[3]
    )
    first_low = first_out.astype(bf16)
    up_pre = matmul_plain(first_low, full_up) + full_upbias
    share = 0.5 * (1.0 + lax.erf(up_pre * root_half))
    gelu_out = (up_pre * share).astype(bf16)
    density = jnp.exp(-0.5 * up_pre * up_pre) * density_peak
    slope = (share + up_pre * density).astype(bf16)
    gelu_out, slope = lax.optimization_barrier((gelu_out, slope))
    ffn_out = matmul_plain(gelu_out, full_down) + full_biases[4]
    second_out, second_normed, second_scale = layer_norm_parts(
        first_out + ffn_out, full_gains[1], full_biases[5]
    )
    second_low = second_out.astype(bf16)
    vectors = matmul_plain(second_low, full_proj).astype(bf16)
    doc_vectors = vectors[:row_len]
    query_vectors = vectors[row_len:].reshape(query_count * span, proj_width)
    every_query = links.growing(query_vectors).full().reshape(count * query_count * span, proj_width)
    query_total = count * query_count
    levels = (proj_width, proj_width * 3 // 4, proj_width // 2)
    logits, doc_sums = interaction_logits(levels, span, doc_vectors, member.astype(bf16), every_query)
    logits = logits.transpose(1, 0, 2)
    powers = jnp.exp(logits)
    local_sum = jnp.sum(powers, axis=-1)
    my_row = lax.axis_index(AXES)
    chosen = ((positives - my_row * doc_slots)[:, None] == slot_ids[None, :]).astype(f32)
    local_pick = jnp.sum(logits * chosen[:, None, :], axis=-1)
    both = links.total(jnp.concatenate([local_sum, local_pick], axis=1))
    all_sums, picked = both[:, :3], both[:, 3:]
    loss = jnp.sum(jnp.log(all_sums) - picked) / query_total
    score_derivative = (powers / all_sums[:, :, None] - chosen[:, None, :]) / query_total
    peak_match_derivative = score_derivative / (span * sharpness_divisor)

    query_terms, doc_vec_grad = interaction_grads(
        levels, span, doc_vectors, member_t.astype(bf16), every_query, doc_sums,
        peak_match_derivative.transpose(1, 0, 2),
    )
    query_terms = query_terms.reshape(count, query_count * span, proj_width)
    query_vec_grad = links.shrinking(query_terms, wire=f32).mine()
    grad_vectors = jnp.concatenate([doc_vec_grad, query_vec_grad], axis=0).astype(bf16)

    def spread_rows_of(full):
        return full.reshape(count, full.shape[0] // count, full.shape[1])

    proj_grad = matmul_left_t(second_low, grad_vectors)
    grad_second = matmul_right_t(grad_vectors, full_proj)
    grad_mid, gain_two, bias_two = layer_norm_back(
        grad_second, second_normed, second_scale, full_gains[1]
    )
    grad_ffn = grad_mid.astype(bf16)
    down_grad = matmul_left_t(gelu_out, grad_ffn)
    down_sum = links.shrinking(spread_rows_of(down_grad), 1)
    down_sum.launch()
    down_bias = jnp.sum(grad_ffn, axis=0, dtype=f32)
    grad_gelu = matmul_right_t(after(grad_ffn, down_sum.leaving), full_down)
    grad_up = (grad_gelu * slope.astype(f32)).astype(bf16)
    upbias_grad = jnp.sum(grad_up, axis=0, dtype=f32)
    up_grad = matmul_left_t(first_low, grad_up)
    up_sum = links.shrinking(spread_rows_of(up_grad), 0)
    up_sum.launch()
    down_sum.merge(up_sum.leaving)
    down_sum.launch()
    grad_first = grad_mid + matmul_right_t(after(grad_up, down_sum.leaving), full_up)
    grad_res, gain_one, bias_one = layer_norm_back(
        grad_first, first_normed, first_scale, full_gains[0]
    )
    up_sum.merge(grad_res)
    up_sum.launch()
    grad_attn = after(grad_res.astype(bf16), up_sum.leaving)
    out_bias = jnp.sum(grad_attn, axis=0, dtype=f32)
    out_grad = jnp.concatenate([matmul_left_t(c, grad_attn) for c in contexts], axis=0)
    out_sum = links.shrinking(spread_rows_of(jnp.concatenate([out_grad, proj_grad], axis=1)), 0)
    out_sum.launch()
    input_grad = grad_res
    query_bias, value_bias, qkv_sums = [], [], []
    grad_contexts = [
        matmul_right_t(grad_attn, full_out[side * part : (side + 1) * part]).astype(bf16)
        for side in range(2)
    ]
    down_sum.merge(*grad_contexts)
    down_sum.launch()
    earlier = (out_sum.leaving, down_sum.leaving)
    for side in range(2):
        grad_qkv = attention_backward(
            qkv[side], after(grad_contexts[side], *earlier), contexts[side], *saved[side], segrow,
            segcol, bounds, row_len, span,
        )
        if side == 1:
            up_sum.merge(grad_qkv)
            up_sum.launch()
            down_sum.merge(grad_qkv)
            down_sum.launch()
            qkv_sums[0].merge(grad_qkv)
            qkv_sums[0].launch()
            grad_qkv = after(grad_qkv, up_sum.leaving, down_sum.leaving, qkv_sums[0].leaving)
        query_bias.append(jnp.sum(grad_qkv[:, :part], axis=0, dtype=f32))
        value_bias.append(jnp.sum(grad_qkv[:, 2 * part :], axis=0, dtype=f32))
        qkv_grad = matmul_left_t(tokens, grad_qkv)
        if side == 0:
            qkv_sums.append(links.shrinking(spread_rows_of(qkv_grad), side))
        else:
            wide = qkv_grad.shape[1] // 2
            for lane in range(2):
                piece = qkv_grad[:, lane * wide : (lane + 1) * wide]
                qkv_sums.append(links.shrinking(spread_rows_of(piece), lane))
        for one in qkv_sums[side:]:
            one.launch()
        if side == 0:
            out_sum.merge(qkv_sums[0].leaving)
            out_sum.launch()
            up_sum.merge(qkv_sums[0].leaving)
            up_sum.launch()
            earlier = (qkv_sums[0].leaving, out_sum.leaving, up_sum.leaving)
        grad_qkv = after(grad_qkv, *[one.leaving for one in qkv_sums[side:]])
        input_grad = input_grad + matmul_right_t(grad_qkv, full_qkv[side])
    bias_grads = jnp.stack(
        [
            jnp.concatenate(query_bias),
            jnp.concatenate(value_bias),
            out_bias,
            bias_one,
            down_bias,
            bias_two,
            gain_one,
            gain_two,
        ],
        axis=0,
    )
    small_grads = jnp.concatenate(
        [
            bias_grads.reshape(8, count, shard_cols).transpose(1, 0, 2).reshape(count, -1),
            upbias_grad.reshape(count, -1),
        ],
        axis=1,
    )
    small_sum = links.shrinking(small_grads[:, None, :], 0, wire=f32)
    small_sum.launch()
    first, others, slow = qkv_sums[1:], [small_sum, qkv_sums[0], out_sum], [up_sum, down_sum]
    last = [one.leaving for one in first]
    for hop in range(links.bits):
        for one in first:
            one.merge()
        for one in others:
            one.merge(*last)
        for one in first + others:
            one.launch()
        last = [one.held for one in first]
        if hop == 0 or hop == 3:
            for one in slow:
                one.merge(*last)
                one.launch()
        last = [one.leaving for one in first]
    down_shard, up_shard, out_proj_shard = down_sum.mine(), up_sum.mine(), out_sum.mine()
    qkv_shards = [one.mine() for one in qkv_sums]
    qkv_shards = [qkv_shards[0], jnp.concatenate(qkv_shards[1:], axis=-1)]
    small_shard = small_sum.mine()[0]
    shards = [
        jnp.concatenate([s[:, i * part : (i + 1) * part] for s in qkv_shards], axis=1)
        for i in range(3)
    ]
    return (
        loss,
        input_grad[:row_len].reshape(1, row_len, model_width),
        input_grad[row_len:].reshape(query_count, span, model_width),
        shards[0],
        shards[1],
        shards[2],
        out_proj_shard[:, :model_width],
        up_shard,
        down_shard,
        out_proj_shard[:, model_width:],
        small_shard[: 6 * shard_cols].reshape(6, shard_cols),
        small_shard[6 * shard_cols : 8 * shard_cols].reshape(2, shard_cols),
        small_shard[8 * shard_cols :],
    )


def solution(mesh):
    return jax.shard_map(
        partial(body, make_links(mesh)),
        mesh=mesh,
        in_specs=(
            P(("dp", "fsdp"), None, None),
            P(("dp", "fsdp"), None, None),
            P(("dp", "fsdp"), None),
            P(("dp", "fsdp"), None),
            P(("dp", "fsdp"), None),
            P(("dp", "fsdp"), None),
            P(("dp", "fsdp"), None),
            P(("dp", "fsdp"), None),
            P(("dp", "fsdp"), None),
            P(None, ("dp", "fsdp")),
            P(None, ("dp", "fsdp")),
            P(("dp", "fsdp")),
            P(("dp", "fsdp"), None),
            P(),
        ),
        out_specs=(
            P(),
            P(("dp", "fsdp"), None, None),
            P(("dp", "fsdp"), None, None),
            P(("dp", "fsdp"), None),
            P(("dp", "fsdp"), None),
            P(("dp", "fsdp"), None),
            P(("dp", "fsdp"), None),
            P(("dp", "fsdp"), None),
            P(("dp", "fsdp"), None),
            P(("dp", "fsdp"), None),
            P(None, ("dp", "fsdp")),
            P(None, ("dp", "fsdp")),
            P(("dp", "fsdp")),
        ),
        check_vma=False,
    )
```

```python
from functools import partial

import jax
import jax.numpy as jnp
from jax import lax
from jax.experimental import pallas as pl
from jax.experimental.pallas import tpu as pltpu
from jax.sharding import PartitionSpec as P

softness = 0.1
sharpness_divisor = 0.2
norm_eps = 1e-05
unit_eps = 1e-06
root_half = 0.7071067811865476
density_peak = 0.3989422804014327
head_width = 64
block_queries = 8
masked_score = -1e30
rate = 0.125 * 1.4426950408889634
q_rows = 256
k_rows = 256
f32 = jnp.float32
bf16 = jnp.bfloat16
AXES = ("dp", "fsdp")

def matmul_plain(left, right):
    return jnp.dot(left, right, preferred_element_type=jnp.float32)


def matmul_right_t(left, right):
    return lax.dot_general(
        left, right, (((1,), (1,)), ((), ())), preferred_element_type=jnp.float32
    )


def matmul_left_t(left, right):
    return lax.dot_general(
        left, right, (((0,), (0,)), ((), ())), preferred_element_type=jnp.float32
    )


def layer_norm_parts(values, gain_row, bias_row):
    center = values - jnp.mean(values, axis=-1, keepdims=True)
    spread = jnp.mean(center * center, axis=-1, keepdims=True)
    inv_scale = lax.rsqrt(spread + norm_eps)
    normed = center * inv_scale
    return (normed * gain_row + bias_row, normed, inv_scale)


def layer_norm_back(grad_out, normed, inv_scale, gain_row):
    grad_norm = grad_out * gain_row
    mean_grad = jnp.mean(grad_norm, axis=-1, keepdims=True)
    mean_proj = jnp.mean(grad_norm * normed, axis=-1, keepdims=True)
    grad_in = inv_scale * (grad_norm - mean_grad - normed * mean_proj)
    return (grad_in, jnp.sum(grad_out * normed, axis=0), jnp.sum(grad_out, axis=0))


def dot_nt(a,b): return lax.dot_general(a,b,(((1,),(1,)),((),())),preferred_element_type=f32)
def dot_nn(a,b): return jnp.dot(a,b,preferred_element_type=f32)

def stack_heads(block, first):
    zero=jnp.zeros_like(block)
    return jnp.concatenate([jnp.where(first,block,zero),jnp.where(first,zero,block)],axis=0)

def attend_forward(row_len, qb, kb, lanes, span, bounds, segrow, segcol, q_ref,k_ref,v_ref,ctx_ref,lse_ref,qlse_ref,vt_ref):
    units=lanes//128
    tokens=q_ref.shape[0]
    first_q=lax.broadcasted_iota(jnp.int32,(qb,128),1)<64
    top=lax.broadcasted_iota(jnp.int32,(128,qb),0)<64
    vt_ref[...]=v_ref[...].T
    def q_step(i,_):
        rows=pl.ds(pl.multiple_of(i*qb,qb),qb)
        own=segrow[pl.ds(i,1),:]
        stacked=[stack_heads(q_ref[rows,pl.ds(u*128,128)],first_q) for u in range(units)]
        def k_step(j,carry):
            keys=pl.ds(pl.multiple_of(j*kb,kb),kb)
            allowed=segcol[keys,:]==own
            out=[]
            for u in range(units):
                peak,total,acc=carry[u]
                s=jnp.where(allowed,dot_nt(k_ref[keys,pl.ds(u*128,128)],stacked[u]),masked_score)
                new=jnp.maximum(peak,jnp.max(s,axis=0,keepdims=True))
                p=jnp.exp2((s-new)*rate)
                fade=jnp.exp2((peak-new)*rate)
                total=total*fade+jnp.sum(p,axis=0,keepdims=True)
                acc=acc*fade+dot_nn(vt_ref[pl.ds(u*128,128),keys],p.astype(bf16))
                out.append((new,total,acc))
            return tuple(out)
        start=tuple((jnp.full((1,2*qb),masked_score,f32),jnp.zeros((1,2*qb),f32),jnp.zeros((128,2*qb),f32)) for u in range(units))
        res=lax.fori_loop(bounds[0,i],bounds[1,i],k_step,start)
        for u in range(units):
            peak,total,acc=res[u]
            acc=acc/total
            o=jnp.where(top,acc[:,:qb],acc[:,qb:])
            ctx_ref[rows,pl.ds(u*128,128)]=o.T.astype(bf16)
            lse_ref[u,pl.ds(i,1),:]=peak*rate+jnp.log2(total)
        return 0
    lax.fori_loop(0,row_len//qb,q_step,0)
    nq=tokens-row_len
    firstn=lax.broadcasted_iota(jnp.int32,(nq,128),1)<64
    own=lax.broadcasted_iota(jnp.int32,(nq,2*nq),0)//span
    other=(lax.broadcasted_iota(jnp.int32,(nq,2*nq),1)%nq)//span
    keep=own==other
    for u in range(units):
        cols=pl.ds(u*128,128)
        st=stack_heads(q_ref[row_len:,cols],firstn)
        s=jnp.where(keep,dot_nt(k_ref[row_len:,cols],st),masked_score)
        peak=jnp.max(s,axis=0,keepdims=True)
        p=jnp.exp2((s-peak)*rate)
        total=jnp.sum(p,axis=0,keepdims=True)
        p=(p/total).astype(bf16)
        acc=lax.dot_general(p,v_ref[row_len:,cols],(((0,),(0,)),((),())),preferred_element_type=f32)
        ctx_ref[row_len:,cols]=jnp.where(firstn,acc[:nq],acc[nq:]).astype(bf16)
        qlse_ref[u,:,:]=peak*rate+jnp.log2(total)

def attention_forward(qkv,segrow,segcol,bounds,row_len,span):
    tokens=qkv.shape[0]
    width=qkv.shape[1]//3
    qb,kb,lanes=q_rows,k_rows,width
    nq=tokens-row_len
    steps=width//lanes
    def spec(off): return pl.BlockSpec((tokens,lanes),lambda p,*_:(0,p+off))
    full=lambda a: pl.BlockSpec(a.shape,lambda p,*_:(0,)*a.ndim)
    return pl.pallas_call(
        partial(attend_forward,row_len,qb,kb,lanes,span),
        out_shape=(jax.ShapeDtypeStruct((tokens,width),bf16),jax.ShapeDtypeStruct((width//128,row_len//qb,2*qb),f32),jax.ShapeDtypeStruct((width//128,1,2*nq),f32)),
        grid_spec=pltpu.PrefetchScalarGridSpec(num_scalar_prefetch=1,grid=(steps,),
            in_specs=[full(segrow),full(segcol),spec(0),spec(steps),spec(2*steps)],
            out_specs=[pl.BlockSpec((tokens,lanes),lambda p,*_:(0,p)),pl.BlockSpec((lanes//128,row_len//qb,2*qb),lambda p,*_:(p,0,0)),pl.BlockSpec((lanes//128,1,2*nq),lambda p,*_:(p,0,0))],
            scratch_shapes=[pltpu.VMEM((lanes,tokens),bf16)]),
        compiler_params=pltpu.CompilerParams(vmem_limit_bytes=48<<20),
    )(bounds,segrow,segcol,qkv,qkv,qkv)

def attend_backward(row_len, qb, kb, lanes, span, bounds, segrow, segcol, q_ref,k_ref,v_ref,g_ref,o_ref,lse_ref,qlse_ref,out_ref,kt_ref,dka,dva):
    dq_ref=out_ref.at[:,:lanes]; dk_ref=out_ref.at[:,lanes:2*lanes]; dv_ref=out_ref.at[:,2*lanes:]
    units=lanes//128
    tokens=q_ref.shape[0]
    first_q=lax.broadcasted_iota(jnp.int32,(qb,128),1)<64
    top=lax.broadcasted_iota(jnp.int32,(128,qb),0)<64
    kt_ref[...]=k_ref[...].T
    dka[...]=jnp.zeros_like(dka); dva[...]=jnp.zeros_like(dva)
    def q_step(i,_):
        rows=pl.ds(pl.multiple_of(i*qb,qb),qb)
        own=segrow[pl.ds(i,1),:]
        sq=[];sg=[];dr=[];ls=[]
        for u in range(units):
            cols=pl.ds(u*128,128)
            g=g_ref[rows,cols]
            sq.append(stack_heads(q_ref[rows,cols],first_q)); sg.append(stack_heads(g,first_q))
            t=(g.astype(f32)*o_ref[rows,cols].astype(f32)).T
            dr.append(jnp.concatenate([jnp.sum(t[:64],axis=0,keepdims=True),jnp.sum(t[64:],axis=0,keepdims=True)],axis=1))
            ls.append(lse_ref[u,pl.ds(i,1),:])
        def k_step(j,carry):
            keys=pl.ds(pl.multiple_of(j*kb,kb),kb)
            allowed=segcol[keys,:]==own
            out=[]
            for u in range(units):
                cols=pl.ds(u*128,128)
                s=jnp.where(allowed,dot_nt(k_ref[keys,cols],sq[u]),masked_score)
                p=jnp.exp2(s*rate-ls[u])
                dp=dot_nt(v_ref[keys,cols],sg[u])
                ds=(p*(dp-dr[u])).astype(bf16)
                dva[keys,cols]+=dot_nn(p.astype(bf16),sg[u])
                dka[keys,cols]+=dot_nn(ds,sq[u])
                out.append(carry[u]+dot_nn(kt_ref[cols,keys],ds))
            return tuple(out)
        res=lax.fori_loop(bounds[0,i],bounds[1,i],k_step,tuple(jnp.zeros((128,2*qb),f32) for u in range(units)))
        for u in range(units):
            d=jnp.where(top,res[u][:,:qb],res[u][:,qb:])*0.125
            dq_ref[rows,pl.ds(u*128,128)]=d.T.astype(bf16)
        return 0
    lax.fori_loop(0,row_len//qb,q_step,0)
    dk_ref[:row_len,:]=(dka[...]*0.125).astype(bf16)
    dv_ref[:row_len,:]=dva[...].astype(bf16)
    nq=tokens-row_len
    firstn=lax.broadcasted_iota(jnp.int32,(nq,128),1)<64
    own=lax.broadcasted_iota(jnp.int32,(nq,2*nq),0)//span
    other=(lax.broadcasted_iota(jnp.int32,(nq,2*nq),1)%nq)//span
    keep=own==other
    for u in range(units):
        cols=pl.ds(u*128,128)
        q=q_ref[row_len:,cols]; k=k_ref[row_len:,cols]; v=v_ref[row_len:,cols]; g=g_ref[row_len:,cols]
        st=stack_heads(q,firstn); sg=stack_heads(g,firstn)
        s=jnp.where(keep,dot_nt(k,st),masked_score)
        p=jnp.exp2(s*rate-qlse_ref[u])
        dp=dot_nt(v,sg)
        ds=(p*(dp-jnp.sum(p*dp,axis=0,keepdims=True))).astype(bf16)
        dv_ref[row_len:,cols]=dot_nn(p.astype(bf16),sg).astype(bf16)
        dk_ref[row_len:,cols]=(dot_nn(ds,st)*0.125).astype(bf16)
        d=lax.dot_general(ds,k,(((0,),(0,)),((),())),preferred_element_type=f32)
        dq_ref[row_len:,cols]=(jnp.where(firstn,d[:nq],d[nq:])*0.125).astype(bf16)

def attention_backward(qkv,g,o,lse,qlse,segrow,segcol,bounds,row_len,span):
    tokens,width=g.shape
    qb,kb,lanes=q_rows,k_rows,width
    nq=tokens-row_len
    steps=width//lanes
    def spec(off): return pl.BlockSpec((tokens,lanes),lambda p,*_:(0,p+off))
    full=lambda a: pl.BlockSpec(a.shape,lambda p,*_:(0,)*a.ndim)
    sd=jax.ShapeDtypeStruct((tokens,3*width),bf16)
    return pl.pallas_call(
        partial(attend_backward,row_len,qb,kb,lanes,span),
        out_shape=sd,
        grid_spec=pltpu.PrefetchScalarGridSpec(num_scalar_prefetch=1,grid=(steps,),
            in_specs=[full(segrow),full(segcol)]+[spec(0),spec(1),spec(2),spec(0),spec(0)]+[pl.BlockSpec((lanes//128,row_len//qb,2*qb),lambda p,*_:(p,0,0)),pl.BlockSpec((lanes//128,1,2*nq),lambda p,*_:(p,0,0))],
            out_specs=pl.BlockSpec((tokens,3*lanes),lambda p,*_:(0,0)),
            scratch_shapes=[pltpu.VMEM((lanes,tokens),bf16),pltpu.VMEM((row_len,lanes),f32),pltpu.VMEM((row_len,lanes),f32)]),
        compiler_params=pltpu.CompilerParams(vmem_limit_bytes=56<<20),
    )(bounds,segrow,segcol,qkv,qkv,qkv,g,o,lse,qlse)


def level_units(values, width):
    lanes = lax.broadcasted_iota(jnp.int32, values.shape, 1)
    part_cols = jnp.where(lanes < width, values, 0.0)
    inv_scale = lax.rsqrt(jnp.sum(part_cols * part_cols, axis=-1, keepdims=True) + unit_eps)
    return part_cols * inv_scale, inv_scale


def three_parts(values):
    top = values.astype(bf16)
    rest = values - top.astype(f32)
    middle = rest.astype(bf16)
    return top, middle, (rest - middle.astype(f32)).astype(bf16)


def exact_dot(values, marks):
    return sum(dot_nn(part, marks) for part in three_parts(values))


def keep_doc_units(levels, doc_ref, low_ref):
    @pl.when(pl.program_id(0) == 0)
    def _():
        docs = doc_ref[...].astype(f32)
        for position, width in enumerate(levels):
            low_ref[position] = level_units(docs, width)[0].astype(bf16)


def interact_forward(levels, span, doc_ref, member_ref, query_ref, logit_ref, sums_ref, low_ref):
    keep_doc_units(levels, doc_ref, low_ref)
    queries = query_ref[...].astype(f32)
    member = member_ref[...]
    for position, width in enumerate(levels):
        unit_rows = level_units(queries, width)[0].astype(bf16)
        powers = jnp.exp(dot_nt(unit_rows, low_ref[position]) / softness)
        doc_sums = exact_dot(powers, member)
        sums_ref[position] = doc_sums
        logs = (softness * jnp.log(doc_sums)).reshape(-1, span, doc_sums.shape[1])
        logit_ref[position] = jnp.sum(logs, axis=1) / (span * sharpness_divisor)


def interact_backward(
    levels, span, doc_ref, member_t_ref, query_ref, sums_ref, grad_ref, query_grad_ref,
    doc_grad_ref, low_ref, held_ref,
):
    keep_doc_units(levels, doc_ref, low_ref)

    @pl.when(pl.program_id(0) == 0)
    def _():
        held_ref[...] = jnp.zeros_like(held_ref)

    queries = query_ref[...].astype(f32)
    member_t = member_t_ref[...]
    total = jnp.zeros(queries.shape, f32)
    for position, width in enumerate(levels):
        unit_full, inv_scale = level_units(queries, width)
        unit_rows = unit_full.astype(bf16)
        powers = jnp.exp(dot_nt(unit_rows, low_ref[position]) / softness)
        grads = grad_ref[position]
        rows = jnp.broadcast_to(grads[:, None, :], (grads.shape[0], span, grads.shape[1]))
        rows = rows.reshape(-1, grads.shape[1]) / sums_ref[position]
        grad_scores = (powers * exact_dot(rows, member_t)).astype(bf16)
        grad_unit = dot_nn(grad_scores, low_ref[position])
        held_ref[position] += matmul_left_t(grad_scores, unit_rows)
        total = total + inv_scale * (
            grad_unit - unit_full * jnp.sum(grad_unit * unit_full, axis=-1, keepdims=True)
        )
    query_grad_ref[...] = total

    @pl.when(pl.program_id(0) == pl.num_programs(0) - 1)
    def _():
        docs = doc_ref[...].astype(f32)
        doc_total = jnp.zeros(docs.shape, f32)
        for position, width in enumerate(levels):
            unit_full, inv_scale = level_units(docs, width)
            grad_unit = held_ref[position]
            doc_total = doc_total + inv_scale * (
                grad_unit - unit_full * jnp.sum(grad_unit * unit_full, axis=-1, keepdims=True)
            )
        doc_grad_ref[...] = doc_total


def interaction_logits(levels, span, docs, member, queries):
    tokens, width = queries.shape
    row_len, slots = member.shape
    rows = block_queries * span
    return pl.pallas_call(
        partial(interact_forward, levels, span),
        grid=(tokens // rows,),
        out_shape=(
            jax.ShapeDtypeStruct((3, tokens // span, slots), f32),
            jax.ShapeDtypeStruct((3, tokens, slots), f32),
        ),
        in_specs=[
            pl.BlockSpec((row_len, width), lambda i: (0, 0)),
            pl.BlockSpec((row_len, slots), lambda i: (0, 0)),
            pl.BlockSpec((rows, width), lambda i: (i, 0)),
        ],
        out_specs=(
            pl.BlockSpec((3, block_queries, slots), lambda i: (0, i, 0)),
            pl.BlockSpec((3, rows, slots), lambda i: (0, i, 0)),
        ),
        scratch_shapes=[pltpu.VMEM((3, row_len, width), bf16)],
        compiler_params=pltpu.CompilerParams(vmem_limit_bytes=40 << 20),
    )(docs, member, queries)


def interaction_grads(levels, span, docs, member_t, queries, sums, grads):
    tokens, width = queries.shape
    slots, row_len = member_t.shape
    rows = block_queries * span
    return pl.pallas_call(
        partial(interact_backward, levels, span),
        grid=(tokens // rows,),
        out_shape=(
            jax.ShapeDtypeStruct((tokens, width), f32),
            jax.ShapeDtypeStruct((row_len, width), f32),
        ),
        in_specs=[
            pl.BlockSpec((row_len, width), lambda i: (0, 0)),
            pl.BlockSpec((slots, row_len), lambda i: (0, 0)),
            pl.BlockSpec((rows, width), lambda i: (i, 0)),
            pl.BlockSpec((3, rows, slots), lambda i: (0, i, 0)),
            pl.BlockSpec((3, block_queries, slots), lambda i: (0, i, 0)),
        ],
        out_specs=(
            pl.BlockSpec((rows, width), lambda i: (i, 0)),
            pl.BlockSpec((row_len, width), lambda i: (0, 0)),
        ),
        scratch_shapes=[
            pltpu.VMEM((3, row_len, width), bf16),
            pltpu.VMEM((3, row_len, width), f32),
        ],
        compiler_params=pltpu.CompilerParams(vmem_limit_bytes=40 << 20),
    )(docs, member_t, queries, sums, grads)


def after(value, *earlier):
    return lax.optimization_barrier((value, *earlier))[0]


def exchange(dp, fsdp, scatter, add, mine_ref, out_ref, held, send_sem, recv_sem):
    count = dp * fsdp
    me = lax.axis_index("dp") * fsdp + lax.axis_index("fsdp")

    def device(other):
        return (other // fsdp, other % fsdp)

    def copy(step, other, place):
        return pltpu.make_async_remote_copy(
            src_ref=mine_ref.at[other] if scatter else mine_ref,
            dst_ref=held.at[place],
            send_sem=send_sem.at[step],
            recv_sem=recv_sem.at[step],
            device_id=device(other),
            device_id_type=pl.DeviceIdType.MESH,
        )

    barrier = pltpu.get_barrier_semaphore()

    @pl.loop(1, count)
    def _(step):
        pl.semaphore_signal(
            barrier, inc=1, device_id=device((me + step) % count),
            device_id_type=pl.DeviceIdType.MESH,
        )

    pl.semaphore_wait(barrier, count - 1)

    @pl.loop(1, count)
    def _(step):
        copy(step, (me + step) % count, me).start()

    held[me] = mine_ref[me] if scatter else mine_ref[...]

    @pl.loop(1, count)
    def _(step):
        arriving = copy(step, (me + step) % count, (me + count - step) % count)
        arriving.wait_send()
        arriving.wait_recv()

    if add:
        out_ref[...] = jnp.sum(held[...].astype(f32), axis=0)
    else:
        out_ref[...] = held[...]


def exchanged(links, value, scatter, add, name):
    block = value.shape[1:] if scatter else value.shape
    whole = (links.count,) + block
    return pl.pallas_call(
        partial(exchange, links.dp, links.fsdp, scatter, add),
        out_shape=jax.ShapeDtypeStruct(block if add else whole, f32 if add else value.dtype),
        in_specs=[pl.BlockSpec(memory_space=pltpu.VMEM)],
        out_specs=pl.BlockSpec(memory_space=pltpu.VMEM),
        scratch_shapes=[
            pltpu.VMEM(whole, value.dtype),
            pltpu.SemaphoreType.DMA((links.count,)),
            pltpu.SemaphoreType.DMA((links.count,)),
        ],
        compiler_params=pltpu.CompilerParams(collective_id=name, has_side_effects=True),
    )(value)


class Growing:
    def __init__(self, links, shard, lane):
        self.links, self.order, self.block = links, list(links.orders[lane]), shard.shape
        self.held = shard.reshape((1,) * links.bits + shard.shape)

    def wait(self, *earlier):
        self.held = after(self.held, *earlier)

    def launch(self):
        self.place = self.order.pop(0)
        self.before = self.held
        self.arrived = self.links.swap(self.held, 1 << self.place)

    def merge(self, *earlier):
        axis = self.links.bits - 1 - self.place
        mine = self.links.side(self.place)
        held = self.held
        arrived = after(self.arrived, *earlier) if earlier else self.arrived
        shape = held.shape[:axis] + (2,) + held.shape[axis + 1 :]
        own = lax.broadcasted_iota(jnp.int32, shape, axis) == mine
        self.held = lax.optimization_barrier(jnp.where(own, held, arrived))

    def full(self):
        while self.order:
            self.launch()
            self.merge()
        return self.held.reshape((self.links.count,) + self.block)


class Shrinking:
    def __init__(self, links, blocks, lane, wire):
        self.links, self.order, self.block = links, list(links.orders[lane]), blocks.shape[1:]
        self.wire = wire
        self.held = blocks.astype(wire).reshape((2,) * links.bits + self.block)

    def wait(self, *earlier):
        self.held = after(self.held, *earlier)

    def launch(self):
        if not self.order:
            return
        self.place = self.order.pop()
        axis = self.links.bits - 1 - self.place
        self.leaving = lax.dynamic_slice_in_dim(
            self.held, 1 - self.links.side(self.place), 1, axis
        )
        self.arrived = self.links.swap(self.leaving, 1 << self.place)

    def merge(self, *earlier):
        if self.arrived is None:
            return
        axis = self.links.bits - 1 - self.place
        kept = lax.dynamic_slice_in_dim(self.held, self.links.side(self.place), 1, axis)
        arrived = after(self.arrived, *earlier) if earlier else self.arrived
        total = kept.astype(f32) + arrived.astype(f32)
        self.held = total.astype(self.wire) if self.order else total
        self.arrived = None

    def mine(self):
        while self.order:
            self.launch()
            self.merge()
        return self.held.reshape(self.block)


class Links:
    def __init__(self, dp, fsdp):
        self.dp, self.fsdp, self.count = dp, fsdp, dp * fsdp
        self.bits = self.count.bit_length() - 1
        inner_bits = fsdp.bit_length() - 1
        low, high = list(range(inner_bits)), list(range(inner_bits, self.bits))
        inner, rest = low[:1], low[1:]
        near, far = high[:1], high[1:][::-1]
        self.orders = (far + rest[::-1] + near + inner, far + near + rest[::-1] + inner)

    def side(self, place):
        return (lax.axis_index(AXES) >> place) & 1

    def swap(self, value, bit):
        return lax.ppermute(value, AXES, [(d, d ^ bit) for d in range(self.count)])

    def growing(self, shard, lane=0):
        return Growing(self, shard, lane)

    def shrinking(self, blocks, lane=0, wire=bf16):
        return Shrinking(self, blocks, lane, wire)

    def total(self, value):
        high, wide = value.shape
        padded = jnp.pad(value, ((0, -high % 8), (0, -wide % 128)))
        return exchanged(self, padded, False, True, 0)[:high, :wide]

    def everyone(self, value):
        return exchanged(self, value, False, False, 1)

    def owners_sum(self, blocks):
        return exchanged(self, blocks.astype(bf16), True, True, 2)


class Whole:
    def __init__(self, value):
        self.held = self.before = self.leaving = value

    def wait(self, *earlier):
        pass

    def launch(self):
        pass

    def merge(self, *earlier):
        pass

    def full(self):
        return self.held

    def mine(self):
        return self.held


class PlainLinks(Links):
    def growing(self, shard, lane=0):
        return Whole(lax.all_gather(shard, AXES, axis=0))

    def shrinking(self, blocks, lane=0, wire=bf16):
        return Whole(lax.psum_scatter(blocks, AXES, scatter_dimension=0, tiled=False))

    def total(self, value):
        return lax.psum(value, AXES)

    def everyone(self, value):
        return lax.all_gather(value, AXES, axis=0)

    def owners_sum(self, blocks):
        return lax.psum_scatter(blocks, AXES, scatter_dimension=0, tiled=False)


def make_links(mesh):
    dp, fsdp = mesh.shape["dp"], mesh.shape["fsdp"]
    paired = (dp & (dp - 1)) == 0 and (fsdp & (fsdp - 1)) == 0 and dp * fsdp <= 64
    return (Links if paired else PlainLinks)(dp, fsdp)


def tables(lengths, row_len):
    ends = jnp.cumsum(lengths)
    starts = ends - lengths
    places = jnp.arange(row_len, dtype=jnp.int32)
    segment = jnp.sum((places[:, None] >= ends[None, :]).astype(jnp.int32), axis=1)
    rows = segment.reshape(row_len // q_rows, q_rows)
    ids = jnp.arange(lengths.shape[0])
    low = jnp.sum(jnp.where(rows[:, :1] == ids[None, :], starts[None, :], 0), axis=1)
    high = jnp.sum(jnp.where(rows[:, -1:] == ids[None, :], ends[None, :], 0), axis=1)
    bounds = jnp.stack([low // k_rows, (high + k_rows - 1) // k_rows]).astype(jnp.int32)
    return segment, jnp.concatenate([rows, rows], axis=1), segment[:, None], bounds


def body(
    links,
    doc_hidden,
    query_hidden,
    w_query,
    w_key,
    w_value,
    w_out,
    w_up,
    w_down,
    w_proj,
    biases,
    gains,
    up_bias,
    seg_lengths,
    positives,
):
    count = links.count
    row_len = doc_hidden.shape[1]
    model_width = doc_hidden.shape[2]
    query_count = query_hidden.shape[0]
    span = query_hidden.shape[1]
    doc_slots = seg_lengths.shape[1] - 1
    proj_width = w_proj.shape[1]
    ff = up_bias.shape[0] * count
    shard_cols = biases.shape[1]
    shard_rows = w_query.shape[0]
    part = model_width // 2
    small = jnp.concatenate(
        [biases.reshape(-1), gains.reshape(-1), up_bias.reshape(-1)], axis=0
    )[None]

    def rows_of(full):
        return full.reshape(full.shape[0] * full.shape[1], full.shape[2])

    sides = []
    for side in range(2):
        cut = slice(side * part, (side + 1) * part)
        shard = jnp.concatenate([w_query[:, cut], w_key[:, cut], w_value[:, cut]], axis=1)
        sides.append(links.growing(shard, side))
    small_part = links.growing(small, 0)
    out_part = links.growing(jnp.concatenate([w_out, w_proj], axis=1), 0)
    up_part = links.growing(w_up, 0)
    down_part = links.growing(w_down, 1)
    rest = (out_part, up_part, down_part)
    for hop in range(5):
        for one in sides:
            one.launch()
        if hop > 0:
            small_part.wait(sides[0].before, sides[1].before)
        small_part.launch()
        for one in sides:
            one.merge()
        first = (sides[0].held, sides[1].held)
        small_part.merge(*first)
        for one in rest:
            if hop == 0:
                one.wait(*first)
                one.launch()
            if hop == 2 or hop == 3:
                one.merge(*first)
                one.launch()
    small_full = small_part.full().reshape(count, -1)
    full_qkv = [rows_of(one.full()) for one in sides]
    full_biases = (
        small_full[:, : 6 * shard_cols]
        .reshape(count, 6, shard_cols)
        .transpose(1, 0, 2)
        .reshape(6, model_width)
        .astype(f32)
    )
    full_gains = (
        small_full[:, 6 * shard_cols : 8 * shard_cols]
        .reshape(count, 2, shard_cols)
        .transpose(1, 0, 2)
        .reshape(2, model_width)
        .astype(f32)
    )
    full_upbias = small_full[:, 8 * shard_cols :].reshape(ff).astype(f32)

    tokens = jnp.concatenate(
        [doc_hidden[0], query_hidden.reshape(query_count * span, model_width)], axis=0
    )
    segment, segrow, segcol, bounds = tables(seg_lengths[0], row_len)
    slot_ids = jnp.arange(doc_slots, dtype=jnp.int32)
    member = (segment[:, None] == slot_ids[None, :]).astype(f32)
    member_t = (slot_ids[:, None] == segment[None, :]).astype(f32)
    zero_row = jnp.zeros((part,), f32)
    qkv, contexts, saved = [], [], []
    for side in range(2):
        cut = slice(side * part, (side + 1) * part)
        bias = jnp.concatenate([full_biases[0, cut], zero_row, full_biases[1, cut]])
        qkv.append((matmul_plain(tokens, full_qkv[side]) + bias).astype(bf16))
    for one in rest:
        one.merge(*qkv)
        one.launch()
    for side in range(2):
        qkv[side] = after(qkv[side], *[one.before for one in rest])
        context, lse, query_lse = attention_forward(
            qkv[side], segrow, segcol, bounds, row_len, span
        )
        if side == 0:
            out_part.merge(context)
            out_part.launch()
        contexts.append(context)
        saved.append((lse, query_lse))
    for one in (up_part, down_part):
        one.merge(*contexts)
        one.launch()
    contexts[1] = after(contexts[1], up_part.before, down_part.before)
    out_part.merge()
    out_proj = rows_of(out_part.full())
    full_out, full_proj = out_proj[:, :model_width], out_proj[:, model_width:]
    up_part.merge()
    down_part.merge()
    full_up = rows_of(up_part.full())
    full_down = rows_of(down_part.full())
    attn_out = (
        matmul_plain(contexts[0], full_out[:part])
        + matmul_plain(contexts[1], full_out[part:])
        + full_biases[2]
    )
    first_out, first_normed, first_scale = layer_norm_parts(
        tokens.astype(f32) + attn_out, full_gains[0], full_biases[3]
    )
    first_low = first_out.astype(bf16)
    up_pre = matmul_plain(first_low, full_up) + full_upbias
    share = 0.5 * (1.0 + lax.erf(up_pre * root_half))
    gelu_out = (up_pre * share).astype(bf16)
    density = jnp.exp(-0.5 * up_pre * up_pre) * density_peak
    slope = (share + up_pre * density).astype(bf16)
    gelu_out, slope = lax.optimization_barrier((gelu_out, slope))
    ffn_out = matmul_plain(gelu_out, full_down) + full_biases[4]
    second_out, second_normed, second_scale = layer_norm_parts(
        first_out + ffn_out, full_gains[1], full_biases[5]
    )
    second_low = second_out.astype(bf16)
    vectors = matmul_plain(second_low, full_proj).astype(bf16)
    doc_vectors = vectors[:row_len]
    query_vectors = vectors[row_len:].reshape(query_count * span, proj_width)
    every_query = links.everyone(query_vectors).reshape(count * query_count * span, proj_width)
    query_total = count * query_count
    levels = (proj_width, proj_width * 3 // 4, proj_width // 2)
    logits, doc_sums = interaction_logits(levels, span, doc_vectors, member.astype(bf16), every_query)
    logits = logits.transpose(1, 0, 2)
    powers = jnp.exp(logits)
    local_sum = jnp.sum(powers, axis=-1)
    my_row = lax.axis_index(AXES)
    chosen = ((positives - my_row * doc_slots)[:, None] == slot_ids[None, :]).astype(f32)
    local_pick = jnp.sum(logits * chosen[:, None, :], axis=-1)
    both = links.total(jnp.concatenate([local_sum, local_pick], axis=1).T).T
    all_sums, picked = both[:, :3], both[:, 3:]
    loss = jnp.sum(jnp.log(all_sums) - picked) / query_total
    score_derivative = (powers / all_sums[:, :, None] - chosen[:, None, :]) / query_total
    peak_match_derivative = score_derivative / (span * sharpness_divisor)

    query_terms, doc_vec_grad = interaction_grads(
        levels, span, doc_vectors, member_t.astype(bf16), every_query, doc_sums,
        peak_match_derivative.transpose(1, 0, 2),
    )
    query_terms = query_terms.reshape(count, query_count * span, proj_width)
    query_vec_grad = links.owners_sum(query_terms)
    grad_vectors = jnp.concatenate([doc_vec_grad, query_vec_grad], axis=0).astype(bf16)

    def spread_rows_of(full):
        return full.reshape(count, full.shape[0] // count, full.shape[1])

    proj_grad = matmul_left_t(second_low, grad_vectors)
    grad_second = matmul_right_t(grad_vectors, full_proj)
    grad_mid, gain_two, bias_two = layer_norm_back(
        grad_second, second_normed, second_scale, full_gains[1]
    )
    grad_ffn = grad_mid.astype(bf16)
    down_grad = matmul_left_t(gelu_out, grad_ffn)
    down_sum = links.shrinking(spread_rows_of(down_grad), 1)
    down_sum.launch()
    down_bias = jnp.sum(grad_ffn, axis=0, dtype=f32)
    grad_gelu = matmul_right_t(after(grad_ffn, down_sum.leaving), full_down)
    grad_up = (grad_gelu * slope.astype(f32)).astype(bf16)
    upbias_grad = jnp.sum(grad_up, axis=0, dtype=f32)
    up_grad = matmul_left_t(first_low, grad_up)
    up_sum = links.shrinking(spread_rows_of(up_grad), 0)
    up_sum.launch()
    down_sum.merge(up_sum.leaving)
    down_sum.launch()
    grad_first = grad_mid + matmul_right_t(after(grad_up, down_sum.leaving), full_up)
    grad_res, gain_one, bias_one = layer_norm_back(
        grad_first, first_normed, first_scale, full_gains[0]
    )
    up_sum.merge(grad_res)
    up_sum.launch()
    grad_attn = after(grad_res.astype(bf16), up_sum.leaving)
    out_bias = jnp.sum(grad_attn, axis=0, dtype=f32)
    out_grad = jnp.concatenate([matmul_left_t(c, grad_attn) for c in contexts], axis=0)
    out_sum = links.shrinking(spread_rows_of(jnp.concatenate([out_grad, proj_grad], axis=1)), 0)
    out_sum.launch()
    input_grad = grad_res
    query_bias, value_bias, qkv_sums = [], [], []
    grad_contexts = [
        matmul_right_t(grad_attn, full_out[side * part : (side + 1) * part]).astype(bf16)
        for side in range(2)
    ]
    down_sum.merge(*grad_contexts)
    down_sum.launch()
    earlier = (out_sum.leaving, down_sum.leaving)
    for side in range(2):
        grad_qkv = attention_backward(
            qkv[side], after(grad_contexts[side], *earlier), contexts[side], *saved[side], segrow,
            segcol, bounds, row_len, span,
        )
        if side == 1:
            up_sum.merge(grad_qkv)
            up_sum.launch()
            down_sum.merge(grad_qkv)
            down_sum.launch()
            qkv_sums[0].merge(grad_qkv)
            qkv_sums[0].launch()
            grad_qkv = after(grad_qkv, up_sum.leaving, down_sum.leaving, qkv_sums[0].leaving)
        query_bias.append(jnp.sum(grad_qkv[:, :part], axis=0, dtype=f32))
        value_bias.append(jnp.sum(grad_qkv[:, 2 * part :], axis=0, dtype=f32))
        qkv_grad = matmul_left_t(tokens, grad_qkv)
        if side == 0:
            qkv_sums.append(links.shrinking(spread_rows_of(qkv_grad), side))
        else:
            wide = qkv_grad.shape[1] // 2
            for lane in range(2):
                piece = qkv_grad[:, lane * wide : (lane + 1) * wide]
                qkv_sums.append(links.shrinking(spread_rows_of(piece), lane))
        for one in qkv_sums[side:]:
            one.launch()
        if side == 0:
            out_sum.merge(qkv_sums[0].leaving)
            out_sum.launch()
            up_sum.merge(qkv_sums[0].leaving)
            up_sum.launch()
            earlier = (qkv_sums[0].leaving, out_sum.leaving, up_sum.leaving)
        grad_qkv = after(grad_qkv, *[one.leaving for one in qkv_sums[side:]])
        input_grad = input_grad + matmul_right_t(grad_qkv, full_qkv[side])
    bias_grads = jnp.stack(
        [
            jnp.concatenate(query_bias),
            jnp.concatenate(value_bias),
            out_bias,
            bias_one,
            down_bias,
            bias_two,
            gain_one,
            gain_two,
        ],
        axis=0,
    )
    small_grads = jnp.concatenate(
        [
            bias_grads.reshape(8, count, shard_cols).transpose(1, 0, 2).reshape(count, -1),
            upbias_grad.reshape(count, -1),
        ],
        axis=1,
    )
    small_sum = links.shrinking(small_grads[:, None, :], 0, wire=f32)
    small_sum.launch()
    first, others, slow = qkv_sums[1:], [small_sum, qkv_sums[0], out_sum], [up_sum, down_sum]
    last = [one.leaving for one in first]
    for hop in range(links.bits):
        for one in first:
            one.merge()
        for one in others:
            one.merge(*last)
        for one in first + others:
            one.launch()
        last = [one.held for one in first]
        if hop == 0 or hop == 3:
            for one in slow:
                one.merge(*last)
                one.launch()
        last = [one.leaving for one in first]
    down_shard, up_shard, out_proj_shard = down_sum.mine(), up_sum.mine(), out_sum.mine()
    qkv_shards = [one.mine() for one in qkv_sums]
    qkv_shards = [qkv_shards[0], jnp.concatenate(qkv_shards[1:], axis=-1)]
    small_shard = small_sum.mine()[0]
    shards = [
        jnp.concatenate([s[:, i * part : (i + 1) * part] for s in qkv_shards], axis=1)
        for i in range(3)
    ]
    return (
        loss,
        input_grad[:row_len].reshape(1, row_len, model_width),
        input_grad[row_len:].reshape(query_count, span, model_width),
        shards[0],
        shards[1],
        shards[2],
        out_proj_shard[:, :model_width],
        up_shard,
        down_shard,
        out_proj_shard[:, model_width:],
        small_shard[: 6 * shard_cols].reshape(6, shard_cols),
        small_shard[6 * shard_cols : 8 * shard_cols].reshape(2, shard_cols),
        small_shard[8 * shard_cols :],
    )


def solution(mesh):
    return jax.shard_map(
        partial(body, make_links(mesh)),
        mesh=mesh,
        in_specs=(
            P(("dp", "fsdp"), None, None),
            P(("dp", "fsdp"), None, None),
            P(("dp", "fsdp"), None),
            P(("dp", "fsdp"), None),
            P(("dp", "fsdp"), None),
            P(("dp", "fsdp"), None),
            P(("dp", "fsdp"), None),
            P(("dp", "fsdp"), None),
            P(("dp", "fsdp"), None),
            P(None, ("dp", "fsdp")),
            P(None, ("dp", "fsdp")),
            P(("dp", "fsdp")),
            P(("dp", "fsdp"), None),
            P(),
        ),
        out_specs=(
            P(),
            P(("dp", "fsdp"), None, None),
            P(("dp", "fsdp"), None, None),
            P(("dp", "fsdp"), None),
            P(("dp", "fsdp"), None),
            P(("dp", "fsdp"), None),
            P(("dp", "fsdp"), None),
            P(("dp", "fsdp"), None),
            P(("dp", "fsdp"), None),
            P(("dp", "fsdp"), None),
            P(None, ("dp", "fsdp")),
            P(None, ("dp", "fsdp")),
            P(("dp", "fsdp")),
        ),
        check_vma=False,
    )
```

```python
from functools import partial

import jax
import jax.numpy as jnp
from jax import lax
from jax.experimental import pallas as pl
from jax.experimental.pallas import tpu as pltpu
from jax.sharding import PartitionSpec as P

softness = 0.1
sharpness_divisor = 0.2
norm_eps = 1e-05
unit_eps = 1e-06
root_half = 0.7071067811865476
density_peak = 0.3989422804014327
head_width = 64
block_queries = 8
masked_score = -1e30
rate = 0.125 * 1.4426950408889634
q_rows = 256
k_rows = 256
f32 = jnp.float32
bf16 = jnp.bfloat16
AXES = ("dp", "fsdp")

def matmul_plain(left, right):
    return jnp.dot(left, right, preferred_element_type=jnp.float32)


def matmul_right_t(left, right):
    return lax.dot_general(
        left, right, (((1,), (1,)), ((), ())), preferred_element_type=jnp.float32
    )


def matmul_left_t(left, right):
    return lax.dot_general(
        left, right, (((0,), (0,)), ((), ())), preferred_element_type=jnp.float32
    )


def layer_norm_parts(values, gain_row, bias_row):
    center = values - jnp.mean(values, axis=-1, keepdims=True)
    spread = jnp.mean(center * center, axis=-1, keepdims=True)
    inv_scale = lax.rsqrt(spread + norm_eps)
    normed = center * inv_scale
    return (normed * gain_row + bias_row, normed, inv_scale)


def layer_norm_back(grad_out, normed, inv_scale, gain_row):
    grad_norm = grad_out * gain_row
    mean_grad = jnp.mean(grad_norm, axis=-1, keepdims=True)
    mean_proj = jnp.mean(grad_norm * normed, axis=-1, keepdims=True)
    grad_in = inv_scale * (grad_norm - mean_grad - normed * mean_proj)
    return (grad_in, jnp.sum(grad_out * normed, axis=0), jnp.sum(grad_out, axis=0))


def dot_nt(a,b): return lax.dot_general(a,b,(((1,),(1,)),((),())),preferred_element_type=f32)
def dot_nn(a,b): return jnp.dot(a,b,preferred_element_type=f32)

def stack_heads(block, first):
    zero=jnp.zeros_like(block)
    return jnp.concatenate([jnp.where(first,block,zero),jnp.where(first,zero,block)],axis=0)

def attend_forward(row_len, qb, kb, lanes, span, bounds, segrow, segcol, q_ref,k_ref,v_ref,ctx_ref,lse_ref,qlse_ref,vt_ref):
    units=lanes//128
    tokens=q_ref.shape[0]
    first_q=lax.broadcasted_iota(jnp.int32,(qb,128),1)<64
    top=lax.broadcasted_iota(jnp.int32,(128,qb),0)<64
    vt_ref[...]=v_ref[...].T
    def q_step(i,_):
        rows=pl.ds(pl.multiple_of(i*qb,qb),qb)
        own=segrow[pl.ds(i,1),:]
        stacked=[stack_heads(q_ref[rows,pl.ds(u*128,128)],first_q) for u in range(units)]
        def k_step(j,carry):
            keys=pl.ds(pl.multiple_of(j*kb,kb),kb)
            allowed=segcol[keys,:]==own
            out=[]
            for u in range(units):
                peak,total,acc=carry[u]
                s=jnp.where(allowed,dot_nt(k_ref[keys,pl.ds(u*128,128)],stacked[u]),masked_score)
                new=jnp.maximum(peak,jnp.max(s,axis=0,keepdims=True))
                p=jnp.exp2((s-new)*rate)
                fade=jnp.exp2((peak-new)*rate)
                total=total*fade+jnp.sum(p,axis=0,keepdims=True)
                acc=acc*fade+dot_nn(vt_ref[pl.ds(u*128,128),keys],p.astype(bf16))
                out.append((new,total,acc))
            return tuple(out)
        start=tuple((jnp.full((1,2*qb),masked_score,f32),jnp.zeros((1,2*qb),f32),jnp.zeros((128,2*qb),f32)) for u in range(units))
        res=lax.fori_loop(bounds[0,i],bounds[1,i],k_step,start)
        for u in range(units):
            peak,total,acc=res[u]
            acc=acc/total
            o=jnp.where(top,acc[:,:qb],acc[:,qb:])
            ctx_ref[rows,pl.ds(u*128,128)]=o.T.astype(bf16)
            lse_ref[u,pl.ds(i,1),:]=peak*rate+jnp.log2(total)
        return 0
    lax.fori_loop(0,row_len//qb,q_step,0)
    nq=tokens-row_len
    firstn=lax.broadcasted_iota(jnp.int32,(nq,128),1)<64
    own=lax.broadcasted_iota(jnp.int32,(nq,2*nq),0)//span
    other=(lax.broadcasted_iota(jnp.int32,(nq,2*nq),1)%nq)//span
    keep=own==other
    for u in range(units):
        cols=pl.ds(u*128,128)
        st=stack_heads(q_ref[row_len:,cols],firstn)
        s=jnp.where(keep,dot_nt(k_ref[row_len:,cols],st),masked_score)
        peak=jnp.max(s,axis=0,keepdims=True)
        p=jnp.exp2((s-peak)*rate)
        total=jnp.sum(p,axis=0,keepdims=True)
        p=(p/total).astype(bf16)
        acc=lax.dot_general(p,v_ref[row_len:,cols],(((0,),(0,)),((),())),preferred_element_type=f32)
        ctx_ref[row_len:,cols]=jnp.where(firstn,acc[:nq],acc[nq:]).astype(bf16)
        qlse_ref[u,:,:]=peak*rate+jnp.log2(total)

def attention_forward(qkv,segrow,segcol,bounds,row_len,span):
    tokens=qkv.shape[0]
    width=qkv.shape[1]//3
    qb,kb,lanes=q_rows,k_rows,width
    nq=tokens-row_len
    steps=width//lanes
    def spec(off): return pl.BlockSpec((tokens,lanes),lambda p,*_:(0,p+off))
    full=lambda a: pl.BlockSpec(a.shape,lambda p,*_:(0,)*a.ndim)
    return pl.pallas_call(
        partial(attend_forward,row_len,qb,kb,lanes,span),
        out_shape=(jax.ShapeDtypeStruct((tokens,width),bf16),jax.ShapeDtypeStruct((width//128,row_len//qb,2*qb),f32),jax.ShapeDtypeStruct((width//128,1,2*nq),f32)),
        grid_spec=pltpu.PrefetchScalarGridSpec(num_scalar_prefetch=1,grid=(steps,),
            in_specs=[full(segrow),full(segcol),spec(0),spec(steps),spec(2*steps)],
            out_specs=[pl.BlockSpec((tokens,lanes),lambda p,*_:(0,p)),pl.BlockSpec((lanes//128,row_len//qb,2*qb),lambda p,*_:(p,0,0)),pl.BlockSpec((lanes//128,1,2*nq),lambda p,*_:(p,0,0))],
            scratch_shapes=[pltpu.VMEM((lanes,tokens),bf16)]),
        compiler_params=pltpu.CompilerParams(vmem_limit_bytes=48<<20),
    )(bounds,segrow,segcol,qkv,qkv,qkv)

def attend_backward(row_len, qb, kb, lanes, span, bounds, segrow, segcol, q_ref,k_ref,v_ref,g_ref,o_ref,lse_ref,qlse_ref,out_ref,kt_ref,dka,dva):
    dq_ref=out_ref.at[:,:lanes]; dk_ref=out_ref.at[:,lanes:2*lanes]; dv_ref=out_ref.at[:,2*lanes:]
    units=lanes//128
    tokens=q_ref.shape[0]
    first_q=lax.broadcasted_iota(jnp.int32,(qb,128),1)<64
    top=lax.broadcasted_iota(jnp.int32,(128,qb),0)<64
    kt_ref[...]=k_ref[...].T
    dka[...]=jnp.zeros_like(dka); dva[...]=jnp.zeros_like(dva)
    def q_step(i,_):
        rows=pl.ds(pl.multiple_of(i*qb,qb),qb)
        own=segrow[pl.ds(i,1),:]
        sq=[];sg=[];dr=[];ls=[]
        for u in range(units):
            cols=pl.ds(u*128,128)
            g=g_ref[rows,cols]
            sq.append(stack_heads(q_ref[rows,cols],first_q)); sg.append(stack_heads(g,first_q))
            t=(g.astype(f32)*o_ref[rows,cols].astype(f32)).T
            dr.append(jnp.concatenate([jnp.sum(t[:64],axis=0,keepdims=True),jnp.sum(t[64:],axis=0,keepdims=True)],axis=1))
            ls.append(lse_ref[u,pl.ds(i,1),:])
        def k_step(j,carry):
            keys=pl.ds(pl.multiple_of(j*kb,kb),kb)
            allowed=segcol[keys,:]==own
            out=[]
            for u in range(units):
                cols=pl.ds(u*128,128)
                s=jnp.where(allowed,dot_nt(k_ref[keys,cols],sq[u]),masked_score)
                p=jnp.exp2(s*rate-ls[u])
                dp=dot_nt(v_ref[keys,cols],sg[u])
                ds=(p*(dp-dr[u])).astype(bf16)
                dva[keys,cols]+=dot_nn(p.astype(bf16),sg[u])
                dka[keys,cols]+=dot_nn(ds,sq[u])
                out.append(carry[u]+dot_nn(kt_ref[cols,keys],ds))
            return tuple(out)
        res=lax.fori_loop(bounds[0,i],bounds[1,i],k_step,tuple(jnp.zeros((128,2*qb),f32) for u in range(units)))
        for u in range(units):
            d=jnp.where(top,res[u][:,:qb],res[u][:,qb:])*0.125
            dq_ref[rows,pl.ds(u*128,128)]=d.T.astype(bf16)
        return 0
    lax.fori_loop(0,row_len//qb,q_step,0)
    dk_ref[:row_len,:]=(dka[...]*0.125).astype(bf16)
    dv_ref[:row_len,:]=dva[...].astype(bf16)
    nq=tokens-row_len
    firstn=lax.broadcasted_iota(jnp.int32,(nq,128),1)<64
    own=lax.broadcasted_iota(jnp.int32,(nq,2*nq),0)//span
    other=(lax.broadcasted_iota(jnp.int32,(nq,2*nq),1)%nq)//span
    keep=own==other
    for u in range(units):
        cols=pl.ds(u*128,128)
        q=q_ref[row_len:,cols]; k=k_ref[row_len:,cols]; v=v_ref[row_len:,cols]; g=g_ref[row_len:,cols]
        st=stack_heads(q,firstn); sg=stack_heads(g,firstn)
        s=jnp.where(keep,dot_nt(k,st),masked_score)
        p=jnp.exp2(s*rate-qlse_ref[u])
        dp=dot_nt(v,sg)
        ds=(p*(dp-jnp.sum(p*dp,axis=0,keepdims=True))).astype(bf16)
        dv_ref[row_len:,cols]=dot_nn(p.astype(bf16),sg).astype(bf16)
        dk_ref[row_len:,cols]=(dot_nn(ds,st)*0.125).astype(bf16)
        d=lax.dot_general(ds,k,(((0,),(0,)),((),())),preferred_element_type=f32)
        dq_ref[row_len:,cols]=(jnp.where(firstn,d[:nq],d[nq:])*0.125).astype(bf16)

def attention_backward(qkv,g,o,lse,qlse,segrow,segcol,bounds,row_len,span):
    tokens,width=g.shape
    qb,kb,lanes=q_rows,k_rows,width
    nq=tokens-row_len
    steps=width//lanes
    def spec(off): return pl.BlockSpec((tokens,lanes),lambda p,*_:(0,p+off))
    full=lambda a: pl.BlockSpec(a.shape,lambda p,*_:(0,)*a.ndim)
    sd=jax.ShapeDtypeStruct((tokens,3*width),bf16)
    return pl.pallas_call(
        partial(attend_backward,row_len,qb,kb,lanes,span),
        out_shape=sd,
        grid_spec=pltpu.PrefetchScalarGridSpec(num_scalar_prefetch=1,grid=(steps,),
            in_specs=[full(segrow),full(segcol)]+[spec(0),spec(1),spec(2),spec(0),spec(0)]+[pl.BlockSpec((lanes//128,row_len//qb,2*qb),lambda p,*_:(p,0,0)),pl.BlockSpec((lanes//128,1,2*nq),lambda p,*_:(p,0,0))],
            out_specs=pl.BlockSpec((tokens,3*lanes),lambda p,*_:(0,0)),
            scratch_shapes=[pltpu.VMEM((lanes,tokens),bf16),pltpu.VMEM((row_len,lanes),f32),pltpu.VMEM((row_len,lanes),f32)]),
        compiler_params=pltpu.CompilerParams(vmem_limit_bytes=56<<20),
    )(bounds,segrow,segcol,qkv,qkv,qkv,g,o,lse,qlse)


def level_units(values, width):
    lanes = lax.broadcasted_iota(jnp.int32, values.shape, 1)
    part_cols = jnp.where(lanes < width, values, 0.0)
    inv_scale = lax.rsqrt(jnp.sum(part_cols * part_cols, axis=-1, keepdims=True) + unit_eps)
    return part_cols * inv_scale, inv_scale


def three_parts(values):
    top = values.astype(bf16)
    rest = values - top.astype(f32)
    middle = rest.astype(bf16)
    return top, middle, (rest - middle.astype(f32)).astype(bf16)


def exact_dot(values, marks):
    return sum(dot_nn(part, marks) for part in three_parts(values))


def keep_doc_units(levels, doc_ref, low_ref):
    @pl.when(pl.program_id(0) == 0)
    def _():
        docs = doc_ref[...].astype(f32)
        for position, width in enumerate(levels):
            low_ref[position] = level_units(docs, width)[0].astype(bf16)


def interact_forward(levels, span, doc_ref, member_ref, query_ref, logit_ref, sums_ref, low_ref):
    keep_doc_units(levels, doc_ref, low_ref)
    queries = query_ref[...].astype(f32)
    member = member_ref[...]
    for position, width in enumerate(levels):
        unit_rows = level_units(queries, width)[0].astype(bf16)
        powers = jnp.exp(dot_nt(unit_rows, low_ref[position]) / softness)
        doc_sums = exact_dot(powers, member)
        sums_ref[position] = doc_sums
        logs = (softness * jnp.log(doc_sums)).reshape(-1, span, doc_sums.shape[1])
        logit_ref[position] = jnp.sum(logs, axis=1) / (span * sharpness_divisor)


def interact_backward(
    levels, span, doc_ref, member_t_ref, query_ref, sums_ref, grad_ref, query_grad_ref,
    doc_grad_ref, low_ref, held_ref,
):
    keep_doc_units(levels, doc_ref, low_ref)

    @pl.when(pl.program_id(0) == 0)
    def _():
        held_ref[...] = jnp.zeros_like(held_ref)

    queries = query_ref[...].astype(f32)
    member_t = member_t_ref[...]
    total = jnp.zeros(queries.shape, f32)
    for position, width in enumerate(levels):
        unit_full, inv_scale = level_units(queries, width)
        unit_rows = unit_full.astype(bf16)
        powers = jnp.exp(dot_nt(unit_rows, low_ref[position]) / softness)
        grads = grad_ref[position]
        rows = jnp.broadcast_to(grads[:, None, :], (grads.shape[0], span, grads.shape[1]))
        rows = rows.reshape(-1, grads.shape[1]) / sums_ref[position]
        grad_scores = (powers * exact_dot(rows, member_t)).astype(bf16)
        grad_unit = dot_nn(grad_scores, low_ref[position])
        held_ref[position] += matmul_left_t(grad_scores, unit_rows)
        total = total + inv_scale * (
            grad_unit - unit_full * jnp.sum(grad_unit * unit_full, axis=-1, keepdims=True)
        )
    query_grad_ref[...] = total

    @pl.when(pl.program_id(0) == pl.num_programs(0) - 1)
    def _():
        docs = doc_ref[...].astype(f32)
        doc_total = jnp.zeros(docs.shape, f32)
        for position, width in enumerate(levels):
            unit_full, inv_scale = level_units(docs, width)
            grad_unit = held_ref[position]
            doc_total = doc_total + inv_scale * (
                grad_unit - unit_full * jnp.sum(grad_unit * unit_full, axis=-1, keepdims=True)
            )
        doc_grad_ref[...] = doc_total


def interaction_logits(levels, span, docs, member, queries):
    tokens, width = queries.shape
    row_len, slots = member.shape
    rows = block_queries * span
    return pl.pallas_call(
        partial(interact_forward, levels, span),
        grid=(tokens // rows,),
        out_shape=(
            jax.ShapeDtypeStruct((3, tokens // span, slots), f32),
            jax.ShapeDtypeStruct((3, tokens, slots), f32),
        ),
        in_specs=[
            pl.BlockSpec((row_len, width), lambda i: (0, 0)),
            pl.BlockSpec((row_len, slots), lambda i: (0, 0)),
            pl.BlockSpec((rows, width), lambda i: (i, 0)),
        ],
        out_specs=(
            pl.BlockSpec((3, block_queries, slots), lambda i: (0, i, 0)),
            pl.BlockSpec((3, rows, slots), lambda i: (0, i, 0)),
        ),
        scratch_shapes=[pltpu.VMEM((3, row_len, width), bf16)],
        compiler_params=pltpu.CompilerParams(vmem_limit_bytes=40 << 20),
    )(docs, member, queries)


def interaction_grads(levels, span, docs, member_t, queries, sums, grads):
    tokens, width = queries.shape
    slots, row_len = member_t.shape
    rows = block_queries * span
    return pl.pallas_call(
        partial(interact_backward, levels, span),
        grid=(tokens // rows,),
        out_shape=(
            jax.ShapeDtypeStruct((tokens, width), f32),
            jax.ShapeDtypeStruct((row_len, width), f32),
        ),
        in_specs=[
            pl.BlockSpec((row_len, width), lambda i: (0, 0)),
            pl.BlockSpec((slots, row_len), lambda i: (0, 0)),
            pl.BlockSpec((rows, width), lambda i: (i, 0)),
            pl.BlockSpec((3, rows, slots), lambda i: (0, i, 0)),
            pl.BlockSpec((3, block_queries, slots), lambda i: (0, i, 0)),
        ],
        out_specs=(
            pl.BlockSpec((rows, width), lambda i: (i, 0)),
            pl.BlockSpec((row_len, width), lambda i: (0, 0)),
        ),
        scratch_shapes=[
            pltpu.VMEM((3, row_len, width), bf16),
            pltpu.VMEM((3, row_len, width), f32),
        ],
        compiler_params=pltpu.CompilerParams(vmem_limit_bytes=40 << 20),
    )(docs, member_t, queries, sums, grads)


def after(value, *earlier):
    return lax.optimization_barrier((value, *earlier))[0]


def exchange(dp, fsdp, scatter, add, mine_ref, out_ref, held, send_sem, recv_sem):
    count = dp * fsdp
    me = lax.axis_index("dp") * fsdp + lax.axis_index("fsdp")

    def device(other):
        return (other // fsdp, other % fsdp)

    def copy(step, other, place):
        return pltpu.make_async_remote_copy(
            src_ref=mine_ref.at[other] if scatter else mine_ref,
            dst_ref=held.at[place],
            send_sem=send_sem.at[step],
            recv_sem=recv_sem.at[step],
            device_id=device(other),
            device_id_type=pl.DeviceIdType.MESH,
        )

    barrier = pltpu.get_barrier_semaphore()

    @pl.loop(1, count)
    def _(step):
        pl.semaphore_signal(
            barrier, inc=1, device_id=device((me + step) % count),
            device_id_type=pl.DeviceIdType.MESH,
        )

    pl.semaphore_wait(barrier, count - 1)

    @pl.loop(1, count)
    def _(step):
        copy(step, (me + step) % count, me).start()

    held[me] = mine_ref[me] if scatter else mine_ref[...]

    @pl.loop(1, count)
    def _(step):
        arriving = copy(step, (me + step) % count, (me + count - step) % count)
        arriving.wait_send()
        arriving.wait_recv()

    if add:
        out_ref[...] = jnp.sum(held[...].astype(f32), axis=0)
    else:
        out_ref[...] = held[...]


def exchanged(links, value, scatter, add, name):
    block = value.shape[1:] if scatter else value.shape
    whole = (links.count,) + block
    return pl.pallas_call(
        partial(exchange, links.dp, links.fsdp, scatter, add),
        out_shape=jax.ShapeDtypeStruct(block if add else whole, f32 if add else value.dtype),
        in_specs=[pl.BlockSpec(memory_space=pltpu.VMEM)],
        out_specs=pl.BlockSpec(memory_space=pltpu.VMEM),
        scratch_shapes=[
            pltpu.VMEM(whole, value.dtype),
            pltpu.SemaphoreType.DMA((links.count,)),
            pltpu.SemaphoreType.DMA((links.count,)),
        ],
        compiler_params=pltpu.CompilerParams(collective_id=name, has_side_effects=True),
    )(value)


class Growing:
    def __init__(self, links, shard, lane):
        self.links, self.order, self.block = links, list(links.orders[lane]), shard.shape
        self.held = shard.reshape((1,) * links.bits + shard.shape)

    def wait(self, *earlier):
        self.held = after(self.held, *earlier)

    def launch(self):
        self.place = self.order.pop(0)
        self.before = self.held
        self.arrived = self.links.swap(self.held, 1 << self.place)

    def merge(self, *earlier):
        axis = self.links.bits - 1 - self.place
        mine = self.links.side(self.place)
        held = self.held
        arrived = after(self.arrived, *earlier) if earlier else self.arrived
        shape = held.shape[:axis] + (2,) + held.shape[axis + 1 :]
        own = lax.broadcasted_iota(jnp.int32, shape, axis) == mine
        self.held = lax.optimization_barrier(jnp.where(own, held, arrived))

    def full(self):
        while self.order:
            self.launch()
            self.merge()
        return self.held.reshape((self.links.count,) + self.block)


class Shrinking:
    def __init__(self, links, blocks, lane, wire):
        self.links, self.order, self.block = links, list(links.orders[lane]), blocks.shape[1:]
        self.wire = wire
        self.held = blocks.astype(wire).reshape((2,) * links.bits + self.block)

    def wait(self, *earlier):
        self.held = after(self.held, *earlier)

    def launch(self):
        if not self.order:
            return
        self.place = self.order.pop()
        axis = self.links.bits - 1 - self.place
        self.leaving = lax.dynamic_slice_in_dim(
            self.held, 1 - self.links.side(self.place), 1, axis
        )
        self.arrived = self.links.swap(self.leaving, 1 << self.place)

    def merge(self, *earlier):
        if self.arrived is None:
            return
        axis = self.links.bits - 1 - self.place
        kept = lax.dynamic_slice_in_dim(self.held, self.links.side(self.place), 1, axis)
        arrived = after(self.arrived, *earlier) if earlier else self.arrived
        total = kept.astype(f32) + arrived.astype(f32)
        self.held = total.astype(self.wire) if self.order else total
        self.arrived = None

    def mine(self):
        while self.order:
            self.launch()
            self.merge()
        return self.held.reshape(self.block)


class Links:
    def __init__(self, dp, fsdp):
        self.dp, self.fsdp, self.count = dp, fsdp, dp * fsdp
        self.bits = self.count.bit_length() - 1
        inner_bits = fsdp.bit_length() - 1
        low, high = list(range(inner_bits)), list(range(inner_bits, self.bits))
        inner, rest = low[:1], low[1:]
        near, far = high[:1], high[1:][::-1]
        self.orders = (far + rest[::-1] + near + inner, far + near + rest[::-1] + inner)

    def side(self, place):
        return (lax.axis_index(AXES) >> place) & 1

    def swap(self, value, bit):
        return lax.ppermute(value, AXES, [(d, d ^ bit) for d in range(self.count)])

    def growing(self, shard, lane=0):
        return Growing(self, shard, lane)

    def shrinking(self, blocks, lane=0, wire=bf16):
        return Shrinking(self, blocks, lane, wire)

    def total(self, value):
        high, wide = value.shape
        padded = jnp.pad(value, ((0, -high % 8), (0, -wide % 128)))
        return exchanged(self, padded, False, True, 0)[:high, :wide]

    def everyone(self, value):
        return exchanged(self, value, False, False, 1)

    def owners_sum(self, blocks):
        return exchanged(self, blocks.astype(bf16), True, True, 2)


class Whole:
    def __init__(self, value):
        self.held = self.before = self.leaving = value

    def wait(self, *earlier):
        pass

    def launch(self):
        pass

    def merge(self, *earlier):
        pass

    def full(self):
        return self.held

    def mine(self):
        return self.held


class PlainLinks(Links):
    def growing(self, shard, lane=0):
        return Whole(lax.all_gather(shard, AXES, axis=0))

    def shrinking(self, blocks, lane=0, wire=bf16):
        return Whole(lax.psum_scatter(blocks, AXES, scatter_dimension=0, tiled=False))

    def total(self, value):
        return lax.psum(value, AXES)

    def everyone(self, value):
        return lax.all_gather(value, AXES, axis=0)

    def owners_sum(self, blocks):
        return lax.psum_scatter(blocks, AXES, scatter_dimension=0, tiled=False)


def make_links(mesh):
    dp, fsdp = mesh.shape["dp"], mesh.shape["fsdp"]
    paired = (dp & (dp - 1)) == 0 and (fsdp & (fsdp - 1)) == 0 and dp * fsdp <= 64
    return (Links if paired else PlainLinks)(dp, fsdp)


def tables(lengths, row_len):
    ends = jnp.cumsum(lengths)
    starts = ends - lengths
    places = jnp.arange(row_len, dtype=jnp.int32)
    segment = jnp.sum((places[:, None] >= ends[None, :]).astype(jnp.int32), axis=1)
    rows = segment.reshape(row_len // q_rows, q_rows)
    ids = jnp.arange(lengths.shape[0])
    low = jnp.sum(jnp.where(rows[:, :1] == ids[None, :], starts[None, :], 0), axis=1)
    high = jnp.sum(jnp.where(rows[:, -1:] == ids[None, :], ends[None, :], 0), axis=1)
    bounds = jnp.stack([low // k_rows, (high + k_rows - 1) // k_rows]).astype(jnp.int32)
    return segment, jnp.concatenate([rows, rows], axis=1), segment[:, None], bounds


def body(
    links,
    doc_hidden,
    query_hidden,
    w_query,
    w_key,
    w_value,
    w_out,
    w_up,
    w_down,
    w_proj,
    biases,
    gains,
    up_bias,
    seg_lengths,
    positives,
):
    count = links.count
    row_len = doc_hidden.shape[1]
    model_width = doc_hidden.shape[2]
    query_count = query_hidden.shape[0]
    span = query_hidden.shape[1]
    doc_slots = seg_lengths.shape[1] - 1
    proj_width = w_proj.shape[1]
    ff = up_bias.shape[0] * count
    shard_cols = biases.shape[1]
    shard_rows = w_query.shape[0]
    part = model_width // 2
    small = jnp.concatenate(
        [biases.reshape(-1), gains.reshape(-1), up_bias.reshape(-1)], axis=0
    )[None]

    def rows_of(full):
        return full.reshape(full.shape[0] * full.shape[1], full.shape[2])

    sides = []
    for side in range(2):
        cut = slice(side * part, (side + 1) * part)
        shard = jnp.concatenate([w_query[:, cut], w_key[:, cut], w_value[:, cut]], axis=1)
        sides.append(links.growing(shard, side))
    small_part = links.growing(small, 0)
    out_part = links.growing(jnp.concatenate([w_out, w_proj], axis=1), 0)
    up_part = links.growing(w_up, 0)
    down_part = links.growing(w_down, 1)
    near = (out_part, up_part)
    for hop in range(5):
        for one in sides:
            one.launch()
        if hop > 0:
            small_part.wait(sides[0].before, sides[1].before)
        small_part.launch()
        for one in sides:
            one.merge()
        first = (sides[0].held, sides[1].held)
        small_part.merge(*first)
        for one in near:
            if hop == 0:
                one.wait(*first)
            elif hop < 4:
                one.merge(*first)
            if hop < 4:
                one.launch()
        if hop == 1:
            down_part.wait(*first)
        elif hop == 2 or hop == 3:
            down_part.merge(*first)
        if hop > 0 and hop < 4:
            down_part.launch()
    small_full = small_part.full().reshape(count, -1)
    full_qkv = [rows_of(one.full()) for one in sides]
    full_biases = (
        small_full[:, : 6 * shard_cols]
        .reshape(count, 6, shard_cols)
        .transpose(1, 0, 2)
        .reshape(6, model_width)
        .astype(f32)
    )
    full_gains = (
        small_full[:, 6 * shard_cols : 8 * shard_cols]
        .reshape(count, 2, shard_cols)
        .transpose(1, 0, 2)
        .reshape(2, model_width)
        .astype(f32)
    )
    full_upbias = small_full[:, 8 * shard_cols :].reshape(ff).astype(f32)

    tokens = jnp.concatenate(
        [doc_hidden[0], query_hidden.reshape(query_count * span, model_width)], axis=0
    )
    segment, segrow, segcol, bounds = tables(seg_lengths[0], row_len)
    slot_ids = jnp.arange(doc_slots, dtype=jnp.int32)
    member = (segment[:, None] == slot_ids[None, :]).astype(f32)
    member_t = (slot_ids[:, None] == segment[None, :]).astype(f32)
    zero_row = jnp.zeros((part,), f32)
    qkv, contexts, saved = [], [], []
    for side in range(2):
        cut = slice(side * part, (side + 1) * part)
        bias = jnp.concatenate([full_biases[0, cut], zero_row, full_biases[1, cut]])
        qkv.append((matmul_plain(tokens, full_qkv[side]) + bias).astype(bf16))
    for side in range(2):
        qkv[side] = after(qkv[side], (up_part, down_part)[side].before)
        context, lse, query_lse = attention_forward(
            qkv[side], segrow, segcol, bounds, row_len, span
        )
        if side == 0:
            for one in (out_part, down_part):
                one.merge(context)
                one.launch()
        contexts.append(context)
        saved.append((lse, query_lse))
    up_part.merge(*contexts)
    up_part.launch()
    contexts[1] = after(contexts[1], up_part.before)
    out_part.merge()
    out_proj = rows_of(out_part.full())
    full_out, full_proj = out_proj[:, :model_width], out_proj[:, model_width:]
    up_part.merge()
    full_up = rows_of(up_part.full())
    attn_out = (
        matmul_plain(contexts[0], full_out[:part])
        + matmul_plain(contexts[1], full_out[part:])
        + full_biases[2]
    )
    first_out, first_normed, first_scale = layer_norm_parts(
        tokens.astype(f32) + attn_out, full_gains[0], full_biases[3]
    )
    first_low = first_out.astype(bf16)
    down_part.merge(first_low)
    down_part.launch()
    first_low = after(first_low, down_part.before)
    up_pre = matmul_plain(first_low, full_up) + full_upbias
    share = 0.5 * (1.0 + lax.erf(up_pre * root_half))
    gelu_out = (up_pre * share).astype(bf16)
    density = jnp.exp(-0.5 * up_pre * up_pre) * density_peak
    slope = (share + up_pre * density).astype(bf16)
    gelu_out, slope = lax.optimization_barrier((gelu_out, slope))
    down_part.merge()
    full_down = rows_of(down_part.full())
    ffn_out = matmul_plain(gelu_out, full_down) + full_biases[4]
    second_out, second_normed, second_scale = layer_norm_parts(
        first_out + ffn_out, full_gains[1], full_biases[5]
    )
    second_low = second_out.astype(bf16)
    vectors = matmul_plain(second_low, full_proj).astype(bf16)
    doc_vectors = vectors[:row_len]
    query_vectors = vectors[row_len:].reshape(query_count * span, proj_width)
    every_query = links.everyone(query_vectors).reshape(count * query_count * span, proj_width)
    query_total = count * query_count
    levels = (proj_width, proj_width * 3 // 4, proj_width // 2)
    logits, doc_sums = interaction_logits(levels, span, doc_vectors, member.astype(bf16), every_query)
    logits = logits.transpose(1, 0, 2)
    powers = jnp.exp(logits)
    local_sum = jnp.sum(powers, axis=-1)
    my_row = lax.axis_index(AXES)
    chosen = ((positives - my_row * doc_slots)[:, None] == slot_ids[None, :]).astype(f32)
    local_pick = jnp.sum(logits * chosen[:, None, :], axis=-1)
    both = links.total(jnp.concatenate([local_sum, local_pick], axis=1).T).T
    all_sums, picked = both[:, :3], both[:, 3:]
    loss = jnp.sum(jnp.log(all_sums) - picked) / query_total
    score_derivative = (powers / all_sums[:, :, None] - chosen[:, None, :]) / query_total
    peak_match_derivative = score_derivative / (span * sharpness_divisor)

    query_terms, doc_vec_grad = interaction_grads(
        levels, span, doc_vectors, member_t.astype(bf16), every_query, doc_sums,
        peak_match_derivative.transpose(1, 0, 2),
    )
    query_terms = query_terms.reshape(count, query_count * span, proj_width)
    query_vec_grad = links.owners_sum(query_terms)
    grad_vectors = jnp.concatenate([doc_vec_grad, query_vec_grad], axis=0).astype(bf16)

    def spread_rows_of(full):
        return full.reshape(count, full.shape[0] // count, full.shape[1])

    proj_grad = matmul_left_t(second_low, grad_vectors)
    grad_second = matmul_right_t(grad_vectors, full_proj)
    grad_mid, gain_two, bias_two = layer_norm_back(
        grad_second, second_normed, second_scale, full_gains[1]
    )
    grad_ffn = grad_mid.astype(bf16)
    down_grad = matmul_left_t(gelu_out, grad_ffn)
    down_sum = links.shrinking(spread_rows_of(down_grad), 1)
    down_sum.launch()
    down_bias = jnp.sum(grad_ffn, axis=0, dtype=f32)
    grad_gelu = matmul_right_t(after(grad_ffn, down_sum.leaving), full_down)
    grad_up = (grad_gelu * slope.astype(f32)).astype(bf16)
    upbias_grad = jnp.sum(grad_up, axis=0, dtype=f32)
    up_grad = matmul_left_t(first_low, grad_up)
    up_sum = links.shrinking(spread_rows_of(up_grad), 0)
    up_sum.launch()
    down_sum.merge(up_sum.leaving)
    down_sum.launch()
    grad_first = grad_mid + matmul_right_t(after(grad_up, down_sum.leaving), full_up)
    grad_res, gain_one, bias_one = layer_norm_back(
        grad_first, first_normed, first_scale, full_gains[0]
    )
    up_sum.merge(grad_res)
    up_sum.launch()
    grad_attn = after(grad_res.astype(bf16), up_sum.leaving)
    out_bias = jnp.sum(grad_attn, axis=0, dtype=f32)
    out_grad = jnp.concatenate([matmul_left_t(c, grad_attn) for c in contexts], axis=0)
    out_sum = links.shrinking(spread_rows_of(jnp.concatenate([out_grad, proj_grad], axis=1)), 0)
    out_sum.launch()
    input_grad = grad_res
    query_bias, value_bias, qkv_sums = [], [], []
    grad_contexts = [
        matmul_right_t(grad_attn, full_out[side * part : (side + 1) * part]).astype(bf16)
        for side in range(2)
    ]
    down_sum.merge(*grad_contexts)
    down_sum.launch()
    earlier = (out_sum.leaving, down_sum.leaving)
    for side in range(2):
        grad_qkv = attention_backward(
            qkv[side], after(grad_contexts[side], *earlier), contexts[side], *saved[side], segrow,
            segcol, bounds, row_len, span,
        )
        if side == 1:
            up_sum.merge(grad_qkv)
            up_sum.launch()
            down_sum.merge(grad_qkv)
            down_sum.launch()
            qkv_sums[0].merge(grad_qkv)
            qkv_sums[0].launch()
            grad_qkv = after(grad_qkv, up_sum.leaving, down_sum.leaving, qkv_sums[0].leaving)
        query_bias.append(jnp.sum(grad_qkv[:, :part], axis=0, dtype=f32))
        value_bias.append(jnp.sum(grad_qkv[:, 2 * part :], axis=0, dtype=f32))
        qkv_grad = matmul_left_t(tokens, grad_qkv)
        if side == 0:
            qkv_sums.append(links.shrinking(spread_rows_of(qkv_grad), side))
        else:
            wide = qkv_grad.shape[1] // 2
            for lane in range(2):
                piece = qkv_grad[:, lane * wide : (lane + 1) * wide]
                qkv_sums.append(links.shrinking(spread_rows_of(piece), lane))
        for one in qkv_sums[side:]:
            one.launch()
        if side == 0:
            out_sum.merge(qkv_sums[0].leaving)
            out_sum.launch()
            up_sum.merge(qkv_sums[0].leaving)
            up_sum.launch()
            earlier = (qkv_sums[0].leaving, out_sum.leaving, up_sum.leaving)
        grad_qkv = after(grad_qkv, *[one.leaving for one in qkv_sums[side:]])
        input_grad = input_grad + matmul_right_t(grad_qkv, full_qkv[side])
    bias_grads = jnp.stack(
        [
            jnp.concatenate(query_bias),
            jnp.concatenate(value_bias),
            out_bias,
            bias_one,
            down_bias,
            bias_two,
            gain_one,
            gain_two,
        ],
        axis=0,
    )
    small_grads = jnp.concatenate(
        [
            bias_grads.reshape(8, count, shard_cols).transpose(1, 0, 2).reshape(count, -1),
            upbias_grad.reshape(count, -1),
        ],
        axis=1,
    )
    small_sum = links.shrinking(small_grads[:, None, :], 0, wire=f32)
    small_sum.launch()
    first, others, slow = qkv_sums[1:], [small_sum, qkv_sums[0], out_sum], [up_sum, down_sum]
    last = [one.leaving for one in first]
    for hop in range(links.bits):
        for one in first:
            one.merge()
        for one in others:
            one.merge(*last)
        for one in first + others:
            one.launch()
        last = [one.held for one in first]
        if hop == 0 or hop == 3:
            for one in slow:
                one.merge(*last)
                one.launch()
        last = [one.leaving for one in first]
    down_shard, up_shard, out_proj_shard = down_sum.mine(), up_sum.mine(), out_sum.mine()
    qkv_shards = [one.mine() for one in qkv_sums]
    qkv_shards = [qkv_shards[0], jnp.concatenate(qkv_shards[1:], axis=-1)]
    small_shard = small_sum.mine()[0]
    shards = [
        jnp.concatenate([s[:, i * part : (i + 1) * part] for s in qkv_shards], axis=1)
        for i in range(3)
    ]
    return (
        loss,
        input_grad[:row_len].reshape(1, row_len, model_width),
        input_grad[row_len:].reshape(query_count, span, model_width),
        shards[0],
        shards[1],
        shards[2],
        out_proj_shard[:, :model_width],
        up_shard,
        down_shard,
        out_proj_shard[:, model_width:],
        small_shard[: 6 * shard_cols].reshape(6, shard_cols),
        small_shard[6 * shard_cols : 8 * shard_cols].reshape(2, shard_cols),
        small_shard[8 * shard_cols :],
    )


def solution(mesh):
    return jax.shard_map(
        partial(body, make_links(mesh)),
        mesh=mesh,
        in_specs=(
            P(("dp", "fsdp"), None, None),
            P(("dp", "fsdp"), None, None),
            P(("dp", "fsdp"), None),
            P(("dp", "fsdp"), None),
            P(("dp", "fsdp"), None),
            P(("dp", "fsdp"), None),
            P(("dp", "fsdp"), None),
            P(("dp", "fsdp"), None),
            P(("dp", "fsdp"), None),
            P(None, ("dp", "fsdp")),
            P(None, ("dp", "fsdp")),
            P(("dp", "fsdp")),
            P(("dp", "fsdp"), None),
            P(),
        ),
        out_specs=(
            P(),
            P(("dp", "fsdp"), None, None),
            P(("dp", "fsdp"), None, None),
            P(("dp", "fsdp"), None),
            P(("dp", "fsdp"), None),
            P(("dp", "fsdp"), None),
            P(("dp", "fsdp"), None),
            P(("dp", "fsdp"), None),
            P(("dp", "fsdp"), None),
            P(("dp", "fsdp"), None),
            P(None, ("dp", "fsdp")),
            P(None, ("dp", "fsdp")),
            P(("dp", "fsdp")),
        ),
        check_vma=False,
    )
```

```python
from functools import partial

import jax
import jax.numpy as jnp
from jax import lax
from jax.experimental import pallas as pl
from jax.experimental.pallas import tpu as pltpu
from jax.sharding import PartitionSpec as P

softness = 0.1
sharpness_divisor = 0.2
norm_eps = 1e-05
unit_eps = 1e-06
root_half = 0.7071067811865476
density_peak = 0.3989422804014327
head_width = 64
block_queries = 8
masked_score = -1e30
rate = 0.125 * 1.4426950408889634
q_rows = 256
k_rows = 256
f32 = jnp.float32
bf16 = jnp.bfloat16
AXES = ("dp", "fsdp")

def matmul_plain(left, right):
    return jnp.dot(left, right, preferred_element_type=jnp.float32)


def matmul_right_t(left, right):
    return lax.dot_general(
        left, right, (((1,), (1,)), ((), ())), preferred_element_type=jnp.float32
    )


def matmul_left_t(left, right):
    return lax.dot_general(
        left, right, (((0,), (0,)), ((), ())), preferred_element_type=jnp.float32
    )


def layer_norm_parts(values, gain_row, bias_row):
    center = values - jnp.mean(values, axis=-1, keepdims=True)
    spread = jnp.mean(center * center, axis=-1, keepdims=True)
    inv_scale = lax.rsqrt(spread + norm_eps)
    normed = center * inv_scale
    return (normed * gain_row + bias_row, normed, inv_scale)


def layer_norm_back(grad_out, normed, inv_scale, gain_row):
    grad_norm = grad_out * gain_row
    mean_grad = jnp.mean(grad_norm, axis=-1, keepdims=True)
    mean_proj = jnp.mean(grad_norm * normed, axis=-1, keepdims=True)
    grad_in = inv_scale * (grad_norm - mean_grad - normed * mean_proj)
    return (grad_in, jnp.sum(grad_out * normed, axis=0), jnp.sum(grad_out, axis=0))


def dot_nt(a,b): return lax.dot_general(a,b,(((1,),(1,)),((),())),preferred_element_type=f32)
def dot_nn(a,b): return jnp.dot(a,b,preferred_element_type=f32)

def stack_heads(block, first):
    zero=jnp.zeros_like(block)
    return jnp.concatenate([jnp.where(first,block,zero),jnp.where(first,zero,block)],axis=0)

def attend_forward(row_len, qb, kb, lanes, span, bounds, segrow, segcol, q_ref,k_ref,v_ref,ctx_ref,lse_ref,qlse_ref,vt_ref):
    units=lanes//128
    tokens=q_ref.shape[0]
    first_q=lax.broadcasted_iota(jnp.int32,(qb,128),1)<64
    top=lax.broadcasted_iota(jnp.int32,(128,qb),0)<64
    vt_ref[...]=v_ref[...].T
    def q_step(i,_):
        rows=pl.ds(pl.multiple_of(i*qb,qb),qb)
        own=segrow[pl.ds(i,1),:]
        stacked=[stack_heads(q_ref[rows,pl.ds(u*128,128)],first_q) for u in range(units)]
        def k_step(j,carry):
            keys=pl.ds(pl.multiple_of(j*kb,kb),kb)
            allowed=segcol[keys,:]==own
            out=[]
            for u in range(units):
                peak,total,acc=carry[u]
                s=jnp.where(allowed,dot_nt(k_ref[keys,pl.ds(u*128,128)],stacked[u]),masked_score)
                new=jnp.maximum(peak,jnp.max(s,axis=0,keepdims=True))
                p=jnp.exp2((s-new)*rate)
                fade=jnp.exp2((peak-new)*rate)
                total=total*fade+jnp.sum(p,axis=0,keepdims=True)
                acc=acc*fade+dot_nn(vt_ref[pl.ds(u*128,128),keys],p.astype(bf16))
                out.append((new,total,acc))
            return tuple(out)
        start=tuple((jnp.full((1,2*qb),masked_score,f32),jnp.zeros((1,2*qb),f32),jnp.zeros((128,2*qb),f32)) for u in range(units))
        res=lax.fori_loop(bounds[0,i],bounds[1,i],k_step,start)
        for u in range(units):
            peak,total,acc=res[u]
            acc=acc/total
            o=jnp.where(top,acc[:,:qb],acc[:,qb:])
            ctx_ref[rows,pl.ds(u*128,128)]=o.T.astype(bf16)
            lse_ref[u,pl.ds(i,1),:]=peak*rate+jnp.log2(total)
        return 0
    lax.fori_loop(0,row_len//qb,q_step,0)
    nq=tokens-row_len
    firstn=lax.broadcasted_iota(jnp.int32,(nq,128),1)<64
    own=lax.broadcasted_iota(jnp.int32,(nq,2*nq),0)//span
    other=(lax.broadcasted_iota(jnp.int32,(nq,2*nq),1)%nq)//span
    keep=own==other
    for u in range(units):
        cols=pl.ds(u*128,128)
        st=stack_heads(q_ref[row_len:,cols],firstn)
        s=jnp.where(keep,dot_nt(k_ref[row_len:,cols],st),masked_score)
        peak=jnp.max(s,axis=0,keepdims=True)
        p=jnp.exp2((s-peak)*rate)
        total=jnp.sum(p,axis=0,keepdims=True)
        p=(p/total).astype(bf16)
        acc=lax.dot_general(p,v_ref[row_len:,cols],(((0,),(0,)),((),())),preferred_element_type=f32)
        ctx_ref[row_len:,cols]=jnp.where(firstn,acc[:nq],acc[nq:]).astype(bf16)
        qlse_ref[u,:,:]=peak*rate+jnp.log2(total)

def attention_forward(qkv,segrow,segcol,bounds,row_len,span):
    tokens=qkv.shape[0]
    width=qkv.shape[1]//3
    qb,kb,lanes=q_rows,k_rows,width
    nq=tokens-row_len
    steps=width//lanes
    def spec(off): return pl.BlockSpec((tokens,lanes),lambda p,*_:(0,p+off))
    full=lambda a: pl.BlockSpec(a.shape,lambda p,*_:(0,)*a.ndim)
    return pl.pallas_call(
        partial(attend_forward,row_len,qb,kb,lanes,span),
        out_shape=(jax.ShapeDtypeStruct((tokens,width),bf16),jax.ShapeDtypeStruct((width//128,row_len//qb,2*qb),f32),jax.ShapeDtypeStruct((width//128,1,2*nq),f32)),
        grid_spec=pltpu.PrefetchScalarGridSpec(num_scalar_prefetch=1,grid=(steps,),
            in_specs=[full(segrow),full(segcol),spec(0),spec(steps),spec(2*steps)],
            out_specs=[pl.BlockSpec((tokens,lanes),lambda p,*_:(0,p)),pl.BlockSpec((lanes//128,row_len//qb,2*qb),lambda p,*_:(p,0,0)),pl.BlockSpec((lanes//128,1,2*nq),lambda p,*_:(p,0,0))],
            scratch_shapes=[pltpu.VMEM((lanes,tokens),bf16)]),
        compiler_params=pltpu.CompilerParams(vmem_limit_bytes=48<<20),
    )(bounds,segrow,segcol,qkv,qkv,qkv)

def attend_backward(row_len, qb, kb, lanes, span, bounds, segrow, segcol, q_ref,k_ref,v_ref,g_ref,o_ref,lse_ref,qlse_ref,out_ref,kt_ref,dka,dva):
    dq_ref=out_ref.at[:,:lanes]; dk_ref=out_ref.at[:,lanes:2*lanes]; dv_ref=out_ref.at[:,2*lanes:]
    units=lanes//128
    tokens=q_ref.shape[0]
    first_q=lax.broadcasted_iota(jnp.int32,(qb,128),1)<64
    top=lax.broadcasted_iota(jnp.int32,(128,qb),0)<64
    kt_ref[...]=k_ref[...].T
    dka[...]=jnp.zeros_like(dka); dva[...]=jnp.zeros_like(dva)
    def q_step(i,_):
        rows=pl.ds(pl.multiple_of(i*qb,qb),qb)
        own=segrow[pl.ds(i,1),:]
        sq=[];sg=[];dr=[];ls=[]
        for u in range(units):
            cols=pl.ds(u*128,128)
            g=g_ref[rows,cols]
            sq.append(stack_heads(q_ref[rows,cols],first_q)); sg.append(stack_heads(g,first_q))
            t=(g.astype(f32)*o_ref[rows,cols].astype(f32)).T
            dr.append(jnp.concatenate([jnp.sum(t[:64],axis=0,keepdims=True),jnp.sum(t[64:],axis=0,keepdims=True)],axis=1))
            ls.append(lse_ref[u,pl.ds(i,1),:])
        def k_step(j,carry):
            keys=pl.ds(pl.multiple_of(j*kb,kb),kb)
            allowed=segcol[keys,:]==own
            out=[]
            for u in range(units):
                cols=pl.ds(u*128,128)
                s=jnp.where(allowed,dot_nt(k_ref[keys,cols],sq[u]),masked_score)
                p=jnp.exp2(s*rate-ls[u])
                dp=dot_nt(v_ref[keys,cols],sg[u])
                ds=(p*(dp-dr[u])).astype(bf16)
                dva[keys,cols]+=dot_nn(p.astype(bf16),sg[u])
                dka[keys,cols]+=dot_nn(ds,sq[u])
                out.append(carry[u]+dot_nn(kt_ref[cols,keys],ds))
            return tuple(out)
        res=lax.fori_loop(bounds[0,i],bounds[1,i],k_step,tuple(jnp.zeros((128,2*qb),f32) for u in range(units)))
        for u in range(units):
            d=jnp.where(top,res[u][:,:qb],res[u][:,qb:])*0.125
            dq_ref[rows,pl.ds(u*128,128)]=d.T.astype(bf16)
        return 0
    lax.fori_loop(0,row_len//qb,q_step,0)
    dk_ref[:row_len,:]=(dka[...]*0.125).astype(bf16)
    dv_ref[:row_len,:]=dva[...].astype(bf16)
    nq=tokens-row_len
    firstn=lax.broadcasted_iota(jnp.int32,(nq,128),1)<64
    own=lax.broadcasted_iota(jnp.int32,(nq,2*nq),0)//span
    other=(lax.broadcasted_iota(jnp.int32,(nq,2*nq),1)%nq)//span
    keep=own==other
    for u in range(units):
        cols=pl.ds(u*128,128)
        q=q_ref[row_len:,cols]; k=k_ref[row_len:,cols]; v=v_ref[row_len:,cols]; g=g_ref[row_len:,cols]
        st=stack_heads(q,firstn); sg=stack_heads(g,firstn)
        s=jnp.where(keep,dot_nt(k,st),masked_score)
        p=jnp.exp2(s*rate-qlse_ref[u])
        dp=dot_nt(v,sg)
        ds=(p*(dp-jnp.sum(p*dp,axis=0,keepdims=True))).astype(bf16)
        dv_ref[row_len:,cols]=dot_nn(p.astype(bf16),sg).astype(bf16)
        dk_ref[row_len:,cols]=(dot_nn(ds,st)*0.125).astype(bf16)
        d=lax.dot_general(ds,k,(((0,),(0,)),((),())),preferred_element_type=f32)
        dq_ref[row_len:,cols]=(jnp.where(firstn,d[:nq],d[nq:])*0.125).astype(bf16)

def attention_backward(qkv,g,o,lse,qlse,segrow,segcol,bounds,row_len,span):
    tokens,width=g.shape
    qb,kb,lanes=q_rows,k_rows,width
    nq=tokens-row_len
    steps=width//lanes
    def spec(off): return pl.BlockSpec((tokens,lanes),lambda p,*_:(0,p+off))
    full=lambda a: pl.BlockSpec(a.shape,lambda p,*_:(0,)*a.ndim)
    sd=jax.ShapeDtypeStruct((tokens,3*width),bf16)
    return pl.pallas_call(
        partial(attend_backward,row_len,qb,kb,lanes,span),
        out_shape=sd,
        grid_spec=pltpu.PrefetchScalarGridSpec(num_scalar_prefetch=1,grid=(steps,),
            in_specs=[full(segrow),full(segcol)]+[spec(0),spec(1),spec(2),spec(0),spec(0)]+[pl.BlockSpec((lanes//128,row_len//qb,2*qb),lambda p,*_:(p,0,0)),pl.BlockSpec((lanes//128,1,2*nq),lambda p,*_:(p,0,0))],
            out_specs=pl.BlockSpec((tokens,3*lanes),lambda p,*_:(0,0)),
            scratch_shapes=[pltpu.VMEM((lanes,tokens),bf16),pltpu.VMEM((row_len,lanes),f32),pltpu.VMEM((row_len,lanes),f32)]),
        compiler_params=pltpu.CompilerParams(vmem_limit_bytes=56<<20),
    )(bounds,segrow,segcol,qkv,qkv,qkv,g,o,lse,qlse)


def level_units(values, width):
    lanes = lax.broadcasted_iota(jnp.int32, values.shape, 1)
    part_cols = jnp.where(lanes < width, values, 0.0)
    inv_scale = lax.rsqrt(jnp.sum(part_cols * part_cols, axis=-1, keepdims=True) + unit_eps)
    return part_cols * inv_scale, inv_scale


def three_parts(values):
    top = values.astype(bf16)
    rest = values - top.astype(f32)
    middle = rest.astype(bf16)
    return top, middle, (rest - middle.astype(f32)).astype(bf16)


def exact_dot(values, marks):
    return sum(dot_nn(part, marks) for part in three_parts(values))


def keep_doc_units(levels, doc_ref, low_ref):
    @pl.when(pl.program_id(0) == 0)
    def _():
        docs = doc_ref[...].astype(f32)
        for position, width in enumerate(levels):
            low_ref[position] = level_units(docs, width)[0].astype(bf16)


def interact_forward(levels, span, doc_ref, member_ref, query_ref, logit_ref, sums_ref, low_ref):
    keep_doc_units(levels, doc_ref, low_ref)
    queries = query_ref[...].astype(f32)
    member = member_ref[...]
    for position, width in enumerate(levels):
        unit_rows = level_units(queries, width)[0].astype(bf16)
        powers = jnp.exp(dot_nt(unit_rows, low_ref[position]) / softness)
        doc_sums = exact_dot(powers, member)
        sums_ref[position] = doc_sums
        logs = (softness * jnp.log(doc_sums)).reshape(-1, span, doc_sums.shape[1])
        logit_ref[position] = jnp.sum(logs, axis=1) / (span * sharpness_divisor)


def interact_backward(
    levels, span, doc_ref, member_t_ref, query_ref, sums_ref, grad_ref, query_grad_ref,
    doc_grad_ref, low_ref, held_ref,
):
    keep_doc_units(levels, doc_ref, low_ref)

    @pl.when(pl.program_id(0) == 0)
    def _():
        held_ref[...] = jnp.zeros_like(held_ref)

    queries = query_ref[...].astype(f32)
    member_t = member_t_ref[...]
    total = jnp.zeros(queries.shape, f32)
    for position, width in enumerate(levels):
        unit_full, inv_scale = level_units(queries, width)
        unit_rows = unit_full.astype(bf16)
        powers = jnp.exp(dot_nt(unit_rows, low_ref[position]) / softness)
        grads = grad_ref[position]
        rows = jnp.broadcast_to(grads[:, None, :], (grads.shape[0], span, grads.shape[1]))
        rows = rows.reshape(-1, grads.shape[1]) / sums_ref[position]
        grad_scores = (powers * exact_dot(rows, member_t)).astype(bf16)
        grad_unit = dot_nn(grad_scores, low_ref[position])
        held_ref[position] += matmul_left_t(grad_scores, unit_rows)
        total = total + inv_scale * (
            grad_unit - unit_full * jnp.sum(grad_unit * unit_full, axis=-1, keepdims=True)
        )
    query_grad_ref[...] = total

    @pl.when(pl.program_id(0) == pl.num_programs(0) - 1)
    def _():
        docs = doc_ref[...].astype(f32)
        doc_total = jnp.zeros(docs.shape, f32)
        for position, width in enumerate(levels):
            unit_full, inv_scale = level_units(docs, width)
            grad_unit = held_ref[position]
            doc_total = doc_total + inv_scale * (
                grad_unit - unit_full * jnp.sum(grad_unit * unit_full, axis=-1, keepdims=True)
            )
        doc_grad_ref[...] = doc_total


def interaction_logits(levels, span, docs, member, queries):
    tokens, width = queries.shape
    row_len, slots = member.shape
    rows = block_queries * span
    return pl.pallas_call(
        partial(interact_forward, levels, span),
        grid=(tokens // rows,),
        out_shape=(
            jax.ShapeDtypeStruct((3, tokens // span, slots), f32),
            jax.ShapeDtypeStruct((3, tokens, slots), f32),
        ),
        in_specs=[
            pl.BlockSpec((row_len, width), lambda i: (0, 0)),
            pl.BlockSpec((row_len, slots), lambda i: (0, 0)),
            pl.BlockSpec((rows, width), lambda i: (i, 0)),
        ],
        out_specs=(
            pl.BlockSpec((3, block_queries, slots), lambda i: (0, i, 0)),
            pl.BlockSpec((3, rows, slots), lambda i: (0, i, 0)),
        ),
        scratch_shapes=[pltpu.VMEM((3, row_len, width), bf16)],
        compiler_params=pltpu.CompilerParams(vmem_limit_bytes=40 << 20),
    )(docs, member, queries)


def interaction_grads(levels, span, docs, member_t, queries, sums, grads):
    tokens, width = queries.shape
    slots, row_len = member_t.shape
    rows = block_queries * span
    return pl.pallas_call(
        partial(interact_backward, levels, span),
        grid=(tokens // rows,),
        out_shape=(
            jax.ShapeDtypeStruct((tokens, width), f32),
            jax.ShapeDtypeStruct((row_len, width), f32),
        ),
        in_specs=[
            pl.BlockSpec((row_len, width), lambda i: (0, 0)),
            pl.BlockSpec((slots, row_len), lambda i: (0, 0)),
            pl.BlockSpec((rows, width), lambda i: (i, 0)),
            pl.BlockSpec((3, rows, slots), lambda i: (0, i, 0)),
            pl.BlockSpec((3, block_queries, slots), lambda i: (0, i, 0)),
        ],
        out_specs=(
            pl.BlockSpec((rows, width), lambda i: (i, 0)),
            pl.BlockSpec((row_len, width), lambda i: (0, 0)),
        ),
        scratch_shapes=[
            pltpu.VMEM((3, row_len, width), bf16),
            pltpu.VMEM((3, row_len, width), f32),
        ],
        compiler_params=pltpu.CompilerParams(vmem_limit_bytes=40 << 20),
    )(docs, member_t, queries, sums, grads)


def after(value, *earlier):
    return lax.optimization_barrier((value, *earlier))[0]


def exchange(dp, fsdp, scatter, add, mine_ref, out_ref, held, send_sem, recv_sem):
    count = dp * fsdp
    me = lax.axis_index("dp") * fsdp + lax.axis_index("fsdp")

    def device(other):
        return (other // fsdp, other % fsdp)

    def copy(step, other, place):
        return pltpu.make_async_remote_copy(
            src_ref=mine_ref.at[other] if scatter else mine_ref,
            dst_ref=held.at[place],
            send_sem=send_sem.at[step],
            recv_sem=recv_sem.at[step],
            device_id=device(other),
            device_id_type=pl.DeviceIdType.MESH,
        )

    barrier = pltpu.get_barrier_semaphore()

    @pl.loop(1, count)
    def _(step):
        pl.semaphore_signal(
            barrier, inc=1, device_id=device((me + step) % count),
            device_id_type=pl.DeviceIdType.MESH,
        )

    pl.semaphore_wait(barrier, count - 1)

    @pl.loop(1, count)
    def _(step):
        copy(step, (me + step) % count, me).start()

    held[me] = mine_ref[me] if scatter else mine_ref[...]

    @pl.loop(1, count)
    def _(step):
        arriving = copy(step, (me + step) % count, (me + count - step) % count)
        arriving.wait_send()
        arriving.wait_recv()

    if add:
        out_ref[...] = jnp.sum(held[...].astype(f32), axis=0)
    else:
        out_ref[...] = held[...]


def exchanged(links, value, scatter, add, name):
    block = value.shape[1:] if scatter else value.shape
    whole = (links.count,) + block
    return pl.pallas_call(
        partial(exchange, links.dp, links.fsdp, scatter, add),
        out_shape=jax.ShapeDtypeStruct(block if add else whole, f32 if add else value.dtype),
        in_specs=[pl.BlockSpec(memory_space=pltpu.VMEM)],
        out_specs=pl.BlockSpec(memory_space=pltpu.VMEM),
        scratch_shapes=[
            pltpu.VMEM(whole, value.dtype),
            pltpu.SemaphoreType.DMA((links.count,)),
            pltpu.SemaphoreType.DMA((links.count,)),
        ],
        compiler_params=pltpu.CompilerParams(collective_id=name, has_side_effects=True),
    )(value)


class Growing:
    def __init__(self, links, shard, lane):
        self.links, self.order, self.block = links, list(links.orders[lane]), shard.shape
        self.held = shard.reshape((1,) * links.bits + shard.shape)

    def wait(self, *earlier):
        self.held = after(self.held, *earlier)

    def launch(self):
        self.place = self.order.pop(0)
        self.before = self.held
        self.arrived = self.links.swap(self.held, 1 << self.place)

    def merge(self, *earlier):
        axis = self.links.bits - 1 - self.place
        mine = self.links.side(self.place)
        held = self.held
        arrived = after(self.arrived, *earlier) if earlier else self.arrived
        shape = held.shape[:axis] + (2,) + held.shape[axis + 1 :]
        own = lax.broadcasted_iota(jnp.int32, shape, axis) == mine
        self.held = lax.optimization_barrier(jnp.where(own, held, arrived))

    def full(self):
        while self.order:
            self.launch()
            self.merge()
        return self.held.reshape((self.links.count,) + self.block)


class Shrinking:
    def __init__(self, links, blocks, lane, wire):
        self.links, self.order, self.block = links, list(links.orders[lane]), blocks.shape[1:]
        self.wire = wire
        self.held = blocks.astype(wire).reshape((2,) * links.bits + self.block)

    def wait(self, *earlier):
        self.held = after(self.held, *earlier)

    def launch(self):
        if not self.order:
            return
        self.place = self.order.pop()
        axis = self.links.bits - 1 - self.place
        self.leaving = lax.dynamic_slice_in_dim(
            self.held, 1 - self.links.side(self.place), 1, axis
        )
        self.arrived = self.links.swap(self.leaving, 1 << self.place)

    def merge(self, *earlier):
        if self.arrived is None:
            return
        axis = self.links.bits - 1 - self.place
        kept = lax.dynamic_slice_in_dim(self.held, self.links.side(self.place), 1, axis)
        arrived = after(self.arrived, *earlier) if earlier else self.arrived
        total = kept.astype(f32) + arrived.astype(f32)
        self.held = total.astype(self.wire) if self.order else total
        self.arrived = None

    def mine(self):
        while self.order:
            self.launch()
            self.merge()
        return self.held.reshape(self.block)


class Links:
    def __init__(self, dp, fsdp):
        self.dp, self.fsdp, self.count = dp, fsdp, dp * fsdp
        self.bits = self.count.bit_length() - 1
        inner_bits = fsdp.bit_length() - 1
        low, high = list(range(inner_bits)), list(range(inner_bits, self.bits))
        inner, rest = low[:1], low[1:]
        near, far = high[:1], high[1:][::-1]
        self.orders = (far + rest[::-1] + near + inner, far + near + rest[::-1] + inner)

    def side(self, place):
        return (lax.axis_index(AXES) >> place) & 1

    def swap(self, value, bit):
        return lax.ppermute(value, AXES, [(d, d ^ bit) for d in range(self.count)])

    def growing(self, shard, lane=0):
        return Growing(self, shard, lane)

    def shrinking(self, blocks, lane=0, wire=bf16):
        return Shrinking(self, blocks, lane, wire)

    def total(self, value):
        high, wide = value.shape
        padded = jnp.pad(value, ((0, -high % 8), (0, -wide % 128)))
        return exchanged(self, padded, False, True, 0)[:high, :wide]

    def everyone(self, value):
        return exchanged(self, value, False, False, 1)

    def owners_sum(self, blocks):
        return exchanged(self, blocks.astype(bf16), True, True, 2)


class Whole:
    def __init__(self, value):
        self.held = self.before = self.leaving = value

    def wait(self, *earlier):
        pass

    def launch(self):
        pass

    def merge(self, *earlier):
        pass

    def full(self):
        return self.held

    def mine(self):
        return self.held


class PlainLinks(Links):
    def growing(self, shard, lane=0):
        return Whole(lax.all_gather(shard, AXES, axis=0))

    def shrinking(self, blocks, lane=0, wire=bf16):
        return Whole(lax.psum_scatter(blocks, AXES, scatter_dimension=0, tiled=False))

    def total(self, value):
        return lax.psum(value, AXES)

    def everyone(self, value):
        return lax.all_gather(value, AXES, axis=0)

    def owners_sum(self, blocks):
        return lax.psum_scatter(blocks, AXES, scatter_dimension=0, tiled=False)


def make_links(mesh):
    dp, fsdp = mesh.shape["dp"], mesh.shape["fsdp"]
    paired = (dp & (dp - 1)) == 0 and (fsdp & (fsdp - 1)) == 0 and dp * fsdp <= 64
    return (Links if paired else PlainLinks)(dp, fsdp)


def tables(lengths, row_len):
    ends = jnp.cumsum(lengths)
    starts = ends - lengths
    places = jnp.arange(row_len, dtype=jnp.int32)
    segment = jnp.sum((places[:, None] >= ends[None, :]).astype(jnp.int32), axis=1)
    rows = segment.reshape(row_len // q_rows, q_rows)
    ids = jnp.arange(lengths.shape[0])
    low = jnp.sum(jnp.where(rows[:, :1] == ids[None, :], starts[None, :], 0), axis=1)
    high = jnp.sum(jnp.where(rows[:, -1:] == ids[None, :], ends[None, :], 0), axis=1)
    bounds = jnp.stack([low // k_rows, (high + k_rows - 1) // k_rows]).astype(jnp.int32)
    return segment, jnp.concatenate([rows, rows], axis=1), segment[:, None], bounds


def body(
    links,
    doc_hidden,
    query_hidden,
    w_query,
    w_key,
    w_value,
    w_out,
    w_up,
    w_down,
    w_proj,
    biases,
    gains,
    up_bias,
    seg_lengths,
    positives,
):
    count = links.count
    row_len = doc_hidden.shape[1]
    model_width = doc_hidden.shape[2]
    query_count = query_hidden.shape[0]
    span = query_hidden.shape[1]
    doc_slots = seg_lengths.shape[1] - 1
    proj_width = w_proj.shape[1]
    ff = up_bias.shape[0] * count
    shard_cols = biases.shape[1]
    shard_rows = w_query.shape[0]
    part = model_width // 2
    small = jnp.concatenate(
        [biases.reshape(-1), gains.reshape(-1), up_bias.reshape(-1)], axis=0
    )[None]

    def rows_of(full):
        return full.reshape(full.shape[0] * full.shape[1], full.shape[2])

    sides = []
    for side in range(2):
        cut = slice(side * part, (side + 1) * part)
        shard = jnp.concatenate([w_query[:, cut], w_key[:, cut], w_value[:, cut]], axis=1)
        sides.append(links.growing(shard, side))
    small_part = links.growing(small, 0)
    out_part = links.growing(jnp.concatenate([w_out, w_proj], axis=1), 0)
    up_part = links.growing(w_up, 0)
    down_part = links.growing(w_down, 1)
    near = (out_part, up_part)
    for hop in range(5):
        for one in sides:
            one.launch()
        if hop > 0:
            small_part.wait(sides[0].before, sides[1].before)
        small_part.launch()
        for one in sides:
            one.merge()
        first = (sides[0].held, sides[1].held)
        small_part.merge(*first)
        for one in near:
            if hop == 0:
                one.wait(*first)
            elif hop < 4:
                one.merge(*first)
            if hop < 4:
                one.launch()
        if hop == 1:
            down_part.wait(*first)
        elif hop == 2 or hop == 3:
            down_part.merge(*first)
        if hop > 0 and hop < 4:
            down_part.launch()
    small_full = small_part.full().reshape(count, -1)
    full_qkv = [rows_of(one.full()) for one in sides]
    full_biases = (
        small_full[:, : 6 * shard_cols]
        .reshape(count, 6, shard_cols)
        .transpose(1, 0, 2)
        .reshape(6, model_width)
        .astype(f32)
    )
    full_gains = (
        small_full[:, 6 * shard_cols : 8 * shard_cols]
        .reshape(count, 2, shard_cols)
        .transpose(1, 0, 2)
        .reshape(2, model_width)
        .astype(f32)
    )
    full_upbias = small_full[:, 8 * shard_cols :].reshape(ff).astype(f32)

    tokens = jnp.concatenate(
        [doc_hidden[0], query_hidden.reshape(query_count * span, model_width)], axis=0
    )
    segment, segrow, segcol, bounds = tables(seg_lengths[0], row_len)
    slot_ids = jnp.arange(doc_slots, dtype=jnp.int32)
    member = (segment[:, None] == slot_ids[None, :]).astype(f32)
    member_t = (slot_ids[:, None] == segment[None, :]).astype(f32)
    zero_row = jnp.zeros((part,), f32)
    qkv, contexts, saved = [], [], []
    for side in range(2):
        cut = slice(side * part, (side + 1) * part)
        bias = jnp.concatenate([full_biases[0, cut], zero_row, full_biases[1, cut]])
        qkv.append((matmul_plain(tokens, full_qkv[side]) + bias).astype(bf16))
    for side in range(2):
        qkv[side] = after(qkv[side], (up_part, down_part)[side].before)
        context, lse, query_lse = attention_forward(
            qkv[side], segrow, segcol, bounds, row_len, span
        )
        if side == 0:
            for one in (out_part, down_part):
                one.merge(context)
                one.launch()
        contexts.append(context)
        saved.append((lse, query_lse))
    for one in (up_part, down_part):
        one.merge(*contexts)
        one.launch()
    contexts[1] = after(contexts[1], up_part.before, down_part.before)
    out_part.merge()
    out_proj = rows_of(out_part.full())
    full_out, full_proj = out_proj[:, :model_width], out_proj[:, model_width:]
    up_part.merge()
    full_up = rows_of(up_part.full())
    attn_out = (
        matmul_plain(contexts[0], full_out[:part])
        + matmul_plain(contexts[1], full_out[part:])
        + full_biases[2]
    )
    first_out, first_normed, first_scale = layer_norm_parts(
        tokens.astype(f32) + attn_out, full_gains[0], full_biases[3]
    )
    first_low = first_out.astype(bf16)
    up_pre = matmul_plain(first_low, full_up) + full_upbias
    share = 0.5 * (1.0 + lax.erf(up_pre * root_half))
    gelu_out = (up_pre * share).astype(bf16)
    density = jnp.exp(-0.5 * up_pre * up_pre) * density_peak
    slope = (share + up_pre * density).astype(bf16)
    gelu_out, slope = lax.optimization_barrier((gelu_out, slope))
    down_part.merge()
    full_down = rows_of(down_part.full())
    ffn_out = matmul_plain(gelu_out, full_down) + full_biases[4]
    second_out, second_normed, second_scale = layer_norm_parts(
        first_out + ffn_out, full_gains[1], full_biases[5]
    )
    second_low = second_out.astype(bf16)
    vectors = matmul_plain(second_low, full_proj).astype(bf16)
    doc_vectors = vectors[:row_len]
    query_vectors = vectors[row_len:].reshape(query_count * span, proj_width)
    every_query = links.everyone(query_vectors).reshape(count * query_count * span, proj_width)
    query_total = count * query_count
    levels = (proj_width, proj_width * 3 // 4, proj_width // 2)
    logits, doc_sums = interaction_logits(levels, span, doc_vectors, member.astype(bf16), every_query)
    logits = logits.transpose(1, 0, 2)
    powers = jnp.exp(logits)
    local_sum = jnp.sum(powers, axis=-1)
    my_row = lax.axis_index(AXES)
    chosen = ((positives - my_row * doc_slots)[:, None] == slot_ids[None, :]).astype(f32)
    local_pick = jnp.sum(logits * chosen[:, None, :], axis=-1)
    both = links.total(jnp.concatenate([local_sum, local_pick], axis=1).T).T
    all_sums, picked = both[:, :3], both[:, 3:]
    loss = jnp.sum(jnp.log(all_sums) - picked) / query_total
    score_derivative = (powers / all_sums[:, :, None] - chosen[:, None, :]) / query_total
    peak_match_derivative = score_derivative / (span * sharpness_divisor)

    query_terms, doc_vec_grad = interaction_grads(
        levels, span, doc_vectors, member_t.astype(bf16), every_query, doc_sums,
        peak_match_derivative.transpose(1, 0, 2),
    )
    query_terms = query_terms.reshape(count, query_count * span, proj_width)
    query_vec_grad = links.owners_sum(query_terms)
    grad_vectors = jnp.concatenate([doc_vec_grad, query_vec_grad], axis=0).astype(bf16)

    def spread_rows_of(full):
        return full.reshape(count, full.shape[0] // count, full.shape[1])

    proj_grad = matmul_left_t(second_low, grad_vectors)
    grad_second = matmul_right_t(grad_vectors, full_proj)
    grad_mid, gain_two, bias_two = layer_norm_back(
        grad_second, second_normed, second_scale, full_gains[1]
    )
    grad_ffn = grad_mid.astype(bf16)
    down_grad = matmul_left_t(gelu_out, grad_ffn)
    down_sum = links.shrinking(spread_rows_of(down_grad), 1)
    down_sum.launch()
    down_bias = jnp.sum(grad_ffn, axis=0, dtype=f32)
    grad_gelu = matmul_right_t(after(grad_ffn, down_sum.leaving), full_down)
    grad_up = (grad_gelu * slope.astype(f32)).astype(bf16)
    upbias_grad = jnp.sum(grad_up, axis=0, dtype=f32)
    up_grad = matmul_left_t(first_low, grad_up)
    up_sum = links.shrinking(spread_rows_of(up_grad), 0)
    up_sum.launch()
    down_sum.merge(up_sum.leaving)
    down_sum.launch()
    grad_first = grad_mid + matmul_right_t(after(grad_up, down_sum.leaving), full_up)
    grad_res, gain_one, bias_one = layer_norm_back(
        grad_first, first_normed, first_scale, full_gains[0]
    )
    up_sum.merge(grad_res)
    up_sum.launch()
    grad_attn = after(grad_res.astype(bf16), up_sum.leaving)
    out_bias = jnp.sum(grad_attn, axis=0, dtype=f32)
    out_grad = jnp.concatenate([matmul_left_t(c, grad_attn) for c in contexts], axis=0)
    out_sum = links.shrinking(spread_rows_of(jnp.concatenate([out_grad, proj_grad], axis=1)), 0)
    out_sum.launch()
    input_grad = grad_res
    query_bias, value_bias, qkv_sums = [], [], []
    grad_contexts = [
        matmul_right_t(grad_attn, full_out[side * part : (side + 1) * part]).astype(bf16)
        for side in range(2)
    ]
    down_sum.merge(*grad_contexts)
    down_sum.launch()
    earlier = (out_sum.leaving, down_sum.leaving)
    for side in range(2):
        grad_qkv = attention_backward(
            qkv[side], after(grad_contexts[side], *earlier), contexts[side], *saved[side], segrow,
            segcol, bounds, row_len, span,
        )
        if side == 1:
            up_sum.merge(grad_qkv)
            up_sum.launch()
            down_sum.merge(grad_qkv)
            down_sum.launch()
            qkv_sums[0].merge(grad_qkv)
            qkv_sums[0].launch()
            grad_qkv = after(grad_qkv, up_sum.leaving, down_sum.leaving, qkv_sums[0].leaving)
        query_bias.append(jnp.sum(grad_qkv[:, :part], axis=0, dtype=f32))
        value_bias.append(jnp.sum(grad_qkv[:, 2 * part :], axis=0, dtype=f32))
        qkv_grad = matmul_left_t(tokens, grad_qkv)
        if side == 0:
            qkv_sums.append(links.shrinking(spread_rows_of(qkv_grad), side))
        else:
            wide = qkv_grad.shape[1] // 2
            for lane in range(2):
                piece = qkv_grad[:, lane * wide : (lane + 1) * wide]
                qkv_sums.append(links.shrinking(spread_rows_of(piece), lane))
        for one in qkv_sums[side:]:
            one.launch()
        if side == 0:
            out_sum.merge(qkv_sums[0].leaving)
            out_sum.launch()
            up_sum.merge(qkv_sums[0].leaving)
            up_sum.launch()
            earlier = (qkv_sums[0].leaving, out_sum.leaving, up_sum.leaving)
        grad_qkv = after(grad_qkv, *[one.leaving for one in qkv_sums[side:]])
        input_grad = input_grad + matmul_right_t(grad_qkv, full_qkv[side])
    bias_grads = jnp.stack(
        [
            jnp.concatenate(query_bias),
            jnp.concatenate(value_bias),
            out_bias,
            bias_one,
            down_bias,
            bias_two,
            gain_one,
            gain_two,
        ],
        axis=0,
    )
    small_grads = jnp.concatenate(
        [
            bias_grads.reshape(8, count, shard_cols).transpose(1, 0, 2).reshape(count, -1),
            upbias_grad.reshape(count, -1),
        ],
        axis=1,
    )
    small_sum = links.shrinking(small_grads[:, None, :], 0, wire=f32)
    small_sum.launch()
    first, others, slow = qkv_sums[1:], [small_sum, qkv_sums[0], out_sum], [up_sum, down_sum]
    last = [one.leaving for one in first]
    for hop in range(links.bits):
        for one in first:
            one.merge()
        for one in others:
            one.merge(*last)
        for one in first + others:
            one.launch()
        last = [one.held for one in first]
        if hop == 0 or hop == 3:
            for one in slow:
                one.merge(*last)
                one.launch()
        last = [one.leaving for one in first]
    down_shard, up_shard, out_proj_shard = down_sum.mine(), up_sum.mine(), out_sum.mine()
    qkv_shards = [one.mine() for one in qkv_sums]
    qkv_shards = [qkv_shards[0], jnp.concatenate(qkv_shards[1:], axis=-1)]
    small_shard = small_sum.mine()[0]
    shards = [
        jnp.concatenate([s[:, i * part : (i + 1) * part] for s in qkv_shards], axis=1)
        for i in range(3)
    ]
    return (
        loss,
        input_grad[:row_len].reshape(1, row_len, model_width),
        input_grad[row_len:].reshape(query_count, span, model_width),
        shards[0],
        shards[1],
        shards[2],
        out_proj_shard[:, :model_width],
        up_shard,
        down_shard,
        out_proj_shard[:, model_width:],
        small_shard[: 6 * shard_cols].reshape(6, shard_cols),
        small_shard[6 * shard_cols : 8 * shard_cols].reshape(2, shard_cols),
        small_shard[8 * shard_cols :],
    )


def solution(mesh):
    return jax.shard_map(
        partial(body, make_links(mesh)),
        mesh=mesh,
        in_specs=(
            P(("dp", "fsdp"), None, None),
            P(("dp", "fsdp"), None, None),
            P(("dp", "fsdp"), None),
            P(("dp", "fsdp"), None),
            P(("dp", "fsdp"), None),
            P(("dp", "fsdp"), None),
            P(("dp", "fsdp"), None),
            P(("dp", "fsdp"), None),
            P(("dp", "fsdp"), None),
            P(None, ("dp", "fsdp")),
            P(None, ("dp", "fsdp")),
            P(("dp", "fsdp")),
            P(("dp", "fsdp"), None),
            P(),
        ),
        out_specs=(
            P(),
            P(("dp", "fsdp"), None, None),
            P(("dp", "fsdp"), None, None),
            P(("dp", "fsdp"), None),
            P(("dp", "fsdp"), None),
            P(("dp", "fsdp"), None),
            P(("dp", "fsdp"), None),
            P(("dp", "fsdp"), None),
            P(("dp", "fsdp"), None),
            P(("dp", "fsdp"), None),
            P(None, ("dp", "fsdp")),
            P(None, ("dp", "fsdp")),
            P(("dp", "fsdp")),
        ),
        check_vma=False,
    )
```
